128 devices in a mesh: ha: 8 (over y, z_lo), wa: 16 (over x, z_hi, core).
Axes of the slice: x: 4, y: 4, z: 4 (z_hi: 2, z_lo: 2; z = z_hi * 2 + z_lo), core: 2. Of those that a mesh axis runs over, the one named last changes fastest.
Arguments:
- tokens: bfloat16 [224, 448, 384], P('ha', 'wa'), may hold values from -8 to 8
- cotangent: bfloat16 [224, 448, 384], P('ha', 'wa'), may hold values from -8 to 8
- w_qkv: bfloat16 [384, 1152], replicated, may hold values from -0.3125 to 0.3125
- w_proj: bfloat16 [384, 384], replicated, may hold values from -0.3125 to 0.3125
- w_fc1: bfloat16 [384, 1536], replicated, may hold values from -0.3125 to 0.3125
- w_fc2: bfloat16 [1536, 384], replicated, may hold values from -0.15625 to 0.15625
- bias_table: float32 [169, 12], replicated, may hold values from -4 to 280
- rel_index: int32 [49, 49], replicated, may hold values from 0 to 168, as said below
- region: int32 [224, 448], P('ha', 'wa'), may hold values from 0 to 15, as said below
Outputs:
- block_out: bfloat16 [224, 448, 384], P('ha', 'wa')
- token_grad: bfloat16 [224, 448, 384], P('ha', 'wa')
- grad_qkv: float32 [384, 1152], replicated
- grad_proj: float32 [384, 384], replicated
- grad_fc1: float32 [384, 1536], replicated
- grad_fc2: float32 [1536, 384], replicated
- grad_table: float32 [169, 12], replicated
The draws below stay inside these ranges and needn't reach their ends.
Inputs may be any that keep to these rules, and one draw needn't show every extreme that they name: `rel_index`: pairs of window positions with the same offset share an entry, pairs with different offsets have different entries. `region`: the crop id of the token at each position of the shifted grid.
All inputs are finite; a program needn't handle non-finite values.
Results may differ from the reference program's by a relative error of at most 0.016.
Values may be sent and summed in bfloat16 or wider, within the bound.
No kernel may reach another device: no remote copies, remote signals or barrier semaphores. Data moves between devices by JAX's collectives and lax.ppermute only.
A program may use at most 128 MiB of HBM per device.

```python
import math
import jax
import jax.numpy as jnp
from jax import lax

C = 384
HEADS = 12
FFN = 1536
SIDE = 7
SHIFT = 3
CROPS = 4
HEAD_DIM = 32
WINDOW = 49
TABLE = 169
NH = 224
NW = 448
PARAMS = 1771500


def field_drawn(key, salt):
    values = jax.random.normal(jax.random.fold_in(key, salt), (NH, NW, C), jnp.float32)
    return jnp.clip(values, -8.0, 8.0).astype(jnp.bfloat16)


def draw_tokens(key, part):
    return field_drawn(key, 31)


def draw_cotangent(key, part):
    return field_drawn(key, 41)


def label_order(key):
    return jax.random.permutation(jax.random.fold_in(key, 7), TABLE).astype(jnp.int32)


def draw_rel_index(key, part):
    order = label_order(key)
    places = jnp.arange(WINDOW, dtype=jnp.int32)
    offset_rows = places[:, None] // SIDE - places[None, :] // SIDE + SIDE - 1
    offset_cols = places[:, None] % SIDE - places[None, :] % SIDE + SIDE - 1
    return order[offset_rows * (2 * SIDE - 1) + offset_cols]


def draw_bias_table(key, part):
    values = jax.random.normal(jax.random.fold_in(key, 21), (TABLE, HEADS), jnp.float32)
    return jnp.clip(values, -4.0, 4.0)


def crop_of(places, cuts):
    return jnp.sum((places[:, None] >= cuts[None, :]).astype(jnp.int32), 1)


def draw_region(key, part):
    row_cuts = jax.random.randint(jax.random.fold_in(key, 3), (CROPS - 1,), 1, NH, dtype=jnp.int32)
    col_cuts = jax.random.randint(jax.random.fold_in(key, 4), (CROPS - 1,), 1, NW, dtype=jnp.int32)
    row_places = (jnp.arange(NH, dtype=jnp.int32) + SHIFT) % NH
    col_places = (jnp.arange(NW, dtype=jnp.int32) + SHIFT) % NW
    return crop_of(row_places, row_cuts)[:, None] * CROPS + crop_of(col_places, col_cuts)[None, :]


def scatter_about(own_key, shape, deviation, bound, held_as=jnp.bfloat16):
    return jnp.clip(deviation * jax.random.normal(own_key, shape, jnp.float32), -bound, bound).astype(held_as)


def setup_inputs(seed: int = 0) -> dict:
    splits = jax.random.split(jax.random.key(seed), 10)
    return {
        "tokens": draw_tokens(jax.random.fold_in(splits[9], 71), 0),
        "cotangent": draw_cotangent(jax.random.fold_in(splits[9], 71), 0),
        "w_qkv": scatter_about(splits[2], (C, 3 * C), C ** -0.5, 0.3125),
        "w_proj": scatter_about(splits[3], (C, C), C ** -0.5, 0.3125),
        "w_fc1": scatter_about(splits[4], (C, FFN), C ** -0.5, 0.3125),
        "w_fc2": scatter_about(splits[5], (FFN, C), FFN ** -0.5, 0.15625),
        "bias_table": draw_bias_table(jax.random.fold_in(splits[9], 71), 0),
        "rel_index": draw_rel_index(jax.random.fold_in(splits[9], 71), 0),
        "region": draw_region(jax.random.fold_in(splits[9], 71), 0),
    }


epsilon = 1e-05
highest = lax.Precision.HIGHEST

def rounded(values):
    return lax.optimization_barrier(values.astype(jnp.bfloat16)).astype(jnp.float32)

def normalize(values):
    average = lax.optimization_barrier(jnp.mean(values, -1, keepdims=True))
    centred = values - average
    inverse = lax.rsqrt(lax.optimization_barrier(jnp.mean(centred * centred, -1, keepdims=True)) + epsilon)
    return (centred * inverse, inverse)

def normalize_back(normal_rows, inverse, upstream):
    up_mean = lax.optimization_barrier(jnp.mean(upstream, -1, keepdims=True))
    cross_mean = lax.optimization_barrier(jnp.mean(upstream * normal_rows, -1, keepdims=True))
    return inverse * (upstream - up_mean - normal_rows * cross_mean)

def gelu_slope(pre_act):
    normal_cdf = 0.5 * (1.0 + lax.erf(pre_act * 2.0 ** (-0.5)))
    return normal_cdf + pre_act * jnp.exp(-0.5 * pre_act * pre_act) * (2.0 * math.pi) ** (-0.5)

def to_windows(grid_in):
    row_count, col_count = (grid_in.shape[0], grid_in.shape[1])
    shaped = grid_in.reshape(row_count // SIDE, SIDE, col_count // SIDE, SIDE, -1)
    return shaped.transpose(0, 2, 1, 3, 4).reshape(row_count // SIDE, col_count // SIDE, WINDOW, -1)

def from_windows(grid_in):
    band_count, across, channels = (grid_in.shape[0], grid_in.shape[1], grid_in.shape[3])
    shaped = grid_in.reshape(band_count, across, SIDE, SIDE, channels)
    return shaped.transpose(0, 2, 1, 3, 4).reshape(band_count * SIDE, across * SIDE, channels)

def attend(qkv_win, region_win, pos_bias):
    win_count = qkv_win.shape[0]
    parts_qkv = qkv_win.reshape(win_count, WINDOW, 3, HEADS, HEAD_DIM).astype(jnp.float32)
    queries, keys_in, values = (parts_qkv[:, :, 0], parts_qkv[:, :, 1], parts_qkv[:, :, 2])
    scores = jnp.einsum('wihd,wjhd->whij', queries, keys_in, precision=highest) * HEAD_DIM ** (-0.5) + pos_bias[None]
    same_region = region_win[:, :, None] == region_win[:, None, :]
    scores = jnp.where(same_region[:, None], scores, -1e+30)
    exponent = jnp.exp(scores - lax.optimization_barrier(jnp.max(scores, -1, keepdims=True)))
    attn_probs = exponent / lax.optimization_barrier(jnp.sum(exponent, -1, keepdims=True))
    weighted = jnp.einsum('whij,wjhd->wihd', rounded(attn_probs), values, precision=highest)
    return (weighted.reshape(win_count, WINDOW, HEADS * HEAD_DIM).astype(jnp.bfloat16), attn_probs)

def attend_back(qkv_win, attn_probs, upstream):
    win_count = qkv_win.shape[0]
    parts_qkv = qkv_win.reshape(win_count, WINDOW, 3, HEADS, HEAD_DIM).astype(jnp.float32)
    queries, keys_in, values = (parts_qkv[:, :, 0], parts_qkv[:, :, 1], parts_qkv[:, :, 2])
    grad_out = upstream.reshape(win_count, WINDOW, HEADS, HEAD_DIM).astype(jnp.float32)
    grad_probs = jnp.einsum('wihd,wjhd->whij', grad_out, values, precision=highest)
    grad_values = jnp.einsum('whij,wihd->wjhd', rounded(attn_probs), grad_out, precision=highest)
    grad_scores = attn_probs * (grad_probs - lax.optimization_barrier(jnp.sum(attn_probs * grad_probs, -1, keepdims=True)))
    bias_grad = lax.optimization_barrier(jnp.sum(grad_scores, 0))
    scaled = rounded(grad_scores * HEAD_DIM ** (-0.5))
    grad_queries = jnp.einsum('whij,wjhd->wihd', scaled, keys_in, precision=highest)
    grad_keys = jnp.einsum('whij,wihd->wjhd', scaled, queries, precision=highest)
    stacked = jnp.stack([grad_queries, grad_keys, grad_values], 2)
    return (stacked.reshape(win_count, WINDOW, 3 * HEADS * HEAD_DIM).astype(jnp.bfloat16), bias_grad)

def reference(tokens, cotangent, w_qkv, w_proj, w_fc1, w_fc2, bias_table, rel_index, region):
    row_count, col_count, channels = tokens.shape
    lookup = (rel_index.reshape(-1)[:, None] == jnp.arange(TABLE, dtype=jnp.int32)[None, :]).astype(jnp.float32)
    pos_bias = jnp.dot(lookup, bias_table, precision=highest).T.reshape(HEADS, WINDOW, WINDOW)
    token_f32 = tokens.astype(jnp.float32)
    first_norm, first_scale = normalize(token_f32)
    shifted = jnp.roll(first_norm.astype(jnp.bfloat16), (-SHIFT, -SHIFT), (0, 1))
    flat_shift = shifted.reshape(-1, channels)
    qkv_tok = jnp.dot(flat_shift, w_qkv, preferred_element_type=jnp.float32).astype(jnp.bfloat16)
    qkv_win = to_windows(qkv_tok.reshape(row_count, col_count, 3 * channels))
    region_win = to_windows(region[..., None])[..., 0]

    def forward_band(operands):
        return attend(operands[0], operands[1], pos_bias)
    attn_win, attn_probs = lax.map(forward_band, (qkv_win, region_win))
    attn_tok = from_windows(attn_win).reshape(-1, channels)
    projected = jnp.dot(attn_tok, w_proj, preferred_element_type=jnp.float32).astype(jnp.bfloat16)
    middle = token_f32 + jnp.roll(projected.reshape(row_count, col_count, channels), (SHIFT, SHIFT), (0, 1)).astype(jnp.float32)
    second_norm, second_scale = normalize(middle)
    normed_low = second_norm.astype(jnp.bfloat16).reshape(-1, channels)
    pre_act = jnp.dot(normed_low, w_fc1, preferred_element_type=jnp.float32)
    activated = jax.nn.gelu(pre_act, approximate=False).astype(jnp.bfloat16)
    block_out = (middle + jnp.dot(activated, w_fc2, preferred_element_type=jnp.float32).reshape(row_count, col_count, channels)).astype(jnp.bfloat16)
    upstream = cotangent.reshape(-1, channels)
    raw_fc2 = jnp.dot(activated.T, upstream, preferred_element_type=jnp.float32)
    grad_pre = (jnp.dot(upstream, w_fc2.T, preferred_element_type=jnp.float32) * gelu_slope(pre_act)).astype(jnp.bfloat16)
    raw_fc1 = jnp.dot(normed_low.T, grad_pre, preferred_element_type=jnp.float32)
    grad_second = jnp.dot(grad_pre, w_fc1.T, preferred_element_type=jnp.float32).reshape(row_count, col_count, channels)
    grad_mid = cotangent.astype(jnp.float32) + normalize_back(second_norm, second_scale, grad_second)
    back_rolled = jnp.roll(grad_mid.astype(jnp.bfloat16), (-SHIFT, -SHIFT), (0, 1)).reshape(-1, channels)
    raw_proj = jnp.dot(attn_tok.T, back_rolled, preferred_element_type=jnp.float32)
    grad_attn = jnp.dot(back_rolled, w_proj.T, preferred_element_type=jnp.float32).astype(jnp.bfloat16)
    attn_back = to_windows(grad_attn.reshape(row_count, col_count, channels))

    def backward_band(operands):
        return attend_back(operands[0], operands[1], operands[2])
    qkv_grads, bias_parts = lax.map(backward_band, (qkv_win, attn_probs, attn_back))
    bias_grad = lax.optimization_barrier(jnp.sum(bias_parts, 0))
    raw_table = jnp.dot(lookup.T, bias_grad.reshape(HEADS, -1).T, precision=highest)
    qkv_back = from_windows(qkv_grads).reshape(-1, 3 * channels)
    raw_qkv = jnp.dot(flat_shift.T, qkv_back, preferred_element_type=jnp.float32)
    grad_shift = jnp.dot(qkv_back, w_qkv.T, preferred_element_type=jnp.float32).astype(jnp.bfloat16)
    grad_normed = jnp.roll(grad_shift.reshape(row_count, col_count, channels), (SHIFT, SHIFT), (0, 1))
    token_grad = (grad_mid + normalize_back(first_norm, first_scale, grad_normed.astype(jnp.float32))).astype(jnp.bfloat16)
    raw = (raw_qkv, raw_proj, raw_fc1, raw_fc2, raw_table)
    norm_sq = jnp.sum(jnp.stack([jnp.sum(gradient * gradient) for gradient in raw]))
    factor = jnp.minimum(1.0, math.sqrt(PARAMS) / (jnp.sqrt(norm_sq) + 1e-06))
    return (block_out, token_grad, raw_qkv * factor, raw_proj * factor, raw_fc1 * factor, raw_fc2 * factor, raw_table * factor)
```

```python
import math

import jax
import jax.numpy as jnp
import numpy as np
from jax import lax
from jax.experimental import pallas as pl
from jax.experimental.pallas import tpu as pltpu
from jax.sharding import PartitionSpec as P

HEADS = 12
SIDE = 7
SHIFT = 3
HEAD_DIM = 32
WINDOW = 49
TABLE = 169
PARAMS = 1771500
C = 384
FFN = 1536
TILE = 28
PAD = 64
BAND = 4 * PAD
COLS = 32
GROUPS = 3
CHUNK = 512
BLOCKS = 36
ROWS = BLOCKS * C + C
HALF = ROWS // 2
PIECE = ROWS // 24

EPSILON = 1e-05
SCALE = HEAD_DIM ** (-0.5)
AXES = ("ha", "wa")
F32 = jnp.float32
BF16 = jnp.bfloat16


def row_place(position):
    return (position // SIDE) * 8 + position % SIDE


def band_maps():
    into = np.zeros((BAND, SIDE * COLS), np.float32)
    back = np.zeros((SIDE * COLS, BAND), np.float32)
    for row in range(SIDE):
        for col in range(TILE):
            place = (col // SIDE) * PAD + row * 8 + col % SIDE
            into[place, row * COLS + col] = 1.0
            back[row * COLS + col + SHIFT, place] = 1.0
    return into, back


def nn(a, b):
    return jnp.dot(a, b, preferred_element_type=F32)


def nt(a, b):
    return lax.dot_general(a, b, (((1,), (1,)), ((), ())), preferred_element_type=F32)


def tn(a, b):
    return lax.dot_general(a, b, (((0,), (0,)), ((), ())), preferred_element_type=F32)


def normalize(values):
    average = jnp.mean(values, -1, keepdims=True)
    centred = values - average
    inverse = lax.rsqrt(jnp.mean(centred * centred, -1, keepdims=True) + EPSILON)
    return centred * inverse, inverse


def normalize_back(normal_rows, inverse, upstream):
    up_mean = jnp.mean(upstream, -1, keepdims=True)
    cross_mean = jnp.mean(upstream * normal_rows, -1, keepdims=True)
    return inverse * (upstream - up_mean - normal_rows * cross_mean)


def gelu_parts(v):
    bell = jnp.exp(-0.5 * v * v)
    t = 1.0 / (1.0 + (0.3275911 * 2.0 ** (-0.5)) * jnp.abs(v))
    poly = t * (
        0.254829592
        + t * (-0.284496736 + t * (1.421413741 + t * (-1.453152027 + t * 1.061405429)))
    )
    upper = 0.5 * poly * bell
    return jnp.where(v >= 0, 1.0 - upper, upper), bell * (2.0 * math.pi) ** (-0.5)


def spread(rows):
    tall = jnp.concatenate([rows] * 4, 0)
    head_row = lax.broadcasted_iota(jnp.int32, (BAND, 128), 0) // PAD
    head_lane = lax.broadcasted_iota(jnp.int32, (BAND, 128), 1) // HEAD_DIM
    return jnp.where(head_row == head_lane, tall, jnp.zeros_like(tall))


def gather_heads(tall):
    head_lane = lax.broadcasted_iota(jnp.int32, (PAD, 128), 1) // HEAD_DIM
    out = jnp.where(head_lane == 0, tall[:PAD], 0.0)
    for h in range(1, 4):
        out = out + jnp.where(head_lane == h, tall[h * PAD : (h + 1) * PAD], 0.0)
    return out


def main_body(
    core_ref,
    tokens_ref,
    cot_ref,
    reg_lane_ref,
    reg_row_ref,
    bias_ref,
    into_ref,
    back_ref,
    w_qkv_ref,
    w_proj_ref,
    w_fc1_ref,
    w_fc2_ref,
    out_ref,
    tgrad_ref,
    keep_ref,
    send_ref,
    qkv_s,
    probs_s,
    attn_s,
    gattn_s,
    dqkv_s,
    a_qkv,
    a_proj,
    a_fc1,
    a_fc2,
    a_bias,
    packed,
    sems,
):
    step = pl.program_id(0)

    @pl.when(step == 0)
    def _():
        for ref in (a_qkv, a_proj, a_fc1, a_fc2, a_bias):
            ref[...] = jnp.zeros_like(ref)

    into = into_ref[...]
    back = back_ref[...]
    x = nn(into, tokens_ref[...].reshape(SIDE * COLS, C))
    cot = nn(into, cot_ref[...].reshape(SIDE * COLS, C))
    cot_low = cot.astype(BF16)
    n1, inv1 = normalize(x)
    n1_low = n1.astype(BF16)
    qkv_s[...] = nn(n1_low, w_qkv_ref[...]).astype(BF16)

    def parts(rows, g):
        lanes = slice(g * 128, (g + 1) * 128)
        return [
            qkv_s[rows, pl.ds(k * C + g * 128, 128)] for k in range(3)
        ], lanes

    def forward_window(w, carry):
        rows = pl.ds(pl.multiple_of(w * PAD, PAD), PAD)
        same = reg_row_ref[w] == reg_lane_ref[w]
        for g in range(GROUPS):
            (q, k, v), lanes = parts(rows, g)
            scores = nt(k, spread(q)) * SCALE + bias_ref[:, g * BAND : (g + 1) * BAND]
            scores = jnp.where(same, scores, -1e30)
            exponent = jnp.exp(scores - jnp.max(scores, 0, keepdims=True))
            probs = exponent * (1.0 / jnp.sum(exponent, 0, keepdims=True))
            probs_s[w, g] = probs
            attn_s[rows, lanes] = gather_heads(tn(probs.astype(BF16), v)).astype(BF16)
        return carry

    lax.fori_loop(0, 4, forward_window, 0)

    attn = attn_s[...]
    projected = nn(attn, w_proj_ref[...]).astype(BF16).astype(F32)
    middle = x + projected
    n2, inv2 = normalize(middle)
    n2_low = n2.astype(BF16)
    n2_t = n2_low.T
    cot_t = cot_low.T
    ffn_out = jnp.zeros((BAND, C), F32)
    grad_second = jnp.zeros((BAND, C), F32)
    for f in range(0, FFN, CHUNK):
        hidden = slice(f, f + CHUNK)
        w1 = w_fc1_ref[:, hidden]
        w2 = w_fc2_ref[hidden, :]
        pre = nn(n2_low, w1)
        cdf, density = gelu_parts(pre)
        activated = (pre * cdf).astype(BF16)
        grad_pre = (nt(cot_low, w2) * (cdf + pre * density)).astype(BF16)
        ffn_out = ffn_out + nn(activated, w2)
        grad_second = grad_second + nt(grad_pre, w1)
        a_fc2[:, hidden] += nn(cot_t, activated)
        a_fc1[:, hidden] += nn(n2_t, grad_pre)

    out_ref[...] = nn(back, (middle + ffn_out).astype(BF16)).astype(BF16).reshape(SIDE, COLS, C)

    grad_mid = cot + normalize_back(n2, inv2, grad_second)
    grad_proj = grad_mid.astype(BF16)
    a_proj[...] += nn(attn.T, grad_proj)
    gattn_s[...] = nt(grad_proj, w_proj_ref[...]).astype(BF16)

    def backward_window(w, carry):
        rows = pl.ds(pl.multiple_of(w * PAD, PAD), PAD)
        for g in range(GROUPS):
            (q, k, v), lanes = parts(rows, g)
            grad_tall = spread(gattn_s[rows, lanes])
            grad_probs = nt(v, grad_tall)
            probs = probs_s[w, g]
            grad_v = nn(probs.astype(BF16), grad_tall)
            weighted = probs * grad_probs
            grad_scores = weighted - probs * jnp.sum(weighted, 0, keepdims=True)
            a_bias[:, g * BAND : (g + 1) * BAND] += grad_scores
            scaled = (grad_scores * SCALE).astype(BF16)
            grad_k = nn(scaled, spread(q))
            grad_q = gather_heads(tn(scaled, k))
            for n, value in enumerate((grad_q, grad_k, grad_v)):
                dqkv_s[rows, pl.ds(n * C + g * 128, 128)] = value.astype(BF16)
        return carry

    lax.fori_loop(0, 4, backward_window, 0)

    dqkv = dqkv_s[...]
    a_qkv[...] += nn(n1_low.T, dqkv)
    grad_normed = nt(dqkv, w_qkv_ref[...]).astype(BF16).astype(F32)
    token_grad = (grad_mid + normalize_back(n1, inv1, grad_normed)).astype(BF16)
    tgrad_ref[...] = nn(back, token_grad).astype(BF16).reshape(SIDE, COLS, C)

    @pl.when(step == pl.num_programs(0) - 1)
    def _():
        at = 0
        for ref in (a_qkv, a_proj, a_fc1, a_fc2):
            for b in range(ref.shape[1] // 128):
                packed[at : at + C, :] = ref[:, b * 128 : (b + 1) * 128].astype(BF16)
                at += C
        for b in range(6):
            packed[at : at + PAD, :] = a_bias[:, b * 128 : (b + 1) * 128].astype(BF16)
            at += PAD
        core = core_ref[0]
        mine = pl.ds(pl.multiple_of(core * HALF, 64), HALF)
        other = pl.ds(pl.multiple_of((1 - core) * HALF, 64), HALF)
        one = pltpu.make_async_copy(packed.at[other, :], send_ref, sems.at[0])
        two = pltpu.make_async_copy(packed.at[mine, :], keep_ref, sems.at[1])
        one.start()
        two.start()
        one.wait()
        two.wait()


def run_main(core, tokens, cot, reg_lane, reg_row, bias, into, back, w_qkv, w_proj, w_fc1, w_fc2):
    def whole(a):
        return pl.BlockSpec(a.shape, lambda i, c: (0,) * a.ndim, pipeline_mode=pl.Buffered(1))

    band = pl.BlockSpec((SIDE, COLS, C), lambda i, c: (i, 0, 0))
    hbm = pl.BlockSpec(memory_space=pl.ANY)
    grid_spec = pltpu.PrefetchScalarGridSpec(
        num_scalar_prefetch=1,
        grid=(4,),
        in_specs=[
            band,
            band,
            pl.BlockSpec((4, 1, BAND), lambda i, c: (i, 0, 0)),
            pl.BlockSpec((4, PAD, 1), lambda i, c: (i, 0, 0)),
            *[whole(a) for a in (bias, into, back, w_qkv, w_proj, w_fc1, w_fc2)],
        ],
        out_specs=[band, band, hbm, hbm],
        scratch_shapes=[
            pltpu.VMEM((BAND, 3 * C), BF16),
            pltpu.VMEM((4, GROUPS, PAD, BAND), F32),
            pltpu.VMEM((BAND, C), BF16),
            pltpu.VMEM((BAND, C), BF16),
            pltpu.VMEM((BAND, 3 * C), BF16),
            pltpu.VMEM((C, 3 * C), F32),
            pltpu.VMEM((C, C), F32),
            pltpu.VMEM((C, FFN), F32),
            pltpu.VMEM((C, FFN), F32),
            pltpu.VMEM((PAD, HEADS * PAD), F32),
            pltpu.VMEM((ROWS, 128), BF16),
            pltpu.SemaphoreType.DMA((2,)),
        ],
    )
    grid_out = jax.ShapeDtypeStruct((TILE, COLS, C), BF16)
    half = jax.ShapeDtypeStruct((HALF, 128), BF16)
    return pl.pallas_call(
        main_body,
        grid_spec=grid_spec,
        out_shape=[grid_out, grid_out, half, half],
        compiler_params=pltpu.CompilerParams(
            dimension_semantics=("arbitrary",), vmem_limit_bytes=56 * 1024 * 1024
        ),
        name="block",
    )(core, tokens, cot, reg_lane, reg_row, bias, into, back, w_qkv, w_proj, w_fc1, w_fc2)


def coordinates(index):
    ha, wa = index // 16, index % 16
    return (wa // 4, ha // 2, (wa // 2 % 2) * 2 + ha % 2, wa % 2)


def device_at(x, y, z, core):
    return (y * 2 + z % 2) * 16 + x * 4 + (z // 2) * 2 + core


def ring_pairs(axis, by):
    pairs = []
    for index in range(128):
        place = list(coordinates(index))
        place[axis] = (place[axis] + by) % (2 if axis == 3 else 4)
        pairs.append((index, device_at(*place)))
    return pairs


def move(value, axis, by):
    return lax.ppermute(value, AXES, ring_pairs(axis, by))


def first_sum_body(place_ref, keep_ref, got_ref, *out_refs):
    for part in range(3):
        for k in range(4):
            piece = part * 4 + lax.rem(place_ref[part] + k, 4)
            rows = pl.ds(pl.multiple_of(piece * PIECE, 16), PIECE)
            out_refs[part * 4 + k][...] = (
                keep_ref[rows, :].astype(F32) + got_ref[rows, :].astype(F32)
            ).astype(BF16)


def first_sum(place, keep, got):
    spec = pl.BlockSpec((HALF, 128), lambda i, p: (0, 0))
    piece = pl.BlockSpec((PIECE, 128), lambda i, p: (0, 0))
    return pl.pallas_call(
        first_sum_body,
        grid_spec=pltpu.PrefetchScalarGridSpec(
            num_scalar_prefetch=1, grid=(1,), in_specs=[spec, spec], out_specs=[piece] * 12
        ),
        out_shape=[jax.ShapeDtypeStruct((PIECE, 128), BF16)] * 12,
        name="first_sum",
    )(place, keep, got)


def sum_four(own, a, b, c):
    total = (own.astype(F32) + b.astype(F32)) + (a.astype(F32) + c.astype(F32))
    return total.astype(BF16)


def table_map():
    out = np.zeros((SIDE, 128, 256), np.float32)
    for jr in range(SIDE):
        for head in range(2):
            for ir in range(SIDE):
                for ic in range(SIDE):
                    out[jr, head * PAD + 8 * ir + ic, head * 128 + (ir - jr + 6) * SIDE + ic] = 1.0
    return out


def last_body(
    place_ref,
    mine_ref,
    other_ref,
    map_ref,
    entry_ref,
    g_qkv,
    g_proj,
    g_fc1,
    g_fc2,
    g_table,
    packed,
    table_s,
    sems,
):
    core = place_ref[3]
    copies = []
    for n, source in enumerate((mine_ref, other_ref)):
        half = core if n == 0 else 1 - core
        for part in range(3):
            for k in range(4):
                piece = half * 12 + part * 4 + lax.rem(place_ref[part] + 4 - k, 4)
                at = part * 4 + k
                copies.append(
                    pltpu.make_async_copy(
                        source.at[pl.ds(at * PIECE, PIECE), :],
                        packed.at[pl.ds(pl.multiple_of(piece * PIECE, 16), PIECE), :],
                        sems.at[n * 12 + at],
                    )
                )
    for copy in copies:
        copy.start()
    for copy in copies:
        copy.wait()

    def add_squares(b, acc):
        block = packed[pl.ds(pl.multiple_of(b * C, C), C), :].astype(F32)
        return acc + jnp.sum((block * block).reshape(C // 8, 8, 128), 0)

    squares = lax.fori_loop(0, BLOCKS, add_squares, jnp.zeros((8, 128), F32))

    base = BLOCKS * C
    by_row = jnp.zeros((48, 256), F32)
    for jr in range(SIDE):
        rows = jnp.concatenate(
            [packed[base + b * PAD + 8 * jr : base + b * PAD + 8 * jr + 8, :].astype(F32) for b in range(6)], 0
        )
        by_row = by_row + nn(rows.astype(BF16), map_ref[jr])
    high = by_row.astype(BF16)
    rest = by_row - high.astype(F32)
    mid = rest.astype(BF16)
    low = (rest - mid.astype(F32)).astype(BF16)
    table = jnp.zeros((16, 256), F32)
    for jc in range(SIDE):
        for part in (high, mid, low):
            picked = jnp.concatenate(
                [
                    part[b * 8 + jc : b * 8 + jc + 1, head * 128 : (head + 1) * 128].astype(F32)
                    for b in range(6)
                    for head in range(2)
                ]
                + [jnp.zeros((4, 128), F32)],
                0,
            )
            table = table + nn(picked.astype(BF16), entry_ref[jc])
    norm_sq = jnp.sum(squares) + jnp.sum(table * table)
    norm = jnp.sqrt(jnp.full((8, 128), norm_sq, F32))
    factor = jnp.minimum(1.0, math.sqrt(PARAMS) / (norm + 1e-06))[:1, :]
    table_s[...] = (table * factor[:, :1]).T
    g_table[...] = table_s[:TABLE, :HEADS]
    at = 0
    for ref in (g_qkv, g_proj, g_fc1):
        for b in range(ref.shape[1] // 128):
            ref[:, b * 128 : (b + 1) * 128] = packed[at : at + C, :].astype(F32) * factor
            at += C
    for b in range(12):
        block = packed[at : at + C, :].astype(F32) * factor
        g_fc2[b * 128 : (b + 1) * 128, :] = block.T
        at += C


def run_last(place, mine, other, row_map, entry_map):
    hbm = pl.BlockSpec(memory_space=pl.ANY)

    def whole(shape):
        return pl.BlockSpec(shape, lambda i, p: (0,) * len(shape))

    shapes = [(C, 3 * C), (C, C), (C, FFN), (FFN, C), (TABLE, HEADS)]
    return pl.pallas_call(
        last_body,
        grid_spec=pltpu.PrefetchScalarGridSpec(
            num_scalar_prefetch=1,
            grid=(1,),
            in_specs=[hbm, hbm, whole(row_map.shape), whole(entry_map.shape)],
            out_specs=[whole(s) for s in shapes],
            scratch_shapes=[
                pltpu.VMEM((ROWS, 128), BF16),
                pltpu.VMEM((256, 16), F32),
                pltpu.SemaphoreType.DMA((24,)),
            ],
        ),
        out_shape=[jax.ShapeDtypeStruct(s, F32) for s in shapes],
        compiler_params=pltpu.CompilerParams(vmem_limit_bytes=56 * 1024 * 1024),
        name="clip",
    )(place, mine, other, row_map, entry_map)


def sum_and_clip(place, keep, send, row_map, entry_map):
    got = move(send, 3, 1)
    pieces = first_sum(place, keep, got)
    held = []
    got = [[move(pieces[p * 4 + k], p, k) for k in range(1, 4)] for p in range(3)]
    held = [sum_four(pieces[p * 4], *got[p]) for p in range(3)]
    for stage in (1, 2):
        got = [[move(held[p], (p + stage) % 3, k) for k in range(1, 4)] for p in range(3)]
        held = [sum_four(held[p], *got[p]) for p in range(3)]
    gathered = []
    got = [[move(held[p], p, k) for k in range(1, 4)] for p in range(3)]
    for p in range(3):
        gathered += [held[p], *got[p]]
    mine = jnp.concatenate(gathered, 0)
    other = move(mine, 3, 1)
    return run_last(place, mine, other, row_map, entry_map)


def from_behind(x, steps):
    sizes = [lax.axis_size(axis) for axis in AXES]
    pairs = []
    for i in range(sizes[0]):
        for j in range(sizes[1]):
            to = ((i + steps[0]) % sizes[0]) * sizes[1] + (j + steps[1]) % sizes[1]
            pairs.append((i * sizes[1] + j, to))
    return lax.ppermute(x, AXES, pairs)


def shifted_tiles(*tiles):
    count = len(tiles)
    low = from_behind(jnp.concatenate([t[:SHIFT, SHIFT:] for t in tiles], 0), (-1, 0))
    right = from_behind(jnp.concatenate([t[SHIFT:, :SHIFT] for t in tiles], 0), (0, -1))
    corner = from_behind(jnp.concatenate([t[:SHIFT, :SHIFT] for t in tiles], 0), (-1, -1))
    inner = TILE - SHIFT
    out = []
    for n, t in enumerate(tiles):
        left_part = jnp.concatenate([t[SHIFT:, SHIFT:], low[n * SHIFT : (n + 1) * SHIFT]], 0)
        right_part = jnp.concatenate(
            [right[n * inner : (n + 1) * inner], corner[n * SHIFT : (n + 1) * SHIFT]], 0
        )
        out.append(
            jnp.concatenate([left_part, right_part, jnp.zeros((TILE, COLS - TILE, C), t.dtype)], 1)
        )
    return out


def unshifted(*tiles):
    inner = TILE - SHIFT
    top = from_behind(jnp.concatenate([t[inner:, SHIFT:TILE] for t in tiles], 0), (1, 0))
    left = from_behind(jnp.concatenate([t[:inner, TILE : TILE + SHIFT] for t in tiles], 0), (0, 1))
    corner = from_behind(jnp.concatenate([t[inner:, TILE : TILE + SHIFT] for t in tiles], 0), (1, 1))
    out = []
    for n, t in enumerate(tiles):
        upper = jnp.concatenate(
            [corner[n * SHIFT : (n + 1) * SHIFT], top[n * SHIFT : (n + 1) * SHIFT]], 1
        )
        lower = jnp.concatenate([left[n * inner : (n + 1) * inner], t[:inner, SHIFT:TILE]], 1)
        out.append(jnp.concatenate([upper, lower], 0))
    return out


def window_tables(bias_table, rel_index):
    by_offset = rel_index.reshape(SIDE, SIDE, SIDE, SIDE)
    spread_out = jnp.pad(
        by_offset.transpose(2, 3, 0, 1), ((0, 1), (0, 1), (0, 1), (0, 1)), constant_values=-1
    ).reshape(PAD * PAD)
    lookup = (spread_out[None, :] == jnp.arange(TABLE, dtype=jnp.int32)[:, None]).astype(F32)
    bias = jnp.dot(bias_table.T, lookup, precision=lax.Precision.HIGHEST)
    bias = bias.reshape(HEADS, PAD, PAD).transpose(1, 0, 2).reshape(PAD, HEADS * PAD)
    entries = jnp.concatenate(
        [by_offset[0, :, :0:-1, :].transpose(1, 0, 2), by_offset[:, :, 0, :]], 0
    )
    entries = entries.transpose(2, 0, 1).reshape(SIDE, 13 * SIDE)
    entries = jnp.pad(entries, ((0, 0), (0, 128 - 13 * SIDE)), constant_values=-1)
    entry_map = (entries[:, :, None] == jnp.arange(256, dtype=jnp.int32)).astype(BF16)
    return bias, entry_map


def before_sum(tokens, cotangent, w_qkv, w_proj, w_fc1, w_fc2, bias_table, rel_index, region, core):
    bias, entry_map = window_tables(bias_table, rel_index)
    windows = region.reshape(4, SIDE, 4, SIDE).transpose(0, 2, 1, 3)
    windows = jnp.pad(windows, ((0, 0), (0, 0), (0, 1), (0, 1)), constant_values=-1)
    windows = windows.reshape(16, PAD)
    reg_lane = jnp.tile(windows, (1, 4)).reshape(16, 1, BAND)
    reg_row = windows.reshape(16, PAD, 1)
    into, back = band_maps()
    tok, cot = shifted_tiles(tokens, cotangent)
    out, tgrad, keep, send = run_main(
        core, tok, cot, reg_lane, reg_row, bias,
        jnp.asarray(into, BF16), jnp.asarray(back, BF16), w_qkv, w_proj, w_fc1, w_fc2,
    )
    return out, tgrad, keep, send, entry_map


def local(tokens, cotangent, w_qkv, w_proj, w_fc1, w_fc2, bias_table, rel_index, region):
    index = lax.axis_index("ha") * 16 + lax.axis_index("wa")
    place = jnp.stack(coordinates(index)).astype(jnp.int32)
    out, tgrad, keep, send, entry_map = before_sum(
        tokens, cotangent, w_qkv, w_proj, w_fc1, w_fc2, bias_table, rel_index, region, place[3:]
    )
    block_out, token_grad = unshifted(out, tgrad)
    grads = sum_and_clip(place, keep, send, jnp.asarray(table_map(), BF16), entry_map)
    return (block_out, token_grad, *grads)


def solution(mesh):
    tiled = P("ha", "wa", None)
    return jax.shard_map(
        local,
        mesh=mesh,
        in_specs=(tiled, tiled, P(), P(), P(), P(), P(), P(), P("ha", "wa")),
        out_specs=(tiled, tiled, P(), P(), P(), P(), P()),
        check_vma=False,
    )
```

```python
import math

import jax
import jax.numpy as jnp
import numpy as np
from jax import lax
from jax.experimental import pallas as pl
from jax.experimental.pallas import tpu as pltpu
from jax.sharding import PartitionSpec as P

HEADS = 12
SIDE = 7
SHIFT = 3
HEAD_DIM = 32
WINDOW = 49
TABLE = 169
PARAMS = 1771500
C = 384
FFN = 1536
TILE = 28
PAD = 64
BAND = 4 * PAD
COLS = 32
GROUPS = 3
CHUNK = 512
BLOCKS = 36
ROWS = BLOCKS * C + C
HALF = ROWS // 2
PIECE = ROWS // 24

EPSILON = 1e-05
SCALE = HEAD_DIM ** (-0.5)
AXES = ("ha", "wa")
F32 = jnp.float32
BF16 = jnp.bfloat16


def row_place(position):
    return (position // SIDE) * 8 + position % SIDE


def band_maps():
    into = np.zeros((BAND, SIDE * COLS), np.float32)
    back = np.zeros((SIDE * COLS, BAND), np.float32)
    for row in range(SIDE):
        for col in range(TILE):
            place = (col // SIDE) * PAD + row * 8 + col % SIDE
            into[place, row * COLS + col] = 1.0
            back[row * COLS + col + SHIFT, place] = 1.0
    return into, back


def nn(a, b):
    return jnp.dot(a, b, preferred_element_type=F32)


def nt(a, b):
    return lax.dot_general(a, b, (((1,), (1,)), ((), ())), preferred_element_type=F32)


def tn(a, b):
    return lax.dot_general(a, b, (((0,), (0,)), ((), ())), preferred_element_type=F32)


def normalize(values):
    average = jnp.mean(values, -1, keepdims=True)
    centred = values - average
    inverse = lax.rsqrt(jnp.mean(centred * centred, -1, keepdims=True) + EPSILON)
    return centred * inverse, inverse


def normalize_back(normal_rows, inverse, upstream):
    up_mean = jnp.mean(upstream, -1, keepdims=True)
    cross_mean = jnp.mean(upstream * normal_rows, -1, keepdims=True)
    return inverse * (upstream - up_mean - normal_rows * cross_mean)


def gelu_parts(v):
    bell = jnp.exp(-0.5 * v * v)
    t = 1.0 / (1.0 + (0.3275911 * 2.0 ** (-0.5)) * jnp.abs(v))
    poly = t * (
        0.254829592
        + t * (-0.284496736 + t * (1.421413741 + t * (-1.453152027 + t * 1.061405429)))
    )
    upper = 0.5 * poly * bell
    return jnp.where(v >= 0, 1.0 - upper, upper), bell * (2.0 * math.pi) ** (-0.5)


def spread(rows):
    tall = jnp.concatenate([rows] * 4, 0)
    head_row = lax.broadcasted_iota(jnp.int32, (BAND, 128), 0) // PAD
    head_lane = lax.broadcasted_iota(jnp.int32, (BAND, 128), 1) // HEAD_DIM
    return jnp.where(head_row == head_lane, tall, jnp.zeros_like(tall))


def gather_heads(tall):
    head_lane = lax.broadcasted_iota(jnp.int32, (PAD, 128), 1) // HEAD_DIM
    out = jnp.where(head_lane == 0, tall[:PAD], 0.0)
    for h in range(1, 4):
        out = out + jnp.where(head_lane == h, tall[h * PAD : (h + 1) * PAD], 0.0)
    return out


def main_body(
    core_ref,
    tokens_ref,
    cot_ref,
    reg_lane_ref,
    reg_row_ref,
    bias_ref,
    into_ref,
    back_ref,
    w_qkv_ref,
    w_proj_ref,
    w_fc1_ref,
    w_fc2_ref,
    out_ref,
    tgrad_ref,
    keep_0,
    keep_1,
    keep_2,
    send_0,
    send_1,
    send_2,
    qkv_s,
    probs_s,
    attn_s,
    gattn_s,
    dqkv_s,
    a_qkv,
    a_proj,
    a_fc1,
    a_fc2,
    a_bias,
    packed,
    sems,
):
    step = pl.program_id(0)

    @pl.when(step == 0)
    def _():
        for ref in (a_qkv, a_proj, a_fc1, a_fc2, a_bias):
            ref[...] = jnp.zeros_like(ref)

    into = into_ref[...]
    back = back_ref[...]
    x = nn(into, tokens_ref[...].reshape(SIDE * COLS, C))
    cot = nn(into, cot_ref[...].reshape(SIDE * COLS, C))
    cot_low = cot.astype(BF16)
    n1, inv1 = normalize(x)
    n1_low = n1.astype(BF16)
    qkv_s[...] = nn(n1_low, w_qkv_ref[...]).astype(BF16)

    def parts(rows, g):
        lanes = slice(g * 128, (g + 1) * 128)
        return [
            qkv_s[rows, pl.ds(k * C + g * 128, 128)] for k in range(3)
        ], lanes

    def forward_window(w, carry):
        rows = pl.ds(pl.multiple_of(w * PAD, PAD), PAD)
        same = reg_row_ref[w] == reg_lane_ref[w]
        for g in range(GROUPS):
            (q, k, v), lanes = parts(rows, g)
            scores = nt(k, spread(q)) * SCALE + bias_ref[:, g * BAND : (g + 1) * BAND]
            scores = jnp.where(same, scores, -1e30)
            exponent = jnp.exp(scores - jnp.max(scores, 0, keepdims=True))
            probs = exponent * (1.0 / jnp.sum(exponent, 0, keepdims=True))
            probs_s[w, g] = probs
            attn_s[rows, lanes] = gather_heads(tn(probs.astype(BF16), v)).astype(BF16)
        return carry

    lax.fori_loop(0, 4, forward_window, 0)

    attn = attn_s[...]
    projected = nn(attn, w_proj_ref[...]).astype(BF16).astype(F32)
    middle = x + projected
    n2, inv2 = normalize(middle)
    n2_low = n2.astype(BF16)
    n2_t = n2_low.T
    cot_t = cot_low.T
    ffn_out = jnp.zeros((BAND, C), F32)
    grad_second = jnp.zeros((BAND, C), F32)
    for f in range(0, FFN, CHUNK):
        hidden = slice(f, f + CHUNK)
        w1 = w_fc1_ref[:, hidden]
        w2 = w_fc2_ref[hidden, :]
        pre = nn(n2_low, w1)
        cdf, density = gelu_parts(pre)
        activated = (pre * cdf).astype(BF16)
        grad_pre = (nt(cot_low, w2) * (cdf + pre * density)).astype(BF16)
        ffn_out = ffn_out + nn(activated, w2)
        grad_second = grad_second + nt(grad_pre, w1)
        a_fc2[:, hidden] += nn(cot_t, activated)
        a_fc1[:, hidden] += nn(n2_t, grad_pre)

    out_ref[...] = nn(back, (middle + ffn_out).astype(BF16)).astype(BF16).reshape(SIDE, COLS, C)

    grad_mid = cot + normalize_back(n2, inv2, grad_second)
    grad_proj = grad_mid.astype(BF16)
    a_proj[...] += nn(attn.T, grad_proj)
    gattn_s[...] = nt(grad_proj, w_proj_ref[...]).astype(BF16)

    def backward_window(w, carry):
        rows = pl.ds(pl.multiple_of(w * PAD, PAD), PAD)
        for g in range(GROUPS):
            (q, k, v), lanes = parts(rows, g)
            grad_tall = spread(gattn_s[rows, lanes])
            grad_probs = nt(v, grad_tall)
            probs = probs_s[w, g]
            grad_v = nn(probs.astype(BF16), grad_tall)
            weighted = probs * grad_probs
            grad_scores = weighted - probs * jnp.sum(weighted, 0, keepdims=True)
            a_bias[:, g * BAND : (g + 1) * BAND] += grad_scores
            scaled = (grad_scores * SCALE).astype(BF16)
            grad_k = nn(scaled, spread(q))
            grad_q = gather_heads(tn(scaled, k))
            for n, value in enumerate((grad_q, grad_k, grad_v)):
                dqkv_s[rows, pl.ds(n * C + g * 128, 128)] = value.astype(BF16)
        return carry

    lax.fori_loop(0, 4, backward_window, 0)

    dqkv = dqkv_s[...]
    a_qkv[...] += nn(n1_low.T, dqkv)
    grad_normed = nt(dqkv, w_qkv_ref[...]).astype(BF16).astype(F32)
    token_grad = (grad_mid + normalize_back(n1, inv1, grad_normed)).astype(BF16)
    tgrad_ref[...] = nn(back, token_grad).astype(BF16).reshape(SIDE, COLS, C)

    @pl.when(step == pl.num_programs(0) - 1)
    def _():
        at = 0
        for ref in (a_qkv, a_proj, a_fc1, a_fc2):
            for b in range(ref.shape[1] // 128):
                packed[at : at + C, :] = ref[:, b * 128 : (b + 1) * 128].astype(BF16)
                at += C
        for b in range(6):
            packed[at : at + PAD, :] = a_bias[:, b * 128 : (b + 1) * 128].astype(BF16)
            at += PAD
        core = core_ref[0]
        copies = []
        for n, refs in enumerate(((send_0, send_1, send_2), (keep_0, keep_1, keep_2))):
            half = core if n else 1 - core
            for p in range(3):
                rows = pl.ds(pl.multiple_of((half * 3 + p) * 4 * PIECE, 64), 4 * PIECE)
                copies.append(pltpu.make_async_copy(packed.at[rows, :], refs[p], sems.at[n * 3 + p]))
        for copy in copies:
            copy.start()
        for copy in copies:
            copy.wait()


def run_main(core, tokens, cot, reg_lane, reg_row, bias, into, back, w_qkv, w_proj, w_fc1, w_fc2):
    def whole(a):
        return pl.BlockSpec(a.shape, lambda i, c: (0,) * a.ndim, pipeline_mode=pl.Buffered(1))

    band = pl.BlockSpec((SIDE, COLS, C), lambda i, c: (i, 0, 0))
    hbm = pl.BlockSpec(memory_space=pl.ANY)
    grid_spec = pltpu.PrefetchScalarGridSpec(
        num_scalar_prefetch=1,
        grid=(4,),
        in_specs=[
            band,
            band,
            pl.BlockSpec((4, 1, BAND), lambda i, c: (i, 0, 0)),
            pl.BlockSpec((4, PAD, 1), lambda i, c: (i, 0, 0)),
            *[whole(a) for a in (bias, into, back, w_qkv, w_proj, w_fc1, w_fc2)],
        ],
        out_specs=[band, band, *[hbm] * 6],
        scratch_shapes=[
            pltpu.VMEM((BAND, 3 * C), BF16),
            pltpu.VMEM((4, GROUPS, PAD, BAND), F32),
            pltpu.VMEM((BAND, C), BF16),
            pltpu.VMEM((BAND, C), BF16),
            pltpu.VMEM((BAND, 3 * C), BF16),
            pltpu.VMEM((C, 3 * C), F32),
            pltpu.VMEM((C, C), F32),
            pltpu.VMEM((C, FFN), F32),
            pltpu.VMEM((C, FFN), F32),
            pltpu.VMEM((PAD, HEADS * PAD), F32),
            pltpu.VMEM((ROWS, 128), BF16),
            pltpu.SemaphoreType.DMA((6,)),
        ],
    )
    grid_out = jax.ShapeDtypeStruct((TILE, COLS, C), BF16)
    third = jax.ShapeDtypeStruct((4 * PIECE, 128), BF16)
    return pl.pallas_call(
        main_body,
        grid_spec=grid_spec,
        out_shape=[grid_out, grid_out, *[third] * 6],
        compiler_params=pltpu.CompilerParams(
            dimension_semantics=("arbitrary",), vmem_limit_bytes=56 * 1024 * 1024
        ),
        name="block",
    )(core, tokens, cot, reg_lane, reg_row, bias, into, back, w_qkv, w_proj, w_fc1, w_fc2)


def coordinates(index):
    ha, wa = index // 16, index % 16
    return (wa // 4, ha // 2, (wa // 2 % 2) * 2 + ha % 2, wa % 2)


def device_at(x, y, z, core):
    return (y * 2 + z % 2) * 16 + x * 4 + (z // 2) * 2 + core


def swap(value, axis, turn=0):
    pairs = []
    for index in range(128):
        place = list(coordinates(index))
        if axis == 3:
            place[3] = 1 - place[3]
        elif (turn + place[3]) % 2 == 0:
            place[axis] = place[axis] ^ 1
        else:
            place[axis] = 3 - place[axis]
        pairs.append((index, device_at(*place)))
    return lax.ppermute(value, AXES, pairs)


def quarter_bits(place, core):
    inner = lax.rem(lax.div(place + 1, 2), 2)
    upper = lax.div(place, 2)
    return inner + core * (upper - inner), upper + core * (inner - upper)


def first_sum_body(part, place_ref, keep_ref, got_ref, held_ref, near_ref, far_ref):
    half, quarter = quarter_bits(place_ref[part], place_ref[3])

    def total(h, q):
        rows = pl.ds(pl.multiple_of((h * 2 + q) * PIECE, 16), PIECE)
        return (keep_ref[rows, :].astype(F32) + got_ref[rows, :].astype(F32)).astype(BF16)

    far_ref[:PIECE, :] = total(1 - half, quarter)
    far_ref[PIECE:, :] = total(1 - half, 1 - quarter)
    held_ref[...] = total(half, quarter)
    near_ref[...] = total(half, 1 - quarter)


def first_sum(part, place, keep, got):
    def spec(rows):
        return pl.BlockSpec((rows, 128), lambda i, p: (0, 0))

    def body(*refs):
        first_sum_body(part, *refs)

    return pl.pallas_call(
        body,
        grid_spec=pltpu.PrefetchScalarGridSpec(
            num_scalar_prefetch=1,
            grid=(1,),
            in_specs=[spec(4 * PIECE)] * 2,
            out_specs=[spec(PIECE), spec(PIECE), spec(2 * PIECE)],
        ),
        out_shape=[jax.ShapeDtypeStruct((n * PIECE, 128), BF16) for n in (1, 1, 2)],
        name="first_sum",
    )(place, keep, got)


def add(*values):
    total = values[0].astype(F32)
    for value in values[1:]:
        total = total + value.astype(F32)
    return total.astype(BF16)


def table_map():
    out = np.zeros((SIDE, 128, 256), np.float32)
    for jr in range(SIDE):
        for head in range(2):
            for ir in range(SIDE):
                for ic in range(SIDE):
                    out[jr, head * PAD + 8 * ir + ic, head * 128 + (ir - jr + 6) * SIDE + ic] = 1.0
    return out


def last_body(place_ref, *refs):
    sources = refs[:12]
    map_ref, entry_ref = refs[12:14]
    outs = refs[14:18]
    g_table = refs[18]
    packed = refs[19]
    stages = refs[20:24]
    sems, out_sems = refs[24:]
    core = place_ref[3]
    copies = []
    for n in range(2):
        owner = core if n == 0 else 1 - core
        for part in range(3):
            half, quarter = quarter_bits(place_ref[part], owner)
            for far in range(2):
                for second in range(2):
                    h = half if far == 0 else 1 - half
                    q = quarter if second == 0 else 1 - quarter
                    piece = owner * 12 + part * 4 + h * 2 + q
                    copies.append(
                        pltpu.make_async_copy(
                            sources[n * 6 + part * 2 + far].at[pl.ds(second * PIECE, PIECE), :],
                            packed.at[pl.ds(pl.multiple_of(piece * PIECE, 16), PIECE), :],
                            sems.at[len(copies)],
                        )
                    )
    for copy in copies:
        copy.start()
    for copy in copies:
        copy.wait()

    def add_squares(b, acc):
        block = packed[pl.ds(pl.multiple_of(b * C, C), C), :].astype(F32)
        return acc + jnp.sum((block * block).reshape(4, C // 32, 8, 128), 1)

    squares = lax.fori_loop(0, BLOCKS, add_squares, jnp.zeros((4, 8, 128), F32))

    base = BLOCKS * C
    by_row = jnp.zeros((48, 256), F32)
    for jr in range(SIDE):
        rows = jnp.concatenate(
            [packed[base + b * PAD + 8 * jr : base + b * PAD + 8 * jr + 8, :].astype(F32) for b in range(6)], 0
        )
        by_row = by_row + nn(rows.astype(BF16), map_ref[jr])
    high = by_row.astype(BF16)
    rest = by_row - high.astype(F32)
    mid = rest.astype(BF16)
    low = (rest - mid.astype(F32)).astype(BF16)
    table = jnp.zeros((16, 256), F32)
    for jc in range(SIDE):
        for part in (high, mid, low):
            picked = jnp.concatenate(
                [
                    part[b * 8 + jc : b * 8 + jc + 1, head * 128 : (head + 1) * 128].astype(F32)
                    for b in range(6)
                    for head in range(2)
                ]
                + [jnp.zeros((4, 128), F32)],
                0,
            )
            table = table + nn(picked.astype(BF16), entry_ref[jc])
    norm_sq = jnp.sum(squares) + jnp.sum(table * table)
    norm = jnp.sqrt(jnp.full((8, 128), norm_sq, F32))
    factor = jnp.minimum(1.0, math.sqrt(PARAMS) / (norm + 1e-06))[:1, :]
    g_table[...] = (table * factor[:, :1])[:HEADS, :TABLE]

    first = 0
    for n in range(4):
        stage, out, sem = stages[n], outs[n], out_sems.at[n]

        def scale_block(b, carry, first=first, n=n, stage=stage, out=out, sem=sem):
            rows = pl.ds(pl.multiple_of((first + b) * C, C), C)
            block = packed[rows, :].astype(F32) * factor
            strip = pl.ds(pl.multiple_of(b * 128, 128), 128)
            if n == 3:
                stage[strip, :] = block.T
                pltpu.make_async_copy(stage.at[strip, :], out.at[strip, :], sem).start()
            else:
                stage[:, strip] = block
                pltpu.make_async_copy(stage.at[:, strip], out.at[:, strip], sem).start()
            return carry

        count = stage.shape[0] // 128 if n == 3 else stage.shape[1] // 128
        lax.fori_loop(0, count, scale_block, 0)
        first += count
    for n in range(4):
        pltpu.make_async_copy(stages[n], outs[n], out_sems.at[n]).wait()


def run_last(place, pieces, row_map, entry_map):
    hbm = pl.BlockSpec(memory_space=pl.ANY)

    def whole(shape):
        return pl.BlockSpec(shape, lambda i, p: (0,) * len(shape))

    shapes = [(C, 3 * C), (C, C), (C, FFN), (FFN, C), (HEADS, TABLE)]
    return pl.pallas_call(
        last_body,
        grid_spec=pltpu.PrefetchScalarGridSpec(
            num_scalar_prefetch=1,
            grid=(1,),
            in_specs=[hbm] * 12 + [whole(row_map.shape), whole(entry_map.shape)],
            out_specs=[hbm] * 4 + [whole(shapes[4])],
            scratch_shapes=[
                pltpu.VMEM((ROWS, 128), BF16),
                *[pltpu.VMEM(s, F32) for s in shapes[:4]],
                pltpu.SemaphoreType.DMA((24,)),
                pltpu.SemaphoreType.DMA((4,)),
            ],
        ),
        out_shape=[jax.ShapeDtypeStruct(s, F32) for s in shapes],
        compiler_params=pltpu.CompilerParams(vmem_limit_bytes=40 * 1024 * 1024),
        name="clip",
    )(place, *pieces, row_map, entry_map)


def sum_over_devices(place, keep, send):
    near, far = [], []
    for p in range(3):
        with jax.named_scope(f"core_{p}"):
            got = swap(send[p], 3)
        held, other_quarter, other_half = first_sum(p, place, keep[p], got)
        with jax.named_scope(f"halve_{p}"):
            got = swap(other_half, p, 0)
        with jax.named_scope(f"quarter_{p}"):
            back = swap(add(other_quarter, got[PIECE:]), p, 1)
        held = add(held, got[:PIECE], back)
        for stage in (1, 2):
            for turn in (0, 1):
                with jax.named_scope(f"double_{stage}{turn}_{p}"):
                    held = add(held, swap(held, (p + stage) % 3, turn))
        with jax.named_scope(f"gather_{p}"):
            half = jnp.concatenate([held, swap(held, p, 1)], 0)
        near.append(half)
        with jax.named_scope(f"regather_{p}"):
            far.append(swap(half, p, 0))
    mine = [value for p in range(3) for value in (near[p], far[p])]
    other = []
    for n, value in enumerate(mine):
        with jax.named_scope(f"recore_{n}"):
            other.append(swap(value, 3))
    return mine + other


def from_behind(x, steps):
    sizes = [lax.axis_size(axis) for axis in AXES]
    pairs = []
    for i in range(sizes[0]):
        for j in range(sizes[1]):
            to = ((i + steps[0]) % sizes[0]) * sizes[1] + (j + steps[1]) % sizes[1]
            pairs.append((i * sizes[1] + j, to))
    return lax.ppermute(x, AXES, pairs)


def shifted_tiles(*tiles):
    count = len(tiles)
    low = from_behind(jnp.concatenate([t[:SHIFT, SHIFT:] for t in tiles], 0), (-1, 0))
    right = from_behind(jnp.concatenate([t[SHIFT:, :SHIFT] for t in tiles], 0), (0, -1))
    corner = from_behind(jnp.concatenate([t[:SHIFT, :SHIFT] for t in tiles], 0), (-1, -1))
    inner = TILE - SHIFT
    out = []
    for n, t in enumerate(tiles):
        left_part = jnp.concatenate([t[SHIFT:, SHIFT:], low[n * SHIFT : (n + 1) * SHIFT]], 0)
        right_part = jnp.concatenate(
            [right[n * inner : (n + 1) * inner], corner[n * SHIFT : (n + 1) * SHIFT]], 0
        )
        out.append(
            jnp.concatenate([left_part, right_part, jnp.zeros((TILE, COLS - TILE, C), t.dtype)], 1)
        )
    return out


def unshifted(*tiles):
    inner = TILE - SHIFT
    top = from_behind(jnp.concatenate([t[inner:, SHIFT:TILE] for t in tiles], 0), (1, 0))
    left = from_behind(jnp.concatenate([t[:inner, TILE : TILE + SHIFT] for t in tiles], 0), (0, 1))
    corner = from_behind(jnp.concatenate([t[inner:, TILE : TILE + SHIFT] for t in tiles], 0), (1, 1))
    out = []
    for n, t in enumerate(tiles):
        upper = jnp.concatenate(
            [corner[n * SHIFT : (n + 1) * SHIFT], top[n * SHIFT : (n + 1) * SHIFT]], 1
        )
        lower = jnp.concatenate([left[n * inner : (n + 1) * inner], t[:inner, SHIFT:TILE]], 1)
        out.append(jnp.concatenate([upper, lower], 0))
    return out


def window_tables(bias_table, rel_index):
    by_offset = rel_index.reshape(SIDE, SIDE, SIDE, SIDE)
    spread_out = jnp.pad(
        by_offset.transpose(2, 3, 0, 1), ((0, 1), (0, 1), (0, 1), (0, 1)), constant_values=-1
    ).reshape(PAD * PAD)
    lookup = (spread_out[None, :] == jnp.arange(TABLE, dtype=jnp.int32)[:, None]).astype(F32)
    bias = jnp.dot(bias_table.T, lookup, precision=lax.Precision.HIGHEST)
    bias = bias.reshape(HEADS, PAD, PAD).transpose(1, 0, 2).reshape(PAD, HEADS * PAD)
    entries = jnp.concatenate(
        [by_offset[0, :, :0:-1, :].transpose(1, 0, 2), by_offset[:, :, 0, :]], 0
    )
    entries = entries.transpose(2, 0, 1).reshape(SIDE, 13 * SIDE)
    entries = jnp.pad(entries, ((0, 0), (0, 128 - 13 * SIDE)), constant_values=-1)
    entry_map = (entries[:, :, None] == jnp.arange(256, dtype=jnp.int32)).astype(BF16)
    return bias, entry_map


def before_sum(tokens, cotangent, w_qkv, w_proj, w_fc1, w_fc2, bias_table, rel_index, region, core):
    bias, entry_map = window_tables(bias_table, rel_index)
    windows = region.reshape(4, SIDE, 4, SIDE).transpose(0, 2, 1, 3)
    windows = jnp.pad(windows, ((0, 0), (0, 0), (0, 1), (0, 1)), constant_values=-1)
    windows = windows.reshape(16, PAD)
    reg_lane = jnp.tile(windows, (1, 4)).reshape(16, 1, BAND)
    reg_row = windows.reshape(16, PAD, 1)
    into, back = band_maps()
    tok, cot = shifted_tiles(tokens, cotangent)
    out, tgrad, *parts = run_main(
        core, tok, cot, reg_lane, reg_row, bias,
        jnp.asarray(into, BF16), jnp.asarray(back, BF16), w_qkv, w_proj, w_fc1, w_fc2,
    )
    return out, tgrad, parts[:3], parts[3:], entry_map


def local(tokens, cotangent, w_qkv, w_proj, w_fc1, w_fc2, bias_table, rel_index, region):
    index = lax.axis_index("ha") * 16 + lax.axis_index("wa")
    place = jnp.stack(coordinates(index)).astype(jnp.int32)
    out, tgrad, keep, send, entry_map = before_sum(
        tokens, cotangent, w_qkv, w_proj, w_fc1, w_fc2, bias_table, rel_index, region, place[3:]
    )
    block_out, token_grad = unshifted(out, tgrad)
    pieces = sum_over_devices(place, keep, send)
    *grads, table = run_last(place, pieces, jnp.asarray(table_map(), BF16), entry_map)
    return (block_out, token_grad, *grads, table.T)


def solution(mesh):
    tiled = P("ha", "wa", None)
    return jax.shard_map(
        local,
        mesh=mesh,
        in_specs=(tiled, tiled, P(), P(), P(), P(), P(), P(), P("ha", "wa")),
        out_specs=(tiled, tiled, P(), P(), P(), P(), P()),
        check_vma=False,
    )
```

```python
import math

import jax
import jax.numpy as jnp
import numpy as np
from jax import lax
from jax.experimental import pallas as pl
from jax.experimental.pallas import tpu as pltpu
from jax.sharding import PartitionSpec as P

HEADS = 12
SIDE = 7
SHIFT = 3
HEAD_DIM = 32
WINDOW = 49
TABLE = 169
PARAMS = 1771500
C = 384
FFN = 1536
TILE = 28
PAD = 64
BAND = 4 * PAD
COLS = 48
RIM = 32
EDGE = 4
GROUPS = 3
CHUNK = 256
BLOCKS = 36
ROWS = BLOCKS * C + C
HALF = ROWS // 2
PIECE = ROWS // 24

EPSILON = 1e-05
SCALE = HEAD_DIM ** (-0.5)
AXES = ("ha", "wa")
F32 = jnp.float32
BF16 = jnp.bfloat16


def row_place(position):
    return (position // SIDE) * 8 + position % SIDE


def band_maps():
    into = np.zeros((BAND, SIDE * COLS), np.float32)
    back = np.zeros((SIDE * COLS, BAND), np.float32)
    for row in range(SIDE):
        for col in range(TILE):
            place = (col // SIDE) * PAD + row * 8 + col % SIDE
            at = col + SHIFT if col + SHIFT < TILE else RIM + col + SHIFT - TILE
            into[place, row * COLS + at] = 1.0
            back[row * COLS + at, place] = 1.0
    return into, back


def nn(a, b):
    return jnp.dot(a, b, preferred_element_type=F32)


def nt(a, b):
    return lax.dot_general(a, b, (((1,), (1,)), ((), ())), preferred_element_type=F32)


def tn(a, b):
    return lax.dot_general(a, b, (((0,), (0,)), ((), ())), preferred_element_type=F32)


def normalize(values):
    average = jnp.mean(values, -1, keepdims=True)
    centred = values - average
    inverse = lax.rsqrt(jnp.mean(centred * centred, -1, keepdims=True) + EPSILON)
    return centred * inverse, inverse


def normalize_back(normal_rows, inverse, upstream):
    up_mean = jnp.mean(upstream, -1, keepdims=True)
    cross_mean = jnp.mean(upstream * normal_rows, -1, keepdims=True)
    return inverse * (upstream - up_mean - normal_rows * cross_mean)


def gelu_parts(v):
    density = jnp.exp(v * v * -0.5) * (2.0 * math.pi) ** (-0.5)
    t = 1.0 / (1.0 + (0.3275911 * 2.0 ** (-0.5)) * jnp.abs(v))
    half = 0.5 * (2.0 * math.pi) ** 0.5
    poly = 1.061405429 * half
    for factor in (-1.453152027, 1.421413741, -0.284496736, 0.254829592):
        poly = poly * t + factor * half
    upper = poly * t * density
    return jnp.where(v >= 0, 1.0 - upper, upper), density


def spread(rows):
    tall = jnp.concatenate([rows] * 4, 0)
    head_row = lax.broadcasted_iota(jnp.int32, (BAND, 128), 0) // PAD
    head_lane = lax.broadcasted_iota(jnp.int32, (BAND, 128), 1) // HEAD_DIM
    return jnp.where(head_row == head_lane, tall, jnp.zeros_like(tall))


def gather_heads(tall):
    head_lane = lax.broadcasted_iota(jnp.int32, (PAD, 128), 1) // HEAD_DIM
    out = jnp.where(head_lane == 0, tall[:PAD], 0.0)
    for h in range(1, 4):
        out = out + jnp.where(head_lane == h, tall[h * PAD : (h + 1) * PAD], 0.0)
    return out


def main_body(
    place_ref,
    tokens_ref,
    cot_ref,
    low_ref,
    right_ref,
    corner_ref,
    reg_lane_ref,
    bias_ref,
    into_ref,
    back_ref,
    w_qkv_ref,
    w_proj_ref,
    w_fc1_ref,
    w_fc2_ref,
    out_ref,
    tgrad_ref,
    low_out,
    right_out,
    corner_out,
    keep_0,
    keep_1,
    keep_2,
    send_0,
    send_1,
    send_2,
    rows_s,
    qkv_s,
    probs_s,
    attn_s,
    gattn_s,
    dqkv_s,
    a_qkv,
    a_proj,
    a_fc1,
    a_fc2,
    a_bias,
    pre_s,
    up_s,
    act_s,
    gpre_s,
    ffn_s,
    second_s,
    packed,
    sems,
):
    step = pl.program_id(0)

    @pl.when(step == 0)
    def _():
        for ref in (a_qkv, a_proj, a_fc1, a_fc2, a_bias):
            ref[...] = jnp.zeros_like(ref)
        rows_s[...] = jnp.zeros_like(rows_s)
        for n, ref in enumerate((tokens_ref, cot_ref)):
            rows_s[n, : TILE - SHIFT, :TILE, :] = ref[SHIFT:]
            rows_s[n, TILE - SHIFT :, :TILE, :] = low_ref[n]
            rows_s[n, : TILE - SHIFT, RIM : RIM + EDGE, :] = right_ref[n, SHIFT:]
            rows_s[n, TILE - SHIFT :, RIM : RIM + EDGE, :] = corner_ref[n]

    into = into_ref[...]
    back = back_ref[...]
    band = pl.ds(step * SIDE, SIDE)
    x = nn(into, rows_s[0, band].reshape(SIDE * COLS, C))
    cot = nn(into, rows_s[1, band].reshape(SIDE * COLS, C))

    def same_region(w):
        across = reg_lane_ref[w]
        down = jnp.broadcast_to(across[:, :128], (128, 128)).T[:PAD]
        return jnp.concatenate([down, down], 1) == across

    def put_back(n, ref, values):
        rows = nn(back, values).astype(BF16).reshape(SIDE, COLS, C)
        ref[...] = rows[:, :TILE]
        right_out[n] = rows[:, RIM : RIM + EDGE]

        @pl.when(step == pl.num_programs(0) - 1)
        def _():
            low_out[n] = rows[SIDE - SHIFT :, :TILE]
            corner_out[n] = rows[SIDE - SHIFT :, RIM : RIM + EDGE]

    cot_low = cot.astype(BF16)
    n1, inv1 = normalize(x)
    n1_low = n1.astype(BF16)
    qkv_s[...] = nn(n1_low, w_qkv_ref[...]).astype(BF16)

    def parts(rows, g):
        lanes = slice(g * 128, (g + 1) * 128)
        return [
            qkv_s[rows, pl.ds(k * C + g * 128, 128)] for k in range(3)
        ], lanes

    def forward_windows(pair, carry):
        chains = []
        for n in range(2):
            w = pair * 2 + n
            rows = pl.ds(pl.multiple_of(w * PAD, PAD), PAD)
            same = same_region(w)
            for g in range(GROUPS):
                (q, k, v), lanes = parts(rows, g)
                scores = nt(k, spread(q)) * SCALE + bias_ref[:, g * BAND : (g + 1) * BAND]
                chains.append((w, g, rows, lanes, v, jnp.where(same, scores, -1e30)))
        for w, g, rows, lanes, v, scores in chains:
            exponent = jnp.exp(scores - jnp.max(scores, 0, keepdims=True))
            probs = exponent * (1.0 / jnp.sum(exponent, 0, keepdims=True))
            probs_s[w, g] = probs
            attn_s[rows, lanes] = gather_heads(tn(probs.astype(BF16), v)).astype(BF16)
        return carry

    lax.fori_loop(0, 2, forward_windows, 0)

    attn = attn_s[...]
    projected = nn(attn, w_proj_ref[...]).astype(BF16).astype(F32)
    middle = x + projected
    n2, inv2 = normalize(middle)
    n2_low = n2.astype(BF16)
    n2_t = n2_low.T
    cot_t = cot_low.T
    def enter(f):
        hidden = slice(f, f + CHUNK)
        pre_s[:, hidden] = nn(n2_low, w_fc1_ref[:, hidden])
        up_s[:, hidden] = nt(cot_low, w_fc2_ref[hidden, :])

    def bend(f):
        hidden = slice(f, f + CHUNK)
        pre = pre_s[:, hidden]
        cdf, density = gelu_parts(pre)
        act_s[:, hidden] = (pre * cdf).astype(BF16)
        gpre_s[:, hidden] = (up_s[:, hidden] * (cdf + pre * density)).astype(BF16)

    def leave(f):
        hidden = slice(f, f + CHUNK)
        activated, grad_pre = act_s[:, hidden], gpre_s[:, hidden]
        a_fc2[:, hidden] += nn(cot_t, activated)
        a_fc1[:, hidden] += nn(n2_t, grad_pre)
        forward = nn(activated, w_fc2_ref[hidden, :])
        backward = nt(grad_pre, w_fc1_ref[:, hidden])
        ffn_s[...] = forward if f == 0 else ffn_s[...] + forward
        second_s[...] = backward if f == 0 else second_s[...] + backward

    enter(0)
    for f in range(0, FFN + CHUNK, CHUNK):
        if f + CHUNK < FFN:
            enter(f + CHUNK)
        if f < FFN:
            bend(f)
        if f > 0:
            leave(f - CHUNK)
    ffn_out = ffn_s[...]
    grad_second = second_s[...]

    put_back(0, out_ref, (middle + ffn_out).astype(BF16))

    grad_mid = cot + normalize_back(n2, inv2, grad_second)
    grad_proj = grad_mid.astype(BF16)
    a_proj[...] += nn(attn.T, grad_proj)
    gattn_s[...] = nt(grad_proj, w_proj_ref[...]).astype(BF16)

    def backward_windows(pair, carry):
        chains = []
        for n in range(2):
            w = pair * 2 + n
            rows = pl.ds(pl.multiple_of(w * PAD, PAD), PAD)
            for g in range(GROUPS):
                (q, k, v), lanes = parts(rows, g)
                grad_tall = spread(gattn_s[rows, lanes])
                grad_probs = nt(v, grad_tall)
                grad_v = nn(probs_s[w, g].astype(BF16), grad_tall)
                dqkv_s[rows, pl.ds(2 * C + g * 128, 128)] = grad_v.astype(BF16)
                chains.append((w, g, rows, q, k, grad_probs))
        for w, g, rows, q, k, grad_probs in chains:
            probs = probs_s[w, g]
            weighted = probs * grad_probs
            grad_scores = weighted - probs * jnp.sum(weighted, 0, keepdims=True)
            a_bias[:, g * BAND : (g + 1) * BAND] += grad_scores
            scaled = (grad_scores * SCALE).astype(BF16)
            grad_k = nn(scaled, spread(q))
            grad_q = gather_heads(tn(scaled, k))
            for n, value in enumerate((grad_q, grad_k)):
                dqkv_s[rows, pl.ds(n * C + g * 128, 128)] = value.astype(BF16)
        return carry

    lax.fori_loop(0, 2, backward_windows, 0)

    dqkv = dqkv_s[...]
    a_qkv[...] += nn(n1_low.T, dqkv)
    grad_normed = nt(dqkv, w_qkv_ref[...]).astype(BF16).astype(F32)
    token_grad = (grad_mid + normalize_back(n1, inv1, grad_normed)).astype(BF16)
    put_back(1, tgrad_ref, token_grad)

    @pl.when(step == pl.num_programs(0) - 1)
    def _():
        at = 0
        for ref in (a_qkv, a_proj, a_fc1, a_fc2):
            for b in range(ref.shape[1] // 128):
                packed[at : at + C, :] = ref[:, b * 128 : (b + 1) * 128].astype(BF16)
                at += C
        for b in range(6):
            packed[at : at + PAD, :] = a_bias[:, b * 128 : (b + 1) * 128].astype(BF16)
            at += PAD
        core = place_ref[3]
        copies = []
        for refs, owner in (((send_0, send_1, send_2), 1 - core), ((keep_0, keep_1, keep_2), core)):
            for p in range(3):
                half, quarter = quarter_bits(place_ref[p], owner)
                pieces = (
                    half * 2 + quarter,
                    half * 2 + 1 - quarter,
                    (1 - half) * 2 + quarter,
                    (1 - half) * 2 + 1 - quarter,
                )
                for n, piece in enumerate(pieces):
                    at = ((owner * 3 + p) * 4 + piece) * PIECE
                    copies.append(
                        pltpu.make_async_copy(
                            packed.at[pl.ds(pl.multiple_of(at, 16), PIECE), :],
                            refs[p].at[pl.ds(n * PIECE, PIECE), :],
                            sems.at[len(copies)],
                        )
                    )
        for copy in copies:
            copy.start()
        for copy in copies:
            copy.wait()


def run_main(place, tiles, rims, reg_lane, bias, into, back, weights):
    def whole(a):
        return pl.BlockSpec(a.shape, lambda i, c: (0,) * a.ndim, pipeline_mode=pl.Buffered(1))

    def resident(shape):
        return pl.BlockSpec(shape, lambda i, c: (0,) * len(shape))

    band = pl.BlockSpec((SIDE, TILE, C), lambda i, c: (i, 0, 0))
    hbm = pl.BlockSpec(memory_space=pl.ANY)
    grid_spec = pltpu.PrefetchScalarGridSpec(
        num_scalar_prefetch=1,
        grid=(4,),
        in_specs=[
            *[whole(a) for a in (*tiles, *rims)],
            pl.BlockSpec((4, 1, BAND), lambda i, c: (i, 0, 0)),
            *[whole(a) for a in (bias, into, back, *weights)],
        ],
        out_specs=[
            band,
            band,
            resident(rims[0].shape),
            pl.BlockSpec((2, SIDE, EDGE, C), lambda i, c: (0, i, 0, 0)),
            resident(rims[2].shape),
            *[hbm] * 6,
        ],
        scratch_shapes=[
            pltpu.VMEM((2, TILE, COLS, C), BF16),
            pltpu.VMEM((BAND, 3 * C), BF16),
            pltpu.VMEM((4, GROUPS, PAD, BAND), F32),
            pltpu.VMEM((BAND, C), BF16),
            pltpu.VMEM((BAND, C), BF16),
            pltpu.VMEM((BAND, 3 * C), BF16),
            pltpu.VMEM((C, 3 * C), F32),
            pltpu.VMEM((C, C), F32),
            pltpu.VMEM((C, FFN), F32),
            pltpu.VMEM((C, FFN), F32),
            pltpu.VMEM((PAD, HEADS * PAD), F32),
            pltpu.VMEM((BAND, FFN), F32),
            pltpu.VMEM((BAND, FFN), F32),
            pltpu.VMEM((BAND, FFN), BF16),
            pltpu.VMEM((BAND, FFN), BF16),
            pltpu.VMEM((BAND, C), F32),
            pltpu.VMEM((BAND, C), F32),
            pltpu.VMEM((ROWS, 128), BF16),
            pltpu.SemaphoreType.DMA((24,)),
        ],
    )
    third = jax.ShapeDtypeStruct((4 * PIECE, 128), BF16)
    return pl.pallas_call(
        main_body,
        grid_spec=grid_spec,
        out_shape=[jax.ShapeDtypeStruct(a.shape, BF16) for a in (*tiles, *rims)] + [third] * 6,
        compiler_params=pltpu.CompilerParams(
            dimension_semantics=("arbitrary",), vmem_limit_bytes=56 * 1024 * 1024
        ),
        name="block",
    )(place, *tiles, *rims, reg_lane, bias, into, back, *weights)


def rims_body(tokens_low, tokens_left, cot_low, cot_left, low_ref, right_ref, corner_ref):
    for n, (low, left) in enumerate(((tokens_low, tokens_left), (cot_low, cot_left))):
        low_ref[n] = low[...]
        right_ref[n] = left[:, :EDGE]
        corner_ref[n] = left[:SHIFT, :EDGE]


def cut_rims(tokens, cot):
    low = pl.BlockSpec((SHIFT, TILE, C), lambda i: (0, 0, 0))
    left = pl.BlockSpec((TILE, 16, C), lambda i: (0, 0, 0))
    shapes = [(2, SHIFT, TILE, C), (2, TILE, EDGE, C), (2, SHIFT, EDGE, C)]
    return pl.pallas_call(
        rims_body,
        grid=(1,),
        in_specs=[low, left, low, left],
        out_specs=[pl.BlockSpec(s, lambda i: (0, 0, 0, 0)) for s in shapes],
        out_shape=[jax.ShapeDtypeStruct(s, BF16) for s in shapes],
        name="rims",
    )(tokens, tokens, cot, cot)


def coordinates(index):
    ha, wa = index // 16, index % 16
    return (wa // 4, ha // 2, (wa // 2 % 2) * 2 + ha % 2, wa % 2)


def device_at(x, y, z, core):
    return (y * 2 + z % 2) * 16 + x * 4 + (z // 2) * 2 + core


def swap(value, axis, turn=0):
    pairs = []
    for index in range(128):
        place = list(coordinates(index))
        if axis == 3:
            place[3] = 1 - place[3]
        elif (turn + place[3]) % 2 == 0:
            place[axis] = place[axis] ^ 1
        else:
            place[axis] = 3 - place[axis]
        pairs.append((index, device_at(*place)))
    return lax.ppermute(value, AXES, pairs)


def quarter_bits(place, core):
    inner = lax.rem(lax.div(place + 1, 2), 2)
    upper = lax.div(place, 2)
    return inner + core * (upper - inner), upper + core * (inner - upper)


def add(*values):
    total = values[0].astype(F32)
    for value in values[1:]:
        total = total + value.astype(F32)
    return total.astype(BF16)


def table_map():
    out = np.zeros((SIDE, 128, 256), np.float32)
    for jr in range(SIDE):
        for head in range(2):
            for ir in range(SIDE):
                for ic in range(SIDE):
                    out[jr, head * PAD + 8 * ir + ic, head * 128 + (ir - jr + 6) * SIDE + ic] = 1.0
    return out


def last_body(place_ref, *refs):
    sources = refs[:12]
    map_ref, entry_ref = refs[12:14]
    outs = refs[14:18]
    g_table = refs[18]
    packed = refs[19]
    stages = refs[20:24]
    sems, out_sems = refs[24:]
    core = place_ref[3]
    copies = []
    for n in range(2):
        owner = core if n == 0 else 1 - core
        for part in range(3):
            half, quarter = quarter_bits(place_ref[part], owner)
            for far in range(2):
                for second in range(2):
                    h = half if far == 0 else 1 - half
                    q = quarter if second == 0 else 1 - quarter
                    piece = owner * 12 + part * 4 + h * 2 + q
                    copies.append(
                        pltpu.make_async_copy(
                            sources[n * 6 + part * 2 + far].at[pl.ds(second * PIECE, PIECE), :],
                            packed.at[pl.ds(pl.multiple_of(piece * PIECE, 16), PIECE), :],
                            sems.at[len(copies)],
                        )
                    )
    for copy in copies:
        copy.start()
    for copy in copies:
        copy.wait()

    def add_squares(b, acc):
        block = packed[pl.ds(pl.multiple_of(b * C, C), C), :].astype(F32)
        return acc + jnp.sum((block * block).reshape(4, C // 32, 8, 128), 1)

    squares = lax.fori_loop(0, BLOCKS, add_squares, jnp.zeros((4, 8, 128), F32))

    base = BLOCKS * C
    by_row = jnp.zeros((48, 256), F32)
    for jr in range(SIDE):
        rows = jnp.concatenate(
            [packed[base + b * PAD + 8 * jr : base + b * PAD + 8 * jr + 8, :].astype(F32) for b in range(6)], 0
        )
        by_row = by_row + nn(rows.astype(BF16), map_ref[jr])
    high = by_row.astype(BF16)
    rest = by_row - high.astype(F32)
    mid = rest.astype(BF16)
    low = (rest - mid.astype(F32)).astype(BF16)
    table = jnp.zeros((16, 256), F32)
    for jc in range(SIDE):
        for part in (high, mid, low):
            picked = jnp.concatenate(
                [
                    part[b * 8 + jc : b * 8 + jc + 1, head * 128 : (head + 1) * 128].astype(F32)
                    for b in range(6)
                    for head in range(2)
                ]
                + [jnp.zeros((4, 128), F32)],
                0,
            )
            table = table + nn(picked.astype(BF16), entry_ref[jc])
    norm_sq = jnp.sum(squares) + jnp.sum(table * table)
    norm = jnp.sqrt(jnp.full((8, 128), norm_sq, F32))
    factor = jnp.minimum(1.0, math.sqrt(PARAMS) / (norm + 1e-06))[:1, :]
    g_table[...] = (table * factor[:, :1])[:HEADS, :TABLE]

    first = 0
    for n in range(4):
        stage, out, sem = stages[n], outs[n], out_sems.at[n]

        def scale_block(b, carry, first=first, n=n, stage=stage, out=out, sem=sem):
            rows = pl.ds(pl.multiple_of((first + b) * C, C), C)
            block = packed[rows, :].astype(F32) * factor
            strip = pl.ds(pl.multiple_of(b * 128, 128), 128)
            if n == 3:
                stage[strip, :] = block.T
                pltpu.make_async_copy(stage.at[strip, :], out.at[strip, :], sem).start()
            else:
                stage[:, strip] = block
                pltpu.make_async_copy(stage.at[:, strip], out.at[:, strip], sem).start()
            return carry

        count = stage.shape[0] // 128 if n == 3 else stage.shape[1] // 128
        lax.fori_loop(0, count, scale_block, 0)
        first += count
    for n in range(4):
        pltpu.make_async_copy(stages[n], outs[n], out_sems.at[n]).wait()


def run_last(place, pieces, row_map, entry_map):
    hbm = pl.BlockSpec(memory_space=pl.ANY)

    def whole(shape):
        return pl.BlockSpec(shape, lambda i, p: (0,) * len(shape))

    shapes = [(C, 3 * C), (C, C), (C, FFN), (FFN, C), (HEADS, TABLE)]
    return pl.pallas_call(
        last_body,
        grid_spec=pltpu.PrefetchScalarGridSpec(
            num_scalar_prefetch=1,
            grid=(1,),
            in_specs=[hbm] * 12 + [whole(row_map.shape), whole(entry_map.shape)],
            out_specs=[hbm] * 4 + [whole(shapes[4])],
            scratch_shapes=[
                pltpu.VMEM((ROWS, 128), BF16),
                *[pltpu.VMEM(s, F32) for s in shapes[:4]],
                pltpu.SemaphoreType.DMA((24,)),
                pltpu.SemaphoreType.DMA((4,)),
            ],
        ),
        out_shape=[jax.ShapeDtypeStruct(s, F32) for s in shapes],
        compiler_params=pltpu.CompilerParams(vmem_limit_bytes=40 * 1024 * 1024),
        name="clip",
    )(place, *pieces, row_map, entry_map)


def sum_over_devices(keep, send):
    near, far = [], []
    for p in range(3):
        with jax.named_scope(f"core_{p}"):
            got = swap(send[p], 3)
        held = keep[p][:PIECE].astype(F32) + got[:PIECE].astype(F32)
        other_quarter = keep[p][PIECE : 2 * PIECE].astype(F32) + got[PIECE : 2 * PIECE].astype(F32)
        other_half = add(keep[p][2 * PIECE :], got[2 * PIECE :])
        with jax.named_scope(f"halve_{p}"):
            got = swap(other_half, p, 0)
        with jax.named_scope(f"quarter_{p}"):
            back = swap(add(other_quarter, got[PIECE:]), p, 1)
        held = add(held, got[:PIECE], back)
        for stage in (1, 2):
            for turn in (0, 1):
                with jax.named_scope(f"double_{stage}{turn}_{p}"):
                    held = add(held, swap(held, (p + stage) % 3, turn))
        with jax.named_scope(f"gather_{p}"):
            half = jnp.concatenate([held, swap(held, p, 1)], 0)
        near.append(half)
        with jax.named_scope(f"regather_{p}"):
            far.append(swap(half, p, 0))
    mine = [value for p in range(3) for value in (near[p], far[p])]
    other = []
    for n, value in enumerate(mine):
        with jax.named_scope(f"recore_{n}"):
            other.append(swap(value, 3))
    return mine + other


def from_behind(x, steps):
    sizes = [lax.axis_size(axis) for axis in AXES]
    pairs = []
    for i in range(sizes[0]):
        for j in range(sizes[1]):
            to = ((i + steps[0]) % sizes[0]) * sizes[1] + (j + steps[1]) % sizes[1]
            pairs.append((i * sizes[1] + j, to))
    return lax.ppermute(x, AXES, pairs)


def send_rims(low, right, corner, by):
    return from_behind(low, (by, 0)), from_behind(right, (0, by)), from_behind(corner, (by, by))


def place_rims(n, tile, low, right, corner):
    inner = TILE - SHIFT
    rows = jnp.concatenate([low[n], tile[:inner]], 0)
    left = jnp.concatenate([corner[n, :, :SHIFT], right[n, :inner, :SHIFT]], 0)
    left = jnp.pad(left, ((0, 0), (0, inner), (0, 0)))
    col = lax.broadcasted_iota(jnp.int32, rows.shape, 1)
    return jnp.where(col < SHIFT, left, rows)


def window_tables(bias_table, rel_index):
    by_offset = rel_index.reshape(SIDE, SIDE, SIDE, SIDE)
    spread_out = jnp.pad(
        by_offset.transpose(2, 3, 0, 1), ((0, 1), (0, 1), (0, 1), (0, 1)), constant_values=-1
    ).reshape(PAD * PAD)
    lookup = (spread_out[None, :] == jnp.arange(TABLE, dtype=jnp.int32)[:, None]).astype(F32)
    bias = jnp.dot(bias_table.T, lookup, precision=lax.Precision.HIGHEST)
    bias = bias.reshape(HEADS, PAD, PAD).transpose(1, 0, 2).reshape(PAD, HEADS * PAD)
    entries = jnp.concatenate(
        [by_offset[0, :, :0:-1, :].transpose(1, 0, 2), by_offset[:, :, 0, :]], 0
    )
    entries = entries.transpose(2, 0, 1).reshape(SIDE, 13 * SIDE)
    entries = jnp.pad(entries, ((0, 0), (0, 128 - 13 * SIDE)), constant_values=-1)
    entry_map = (entries[:, :, None] == jnp.arange(256, dtype=jnp.int32)).astype(BF16)
    return bias, entry_map


def local(tokens, cotangent, w_qkv, w_proj, w_fc1, w_fc2, bias_table, rel_index, region):
    index = lax.axis_index("ha") * 16 + lax.axis_index("wa")
    place = jnp.stack(coordinates(index)).astype(jnp.int32)
    rims = send_rims(*cut_rims(tokens, cotangent), -1)
    bias, entry_map = window_tables(bias_table, rel_index)
    windows = region.reshape(4, SIDE, 4, SIDE).transpose(0, 2, 1, 3).astype(F32)
    windows = jnp.pad(windows, ((0, 0), (0, 0), (0, 1), (0, 1)), constant_values=-1.0)
    reg_lane = jnp.tile(windows.reshape(16, PAD), (1, 4)).reshape(16, 1, BAND)
    into, back = band_maps()
    out, tgrad, low, right, corner, *parts = run_main(
        place,
        (tokens, cotangent),
        rims,
        reg_lane,
        bias,
        jnp.asarray(into, BF16),
        jnp.asarray(back, BF16),
        (w_qkv, w_proj, w_fc1, w_fc2),
    )
    rims = send_rims(low, right, corner, 1)
    pieces = sum_over_devices(parts[:3], parts[3:])
    *grads, table = run_last(place, pieces, jnp.asarray(table_map(), BF16), entry_map)
    return (place_rims(0, out, *rims), place_rims(1, tgrad, *rims), *grads, table.T)


def solution(mesh):
    tiled = P("ha", "wa", None)
    return jax.shard_map(
        local,
        mesh=mesh,
        in_specs=(tiled, tiled, P(), P(), P(), P(), P(), P(), P("ha", "wa")),
        out_specs=(tiled, tiled, P(), P(), P(), P(), P()),
        check_vma=False,
    )
```

```python
import math

import jax
import jax.numpy as jnp
import numpy as np
from jax import lax
from jax.experimental import pallas as pl
from jax.experimental.pallas import tpu as pltpu
from jax.sharding import PartitionSpec as P

HEADS = 12
SIDE = 7
SHIFT = 3
HEAD_DIM = 32
WINDOW = 49
TABLE = 169
PARAMS = 1771500
C = 384
FFN = 1536
TILE = 28
PAD = 64
BAND = 4 * PAD
COLS = 48
RIM = 32
EDGE = 4
GROUPS = 3
CHUNK = 256
BLOCKS = 36
BIAS = BLOCKS * C
PIECE = 896
PARTS = 2
ROWS = 2 * PARTS * 4 * PIECE

EPSILON = 1e-05
SCALE = HEAD_DIM ** (-0.5)
AXES = ("ha", "wa")
F32 = jnp.float32
BF16 = jnp.bfloat16


def row_place(position):
    return (position // SIDE) * 8 + position % SIDE


def band_maps():
    into = np.zeros((BAND, SIDE * COLS), np.float32)
    back = np.zeros((SIDE * COLS, BAND), np.float32)
    for row in range(SIDE):
        for col in range(TILE):
            place = (col // SIDE) * PAD + row * 8 + col % SIDE
            at = col + SHIFT if col + SHIFT < TILE else RIM + col + SHIFT - TILE
            into[place, row * COLS + at] = 1.0
            back[row * COLS + at, place] = 1.0
    return into, back


def nn(a, b):
    return jnp.dot(a, b, preferred_element_type=F32)


def nt(a, b):
    return lax.dot_general(a, b, (((1,), (1,)), ((), ())), preferred_element_type=F32)


def tn(a, b):
    return lax.dot_general(a, b, (((0,), (0,)), ((), ())), preferred_element_type=F32)


def normalize(values):
    average = jnp.mean(values, -1, keepdims=True)
    centred = values - average
    inverse = lax.rsqrt(jnp.mean(centred * centred, -1, keepdims=True) + EPSILON)
    return centred * inverse, inverse


def normalize_back(normal_rows, inverse, upstream):
    up_mean = jnp.mean(upstream, -1, keepdims=True)
    cross_mean = jnp.mean(upstream * normal_rows, -1, keepdims=True)
    return inverse * (upstream - up_mean - normal_rows * cross_mean)


def gelu_parts(v):
    density = jnp.exp(v * v * -0.5) * (2.0 * math.pi) ** (-0.5)
    t = 1.0 / (1.0 + (0.3275911 * 2.0 ** (-0.5)) * jnp.abs(v))
    half = 0.5 * (2.0 * math.pi) ** 0.5
    poly = 1.061405429 * half
    for factor in (-1.453152027, 1.421413741, -0.284496736, 0.254829592):
        poly = poly * t + factor * half
    upper = poly * t * density
    return jnp.where(v >= 0, 1.0 - upper, upper), density


def spread(rows):
    tall = jnp.concatenate([rows] * 4, 0)
    head_row = lax.broadcasted_iota(jnp.int32, (BAND, 128), 0) // PAD
    head_lane = lax.broadcasted_iota(jnp.int32, (BAND, 128), 1) // HEAD_DIM
    return jnp.where(head_row == head_lane, tall, jnp.zeros_like(tall))


def gather_heads(tall):
    head_lane = lax.broadcasted_iota(jnp.int32, (PAD, 128), 1) // HEAD_DIM
    out = jnp.where(head_lane == 0, tall[:PAD], 0.0)
    for h in range(1, 4):
        out = out + jnp.where(head_lane == h, tall[h * PAD : (h + 1) * PAD], 0.0)
    return out


def main_body(
    place_ref,
    tokens_ref,
    cot_ref,
    low_ref,
    right_ref,
    corner_ref,
    reg_lane_ref,
    bias_ref,
    into_ref,
    back_ref,
    w_qkv_ref,
    w_proj_ref,
    w_fc1_ref,
    w_fc2_ref,
    out_ref,
    tgrad_ref,
    low_out,
    right_out,
    corner_out,
    keep_0,
    keep_1,
    send_0,
    send_1,
    rows_s,
    qkv_s,
    probs_s,
    attn_s,
    gattn_s,
    dqkv_s,
    a_qkv,
    a_proj,
    a_fc1,
    a_fc2,
    a_bias,
    pre_s,
    up_s,
    act_s,
    gpre_s,
    ffn_s,
    second_s,
    packed,
    sems,
):
    step = pl.program_id(0)

    @pl.when(step == 0)
    def _():
        for ref in (a_qkv, a_proj, a_fc1, a_fc2, a_bias):
            ref[...] = jnp.zeros_like(ref)
        rows_s[...] = jnp.zeros_like(rows_s)
        for n, ref in enumerate((tokens_ref, cot_ref)):
            rows_s[n, : TILE - SHIFT, :TILE, :] = ref[SHIFT:]
            rows_s[n, TILE - SHIFT :, :TILE, :] = low_ref[n]
            rows_s[n, : TILE - SHIFT, RIM : RIM + EDGE, :] = right_ref[n, SHIFT:]
            rows_s[n, TILE - SHIFT :, RIM : RIM + EDGE, :] = corner_ref[n]

    into = into_ref[...]
    back = back_ref[...]
    band = pl.ds(step * SIDE, SIDE)
    x = nn(into, rows_s[0, band].reshape(SIDE * COLS, C))
    cot = nn(into, rows_s[1, band].reshape(SIDE * COLS, C))

    def same_region(w):
        across = reg_lane_ref[w]
        down = jnp.broadcast_to(across[:, :128], (128, 128)).T[:PAD]
        return jnp.concatenate([down, down], 1) == across

    def put_back(n, ref, values):
        rows = nn(back, values).astype(BF16).reshape(SIDE, COLS, C)
        ref[...] = rows[:, :TILE]
        right_out[n] = rows[:, RIM : RIM + EDGE]

        @pl.when(step == pl.num_programs(0) - 1)
        def _():
            low_out[n] = rows[SIDE - SHIFT :, :TILE]
            corner_out[n] = rows[SIDE - SHIFT :, RIM : RIM + EDGE]

    cot_low = cot.astype(BF16)
    n1, inv1 = normalize(x)
    n1_low = n1.astype(BF16)
    qkv_s[...] = nn(n1_low, w_qkv_ref[...]).astype(BF16)

    def parts(rows, g):
        lanes = slice(g * 128, (g + 1) * 128)
        return [
            qkv_s[rows, pl.ds(k * C + g * 128, 128)] for k in range(3)
        ], lanes

    def forward_windows(pair, carry):
        chains = []
        for n in range(2):
            w = pair * 2 + n
            rows = pl.ds(pl.multiple_of(w * PAD, PAD), PAD)
            same = same_region(w)
            for g in range(GROUPS):
                (q, k, v), lanes = parts(rows, g)
                scores = nt(k, spread(q)) * SCALE + bias_ref[:, g * BAND : (g + 1) * BAND]
                chains.append((w, g, rows, lanes, v, jnp.where(same, scores, -1e30)))
        for w, g, rows, lanes, v, scores in chains:
            exponent = jnp.exp(scores - jnp.max(scores, 0, keepdims=True))
            probs = exponent * (1.0 / jnp.sum(exponent, 0, keepdims=True))
            probs_s[w, g] = probs
            attn_s[rows, lanes] = gather_heads(tn(probs.astype(BF16), v)).astype(BF16)
        return carry

    lax.fori_loop(0, 2, forward_windows, 0)

    attn = attn_s[...]
    projected = nn(attn, w_proj_ref[...]).astype(BF16).astype(F32)
    middle = x + projected
    n2, inv2 = normalize(middle)
    n2_low = n2.astype(BF16)
    n2_t = n2_low.T
    cot_t = cot_low.T
    def enter(f):
        hidden = slice(f, f + CHUNK)
        pre_s[:, hidden] = nn(n2_low, w_fc1_ref[:, hidden])
        up_s[:, hidden] = nt(cot_low, w_fc2_ref[hidden, :])

    def bend(f):
        hidden = slice(f, f + CHUNK)
        pre = pre_s[:, hidden]
        cdf, density = gelu_parts(pre)
        act_s[:, hidden] = (pre * cdf).astype(BF16)
        gpre_s[:, hidden] = (up_s[:, hidden] * (cdf + pre * density)).astype(BF16)

    def leave(f):
        hidden = slice(f, f + CHUNK)
        activated, grad_pre = act_s[:, hidden], gpre_s[:, hidden]
        a_fc2[:, hidden] += nn(cot_t, activated)
        a_fc1[:, hidden] += nn(n2_t, grad_pre)
        forward = nn(activated, w_fc2_ref[hidden, :])
        backward = nt(grad_pre, w_fc1_ref[:, hidden])
        ffn_s[...] = forward if f == 0 else ffn_s[...] + forward
        second_s[...] = backward if f == 0 else second_s[...] + backward

    enter(0)
    for f in range(0, FFN + CHUNK, CHUNK):
        if f + CHUNK < FFN:
            enter(f + CHUNK)
        if f < FFN:
            bend(f)
        if f > 0:
            leave(f - CHUNK)
    ffn_out = ffn_s[...]
    grad_second = second_s[...]

    put_back(0, out_ref, (middle + ffn_out).astype(BF16))

    grad_mid = cot + normalize_back(n2, inv2, grad_second)
    grad_proj = grad_mid.astype(BF16)
    a_proj[...] += nn(attn.T, grad_proj)
    gattn_s[...] = nt(grad_proj, w_proj_ref[...]).astype(BF16)

    def backward_windows(pair, carry):
        chains = []
        for n in range(2):
            w = pair * 2 + n
            rows = pl.ds(pl.multiple_of(w * PAD, PAD), PAD)
            for g in range(GROUPS):
                (q, k, v), lanes = parts(rows, g)
                grad_tall = spread(gattn_s[rows, lanes])
                grad_probs = nt(v, grad_tall)
                grad_v = nn(probs_s[w, g].astype(BF16), grad_tall)
                dqkv_s[rows, pl.ds(2 * C + g * 128, 128)] = grad_v.astype(BF16)
                chains.append((w, g, rows, q, k, grad_probs))
        for w, g, rows, q, k, grad_probs in chains:
            probs = probs_s[w, g]
            weighted = probs * grad_probs
            grad_scores = weighted - probs * jnp.sum(weighted, 0, keepdims=True)
            a_bias[:, g * BAND : (g + 1) * BAND] += grad_scores
            scaled = (grad_scores * SCALE).astype(BF16)
            grad_k = nn(scaled, spread(q))
            grad_q = gather_heads(tn(scaled, k))
            for n, value in enumerate((grad_q, grad_k)):
                dqkv_s[rows, pl.ds(n * C + g * 128, 128)] = value.astype(BF16)
        return carry

    lax.fori_loop(0, 2, backward_windows, 0)

    dqkv = dqkv_s[...]
    a_qkv[...] += nn(n1_low.T, dqkv)
    grad_normed = nt(dqkv, w_qkv_ref[...]).astype(BF16).astype(F32)
    token_grad = (grad_mid + normalize_back(n1, inv1, grad_normed)).astype(BF16)
    put_back(1, tgrad_ref, token_grad)

    @pl.when(step == pl.num_programs(0) - 1)
    def _():
        at = 0
        for ref in (a_qkv, a_proj, a_fc1, a_fc2):
            for b in range(ref.shape[1] // 128):
                packed[at : at + C, :] = ref[:, b * 128 : (b + 1) * 128].astype(BF16)
                at += C
        for b in range(6):
            packed[at : at + PAD, :] = a_bias[:, b * 128 : (b + 1) * 128].astype(BF16)
            at += PAD
        packed[at:, :] = jnp.zeros((ROWS - at, 128), BF16)
        core = place_ref[3]
        copies = []
        for refs, owner in (((send_0, send_1), 1 - core), ((keep_0, keep_1), core)):
            for p in range(PARTS):
                half, quarter = quarter_bits(place_ref[p], owner)
                pieces = (
                    half * 2 + quarter,
                    half * 2 + 1 - quarter,
                    (1 - half) * 2 + quarter,
                    (1 - half) * 2 + 1 - quarter,
                )
                for n, piece in enumerate(pieces):
                    at = ((owner * PARTS + p) * 4 + piece) * PIECE
                    copies.append(
                        pltpu.make_async_copy(
                            packed.at[pl.ds(pl.multiple_of(at, 16), PIECE), :],
                            refs[p].at[pl.ds(n * PIECE, PIECE), :],
                            sems.at[len(copies)],
                        )
                    )
        for copy in copies:
            copy.start()
        for copy in copies:
            copy.wait()


def run_main(place, tiles, rims, reg_lane, bias, into, back, weights):
    def whole(a):
        return pl.BlockSpec(a.shape, lambda i, c: (0,) * a.ndim, pipeline_mode=pl.Buffered(1))

    def resident(shape):
        return pl.BlockSpec(shape, lambda i, c: (0,) * len(shape))

    band = pl.BlockSpec((SIDE, TILE, C), lambda i, c: (i, 0, 0))
    hbm = pl.BlockSpec(memory_space=pl.ANY)
    grid_spec = pltpu.PrefetchScalarGridSpec(
        num_scalar_prefetch=1,
        grid=(4,),
        in_specs=[
            *[whole(a) for a in (*tiles, *rims)],
            pl.BlockSpec((4, 1, BAND), lambda i, c: (i, 0, 0)),
            *[whole(a) for a in (bias, into, back, *weights)],
        ],
        out_specs=[
            band,
            band,
            resident(rims[0].shape),
            pl.BlockSpec((2, SIDE, EDGE, C), lambda i, c: (0, i, 0, 0)),
            resident(rims[2].shape),
            *[hbm] * (2 * PARTS),
        ],
        scratch_shapes=[
            pltpu.VMEM((2, TILE, COLS, C), BF16),
            pltpu.VMEM((BAND, 3 * C), BF16),
            pltpu.VMEM((4, GROUPS, PAD, BAND), F32),
            pltpu.VMEM((BAND, C), BF16),
            pltpu.VMEM((BAND, C), BF16),
            pltpu.VMEM((BAND, 3 * C), BF16),
            pltpu.VMEM((C, 3 * C), F32),
            pltpu.VMEM((C, C), F32),
            pltpu.VMEM((C, FFN), F32),
            pltpu.VMEM((C, FFN), F32),
            pltpu.VMEM((PAD, HEADS * PAD), F32),
            pltpu.VMEM((BAND, FFN), F32),
            pltpu.VMEM((BAND, FFN), F32),
            pltpu.VMEM((BAND, FFN), BF16),
            pltpu.VMEM((BAND, FFN), BF16),
            pltpu.VMEM((BAND, C), F32),
            pltpu.VMEM((BAND, C), F32),
            pltpu.VMEM((ROWS, 128), BF16),
            pltpu.SemaphoreType.DMA((8 * PARTS,)),
        ],
    )
    third = jax.ShapeDtypeStruct((4 * PIECE, 128), BF16)
    return pl.pallas_call(
        main_body,
        grid_spec=grid_spec,
        out_shape=[jax.ShapeDtypeStruct(a.shape, BF16) for a in (*tiles, *rims)] + [third] * (2 * PARTS),
        compiler_params=pltpu.CompilerParams(
            dimension_semantics=("arbitrary",), vmem_limit_bytes=56 * 1024 * 1024
        ),
        name="block",
    )(place, *tiles, *rims, reg_lane, bias, into, back, *weights)


def rims_body(tokens_low, tokens_left, cot_low, cot_left, low_ref, right_ref, corner_ref):
    for n, (low, left) in enumerate(((tokens_low, tokens_left), (cot_low, cot_left))):
        low_ref[n] = low[...]
        right_ref[n] = left[:, :EDGE]
        corner_ref[n] = left[:SHIFT, :EDGE]


def cut_rims(tokens, cot):
    low = pl.BlockSpec((SHIFT, TILE, C), lambda i: (0, 0, 0))
    left = pl.BlockSpec((TILE, 16, C), lambda i: (0, 0, 0))
    shapes = [(2, SHIFT, TILE, C), (2, TILE, EDGE, C), (2, SHIFT, EDGE, C)]
    return pl.pallas_call(
        rims_body,
        grid=(1,),
        in_specs=[low, left, low, left],
        out_specs=[pl.BlockSpec(s, lambda i: (0, 0, 0, 0)) for s in shapes],
        out_shape=[jax.ShapeDtypeStruct(s, BF16) for s in shapes],
        name="rims",
    )(tokens, tokens, cot, cot)


def coordinates(index):
    ha, wa = index // 16, index % 16
    return (wa // 4, ha // 2, (wa // 2 % 2) * 2 + ha % 2, wa % 2)


def device_at(x, y, z, core):
    return (y * 2 + z % 2) * 16 + x * 4 + (z // 2) * 2 + core


def swap(value, axis, turn=0):
    pairs = []
    for index in range(128):
        place = list(coordinates(index))
        if axis == 3:
            place[3] = 1 - place[3]
        elif (turn + place[3]) % 2 == 0:
            place[axis] = place[axis] ^ 1
        else:
            place[axis] = 3 - place[axis]
        pairs.append((index, device_at(*place)))
    return lax.ppermute(value, AXES, pairs)


def quarter_bits(place, core):
    inner = lax.rem(lax.div(place + 1, 2), 2)
    upper = lax.div(place, 2)
    return inner + core * (upper - inner), upper + core * (inner - upper)


def add(*values):
    total = values[0].astype(F32)
    for value in values[1:]:
        total = total + value.astype(F32)
    return total.astype(BF16)


def table_map():
    out = np.zeros((SIDE, 128, 256), np.float32)
    for jr in range(SIDE):
        for head in range(2):
            for ir in range(SIDE):
                for ic in range(SIDE):
                    out[jr, head * PAD + 8 * ir + ic, head * 128 + (ir - jr + 6) * SIDE + ic] = 1.0
    return out


def last_body(place_ref, squares_ref, *refs):
    sources = refs[: 4 * PARTS]
    map_ref, entry_ref, *outs, g_table, packed = refs[4 * PARTS : 4 * PARTS + 8]
    stages = refs[4 * PARTS + 8 : 4 * PARTS + 12]
    sems, out_sems = refs[4 * PARTS + 12 :]
    core = place_ref[3]
    copies = []
    for n in range(2):
        owner = core if n == 0 else 1 - core
        for part in range(PARTS):
            half, quarter = quarter_bits(place_ref[part], owner)
            for far in range(2):
                for second in range(2):
                    h = half if far == 0 else 1 - half
                    q = quarter if second == 0 else 1 - quarter
                    piece = (owner * PARTS + part) * 4 + h * 2 + q
                    copies.append(
                        pltpu.make_async_copy(
                            sources[(n * PARTS + part) * 2 + far].at[pl.ds(second * PIECE, PIECE), :],
                            packed.at[pl.ds(pl.multiple_of(piece * PIECE, 16), PIECE), :],
                            sems.at[len(copies)],
                        )
                    )
    for copy in copies:
        copy.start()
    for copy in copies:
        copy.wait()

    base = BIAS
    by_row = jnp.zeros((48, 256), F32)
    for jr in range(SIDE):
        rows = jnp.concatenate(
            [packed[base + b * PAD + 8 * jr : base + b * PAD + 8 * jr + 8, :].astype(F32) for b in range(6)], 0
        )
        by_row = by_row + nn(rows.astype(BF16), map_ref[jr])
    high = by_row.astype(BF16)
    rest = by_row - high.astype(F32)
    mid = rest.astype(BF16)
    low = (rest - mid.astype(F32)).astype(BF16)
    table = jnp.zeros((16, 256), F32)
    for jc in range(SIDE):
        for part in (high, mid, low):
            picked = jnp.concatenate(
                [
                    part[b * 8 + jc : b * 8 + jc + 1, head * 128 : (head + 1) * 128].astype(F32)
                    for b in range(6)
                    for head in range(2)
                ]
                + [jnp.zeros((4, 128), F32)],
                0,
            )
            table = table + nn(picked.astype(BF16), entry_ref[jc])
    norm_sq = jnp.sum(squares_ref[...]) + jnp.sum(table * table)
    norm = jnp.sqrt(jnp.full((8, 128), norm_sq, F32))
    factor = jnp.minimum(1.0, math.sqrt(PARAMS) / (norm + 1e-06))[:1, :]
    g_table[...] = (table * factor[:, :1])[:HEADS, :TABLE]

    first = 0
    for n in range(4):
        stage, out, sem = stages[n], outs[n], out_sems.at[n]

        def scale_block(b, carry, first=first, n=n, stage=stage, out=out, sem=sem):
            rows = pl.ds(pl.multiple_of((first + b) * C, C), C)
            block = packed[rows, :].astype(F32) * factor
            strip = pl.ds(pl.multiple_of(b * 128, 128), 128)
            if n == 3:
                stage[strip, :] = block.T
                pltpu.make_async_copy(stage.at[strip, :], out.at[strip, :], sem).start()
            else:
                stage[:, strip] = block
                pltpu.make_async_copy(stage.at[:, strip], out.at[:, strip], sem).start()
            return carry

        count = stage.shape[0] // 128 if n == 3 else stage.shape[1] // 128
        lax.fori_loop(0, count, scale_block, 0)
        first += count
    for n in range(4):
        pltpu.make_async_copy(stages[n], outs[n], out_sems.at[n]).wait()


def run_last(place, squares, pieces, row_map, entry_map):
    hbm = pl.BlockSpec(memory_space=pl.ANY)

    def whole(shape):
        return pl.BlockSpec(shape, lambda i, p: (0,) * len(shape))

    shapes = [(C, 3 * C), (C, C), (C, FFN), (FFN, C), (HEADS, TABLE)]
    return pl.pallas_call(
        last_body,
        grid_spec=pltpu.PrefetchScalarGridSpec(
            num_scalar_prefetch=1,
            grid=(1,),
            in_specs=[whole((8, 128)), *[hbm] * (4 * PARTS), whole(row_map.shape), whole(entry_map.shape)],
            out_specs=[hbm] * 4 + [whole(shapes[4])],
            scratch_shapes=[
                pltpu.VMEM((ROWS, 128), BF16),
                *[pltpu.VMEM(s, F32) for s in shapes[:4]],
                pltpu.SemaphoreType.DMA((8 * PARTS,)),
                pltpu.SemaphoreType.DMA((4,)),
            ],
        ),
        out_shape=[jax.ShapeDtypeStruct(s, F32) for s in shapes],
        compiler_params=pltpu.CompilerParams(vmem_limit_bytes=40 * 1024 * 1024),
        name="clip",
    )(place, squares, *pieces, row_map, entry_map)


def squares_of(values, is_last):
    values = values.astype(F32).reshape(2, PIECE // 8, 8, 128)
    if is_last is not None:
        block = lax.broadcasted_iota(jnp.int32, values.shape[:3] + (1,), 1)
        hidden = (block * 8 >= BIAS % PIECE) & (is_last.reshape(2, 1, 1, 1) > 0)
        values = jnp.where(hidden, 0.0, values)
    by_piece = jnp.sum(values * values, 1)
    return by_piece[0] + by_piece[1]


def sum_over_devices(place, keep, send):
    near, far, squares = [], [], []
    for p in range(PARTS):
        with jax.named_scope(f"core_{p}"):
            got = swap(send[p], 3)
        held = keep[p][:PIECE].astype(F32) + got[:PIECE].astype(F32)
        other_quarter = keep[p][PIECE : 2 * PIECE].astype(F32) + got[PIECE : 2 * PIECE].astype(F32)
        other_half = add(keep[p][2 * PIECE :], got[2 * PIECE :])
        with jax.named_scope(f"halve_{p}"):
            got = swap(other_half, p, 0)
        with jax.named_scope(f"quarter_{p}"):
            back = swap(add(other_quarter, got[PIECE:]), p, 1)
        held = add(held, got[:PIECE], back)
        for stage in (1, 2):
            for turn in (0, 1):
                with jax.named_scope(f"double_{stage}{turn}_{p}"):
                    held = add(held, swap(held, (p + stage) % 3, turn))
        with jax.named_scope(f"gather_{p}"):
            half = jnp.concatenate([held, swap(held, p, 1)], 0)
        near.append(half)
        with jax.named_scope(f"regather_{p}"):
            far.append(swap(half, p, 0))
        last = [None, None]
        if p == PARTS - 1:
            h, q = quarter_bits(place[p], place[3])
            last = [place[3] * bit * jnp.stack([q, 1 - q]) for bit in (h, 1 - h)]
        squares.append(squares_of(near[p], last[0]) + squares_of(far[p], last[1]))
    mine = [value for p in range(PARTS) for value in (near[p], far[p])]
    other = []
    for n, value in enumerate(mine):
        with jax.named_scope(f"recore_{n}"):
            other.append(swap(value, 3))
    total = squares[0] + squares[1]
    with jax.named_scope("resquare"):
        total = total + swap(total, 3)
    return total, mine + other


def from_behind(x, steps):
    sizes = [lax.axis_size(axis) for axis in AXES]
    pairs = []
    for i in range(sizes[0]):
        for j in range(sizes[1]):
            to = ((i + steps[0]) % sizes[0]) * sizes[1] + (j + steps[1]) % sizes[1]
            pairs.append((i * sizes[1] + j, to))
    return lax.ppermute(x, AXES, pairs)


def send_rims(low, right, corner, by):
    return from_behind(low, (by, 0)), from_behind(right, (0, by)), from_behind(corner, (by, by))


def place_body(out_ref, tgrad_ref, low_ref, right_ref, corner_ref, after_ref, new_out, new_tgrad):
    inner = TILE - SHIFT
    col = lax.broadcasted_iota(jnp.int32, (inner, EDGE, C), 1)
    for n, (source, new) in enumerate(((out_ref, new_out), (tgrad_ref, new_tgrad))):
        new[:SHIFT] = low_ref[n]
        new[SHIFT:] = source[:inner]
        for rows, rim, old in (
            (slice(0, SHIFT), corner_ref[n], low_ref[n, :, :EDGE]),
            (slice(SHIFT, TILE), right_ref[n, :inner], source[:inner, :EDGE]),
        ):
            new[rows, :EDGE] = jnp.where(
                col[: rim.shape[0]] < SHIFT, rim.astype(F32), old.astype(F32)
            ).astype(BF16)


def place_rims(out, tgrad, low, right, corner, after):
    def whole(a):
        return pl.BlockSpec(a.shape, lambda i: (0,) * a.ndim)

    return pl.pallas_call(
        place_body,
        grid=(1,),
        in_specs=[*[whole(a) for a in (out, tgrad, low, right, corner)], pl.BlockSpec(memory_space=pl.ANY)],
        out_specs=[whole(out), whole(tgrad)],
        out_shape=[jax.ShapeDtypeStruct(a.shape, BF16) for a in (out, tgrad)],
        name="place",
    )(out, tgrad, low, right, corner, after)


def window_tables(bias_table, rel_index):
    by_offset = rel_index.reshape(SIDE, SIDE, SIDE, SIDE)
    spread_out = jnp.pad(
        by_offset.transpose(2, 3, 0, 1), ((0, 1), (0, 1), (0, 1), (0, 1)), constant_values=-1
    ).reshape(PAD * PAD)
    lookup = (spread_out[None, :] == jnp.arange(TABLE, dtype=jnp.int32)[:, None]).astype(F32)
    bias = jnp.dot(bias_table.T, lookup, precision=lax.Precision.HIGHEST)
    bias = bias.reshape(HEADS, PAD, PAD).transpose(1, 0, 2).reshape(PAD, HEADS * PAD)
    entries = jnp.concatenate(
        [by_offset[0, :, :0:-1, :].transpose(1, 0, 2), by_offset[:, :, 0, :]], 0
    )
    entries = entries.transpose(2, 0, 1).reshape(SIDE, 13 * SIDE)
    entries = jnp.pad(entries, ((0, 0), (0, 128 - 13 * SIDE)), constant_values=-1)
    entry_map = (entries[:, :, None] == jnp.arange(256, dtype=jnp.int32)).astype(BF16)
    return bias, entry_map


def local(tokens, cotangent, w_qkv, w_proj, w_fc1, w_fc2, bias_table, rel_index, region):
    index = lax.axis_index("ha") * 16 + lax.axis_index("wa")
    place = jnp.stack(coordinates(index)).astype(jnp.int32)
    rims = send_rims(*cut_rims(tokens, cotangent), -1)
    bias, entry_map = window_tables(bias_table, rel_index)
    windows = region.reshape(4, SIDE, 4, SIDE).transpose(0, 2, 1, 3).astype(F32)
    windows = jnp.pad(windows, ((0, 0), (0, 0), (0, 1), (0, 1)), constant_values=-1.0)
    reg_lane = jnp.tile(windows.reshape(16, PAD), (1, 4)).reshape(16, 1, BAND)
    into, back = band_maps()
    out, tgrad, low, right, corner, *parts = run_main(
        place,
        (tokens, cotangent),
        rims,
        reg_lane,
        bias,
        jnp.asarray(into, BF16),
        jnp.asarray(back, BF16),
        (w_qkv, w_proj, w_fc1, w_fc2),
    )
    rims = send_rims(low, right, corner, 1)
    squares, pieces = sum_over_devices(place, parts[:PARTS], parts[PARTS:])
    block_out, token_grad = place_rims(out, tgrad, *rims, pieces[2])
    *grads, table = run_last(place, squares, pieces, jnp.asarray(table_map(), BF16), entry_map)
    return (block_out, token_grad, *grads, table.T)


def solution(mesh):
    tiled = P("ha", "wa", None)
    return jax.shard_map(
        local,
        mesh=mesh,
        in_specs=(tiled, tiled, P(), P(), P(), P(), P(), P(), P("ha", "wa")),
        out_specs=(tiled, tiled, P(), P(), P(), P(), P()),
        check_vma=False,
    )
```

```python
import math

import jax
import jax.numpy as jnp
import numpy as np
from jax import lax
from jax.experimental import pallas as pl
from jax.experimental.pallas import tpu as pltpu
from jax.sharding import PartitionSpec as P

HEADS = 12
SIDE = 7
SHIFT = 3
HEAD_DIM = 32
WINDOW = 49
TABLE = 169
PARAMS = 1771500
C = 384
FFN = 1536
TILE = 28
PAD = 64
BAND = 4 * PAD
COLS = 48
RIM = 32
EDGE = 4
GROUPS = 3
CHUNK = 256
BLOCKS = 36
BIAS = BLOCKS * C
PIECE = 592
PARTS = 3
ROWS = 2 * PARTS * 4 * PIECE

EPSILON = 1e-05
SCALE = HEAD_DIM ** (-0.5)
AXES = ("ha", "wa")
F32 = jnp.float32
BF16 = jnp.bfloat16


def row_place(position):
    return (position // SIDE) * 8 + position % SIDE


def band_maps():
    into = np.zeros((BAND, SIDE * COLS), np.float32)
    back = np.zeros((SIDE * COLS, BAND), np.float32)
    for row in range(SIDE):
        for col in range(TILE):
            place = (col // SIDE) * PAD + row * 8 + col % SIDE
            at = col + SHIFT if col + SHIFT < TILE else RIM + col + SHIFT - TILE
            into[place, row * COLS + at] = 1.0
            back[row * COLS + at, place] = 1.0
    return into, back


def nn(a, b):
    return jnp.dot(a, b, preferred_element_type=F32)


def nt(a, b):
    return lax.dot_general(a, b, (((1,), (1,)), ((), ())), preferred_element_type=F32)


def tn(a, b):
    return lax.dot_general(a, b, (((0,), (0,)), ((), ())), preferred_element_type=F32)


def normalize(values):
    average = jnp.mean(values, -1, keepdims=True)
    centred = values - average
    inverse = lax.rsqrt(jnp.mean(centred * centred, -1, keepdims=True) + EPSILON)
    return centred * inverse, inverse


def normalize_back(normal_rows, inverse, upstream):
    up_mean = jnp.mean(upstream, -1, keepdims=True)
    cross_mean = jnp.mean(upstream * normal_rows, -1, keepdims=True)
    return inverse * (upstream - up_mean - normal_rows * cross_mean)


def gelu_parts(v):
    density = jnp.exp(v * v * -0.5) * (2.0 * math.pi) ** (-0.5)
    t = 1.0 / (1.0 + (0.3275911 * 2.0 ** (-0.5)) * jnp.abs(v))
    half = 0.5 * (2.0 * math.pi) ** 0.5
    poly = 1.061405429 * half
    for factor in (-1.453152027, 1.421413741, -0.284496736, 0.254829592):
        poly = poly * t + factor * half
    upper = poly * t * density
    return jnp.where(v >= 0, 1.0 - upper, upper), density


def spread(rows):
    tall = jnp.concatenate([rows] * 4, 0)
    head_row = lax.broadcasted_iota(jnp.int32, (BAND, 128), 0) // PAD
    head_lane = lax.broadcasted_iota(jnp.int32, (BAND, 128), 1) // HEAD_DIM
    return jnp.where(head_row == head_lane, tall, jnp.zeros_like(tall))


def gather_heads(tall):
    head_lane = lax.broadcasted_iota(jnp.int32, (PAD, 128), 1) // HEAD_DIM
    out = jnp.where(head_lane == 0, tall[:PAD], 0.0)
    for h in range(1, 4):
        out = out + jnp.where(head_lane == h, tall[h * PAD : (h + 1) * PAD], 0.0)
    return out


def main_body(
    place_ref,
    tokens_ref,
    cot_ref,
    low_ref,
    right_ref,
    corner_ref,
    reg_lane_ref,
    bias_ref,
    into_ref,
    back_ref,
    w_qkv_far,
    w_proj_far,
    w_fc1_far,
    w_fc2_far,
    out_ref,
    tgrad_ref,
    low_out,
    right_out,
    corner_out,
    keep_0,
    keep_1,
    keep_2,
    send_0,
    send_1,
    send_2,
    rows_s,
    w_qkv_ref,
    w_proj_ref,
    w_fc1_ref,
    w_fc2_ref,
    qkv_s,
    probs_s,
    attn_s,
    gattn_s,
    dqkv_s,
    a_qkv,
    a_proj,
    a_fc1,
    a_fc2,
    a_bias,
    pre_s,
    up_s,
    act_s,
    gpre_s,
    ffn_s,
    second_s,
    packed,
    sems,
):
    step = pl.program_id(0)

    def weight_copy(n):
        far = (w_qkv_far, w_proj_far, w_fc1_far, w_fc2_far)[n]
        near = (w_qkv_ref, w_proj_ref, w_fc1_ref, w_fc2_ref)[n]
        return pltpu.make_async_copy(far, near, sems.at[n])

    @pl.when(step == 0)
    def _():
        for n in range(4):
            weight_copy(n).start()
        for ref in (a_qkv, a_proj, a_fc1, a_fc2, a_bias):
            ref[...] = jnp.zeros_like(ref)
        rows_s[...] = jnp.zeros_like(rows_s)
        for n, ref in enumerate((tokens_ref, cot_ref)):
            rows_s[n, : TILE - SHIFT, :TILE, :] = ref[SHIFT:]
            rows_s[n, TILE - SHIFT :, :TILE, :] = low_ref[n]
            rows_s[n, : TILE - SHIFT, RIM : RIM + EDGE, :] = right_ref[n, SHIFT:]
            rows_s[n, TILE - SHIFT :, RIM : RIM + EDGE, :] = corner_ref[n]

    into = into_ref[...]
    back = back_ref[...]
    band = pl.ds(step * SIDE, SIDE)
    x = nn(into, rows_s[0, band].reshape(SIDE * COLS, C))
    cot = nn(into, rows_s[1, band].reshape(SIDE * COLS, C))

    def same_region(w):
        across = reg_lane_ref[w]
        down = jnp.broadcast_to(across[:, :128], (128, 128)).T[:PAD]
        return jnp.concatenate([down, down], 1) == across

    def put_back(n, ref, values):
        rows = nn(back, values).astype(BF16).reshape(SIDE, COLS, C)
        ref[...] = rows[:, :TILE]
        right_out[n] = rows[:, RIM : RIM + EDGE]

        @pl.when(step == pl.num_programs(0) - 1)
        def _():
            low_out[n] = rows[SIDE - SHIFT :, :TILE]
            corner_out[n] = rows[SIDE - SHIFT :, RIM : RIM + EDGE]

    cot_low = cot.astype(BF16)
    n1, inv1 = normalize(x)
    n1_low = n1.astype(BF16)

    @pl.when(step == 0)
    def _():
        weight_copy(0).wait()

    qkv_s[...] = nn(n1_low, w_qkv_ref[...]).astype(BF16)

    def parts(rows, g):
        lanes = slice(g * 128, (g + 1) * 128)
        return [
            qkv_s[rows, pl.ds(k * C + g * 128, 128)] for k in range(3)
        ], lanes

    def forward_windows(pair, carry):
        chains = []
        for n in range(2):
            w = pair * 2 + n
            rows = pl.ds(pl.multiple_of(w * PAD, PAD), PAD)
            same = same_region(w)
            for g in range(GROUPS):
                (q, k, v), lanes = parts(rows, g)
                scores = nt(k, spread(q)) * SCALE + bias_ref[:, g * BAND : (g + 1) * BAND]
                chains.append((w, g, rows, lanes, v, jnp.where(same, scores, -1e30)))
        for w, g, rows, lanes, v, scores in chains:
            exponent = jnp.exp(scores - jnp.max(scores, 0, keepdims=True))
            probs = exponent * (1.0 / jnp.sum(exponent, 0, keepdims=True))
            probs_s[w, g] = probs
            attn_s[rows, lanes] = gather_heads(tn(probs.astype(BF16), v)).astype(BF16)
        return carry

    lax.fori_loop(0, 2, forward_windows, 0)

    @pl.when(step == 0)
    def _():
        for n in range(1, 4):
            weight_copy(n).wait()

    attn = attn_s[...]
    projected = nn(attn, w_proj_ref[...]).astype(BF16).astype(F32)
    middle = x + projected
    n2, inv2 = normalize(middle)
    n2_low = n2.astype(BF16)
    n2_t = n2_low.T
    cot_t = cot_low.T
    def enter(f):
        hidden = slice(f, f + CHUNK)
        pre_s[:, hidden] = nn(n2_low, w_fc1_ref[:, hidden])
        up_s[:, hidden] = nt(cot_low, w_fc2_ref[hidden, :])

    def bend(f):
        hidden = slice(f, f + CHUNK)
        pre = pre_s[:, hidden]
        cdf, density = gelu_parts(pre)
        act_s[:, hidden] = (pre * cdf).astype(BF16)
        gpre_s[:, hidden] = (up_s[:, hidden] * (cdf + pre * density)).astype(BF16)

    def leave(f):
        hidden = slice(f, f + CHUNK)
        activated, grad_pre = act_s[:, hidden], gpre_s[:, hidden]
        a_fc2[:, hidden] += nn(cot_t, activated)
        a_fc1[:, hidden] += nn(n2_t, grad_pre)
        forward = nn(activated, w_fc2_ref[hidden, :])
        backward = nt(grad_pre, w_fc1_ref[:, hidden])
        ffn_s[...] = forward if f == 0 else ffn_s[...] + forward
        second_s[...] = backward if f == 0 else second_s[...] + backward

    enter(0)
    for f in range(0, FFN + CHUNK, CHUNK):
        if f + CHUNK < FFN:
            enter(f + CHUNK)
        if f < FFN:
            bend(f)
        if f > 0:
            leave(f - CHUNK)
    ffn_out = ffn_s[...]
    grad_second = second_s[...]

    put_back(0, out_ref, (middle + ffn_out).astype(BF16))

    grad_mid = cot + normalize_back(n2, inv2, grad_second)
    grad_proj = grad_mid.astype(BF16)
    a_proj[...] += nn(attn.T, grad_proj)
    gattn_s[...] = nt(grad_proj, w_proj_ref[...]).astype(BF16)

    def backward_windows(pair, carry):
        chains = []
        for n in range(2):
            w = pair * 2 + n
            rows = pl.ds(pl.multiple_of(w * PAD, PAD), PAD)
            for g in range(GROUPS):
                (q, k, v), lanes = parts(rows, g)
                grad_tall = spread(gattn_s[rows, lanes])
                grad_probs = nt(v, grad_tall)
                grad_v = nn(probs_s[w, g].astype(BF16), grad_tall)
                dqkv_s[rows, pl.ds(2 * C + g * 128, 128)] = grad_v.astype(BF16)
                chains.append((w, g, rows, q, k, grad_probs))
        for w, g, rows, q, k, grad_probs in chains:
            probs = probs_s[w, g]
            weighted = probs * grad_probs
            grad_scores = weighted - probs * jnp.sum(weighted, 0, keepdims=True)
            a_bias[:, g * BAND : (g + 1) * BAND] += grad_scores
            scaled = (grad_scores * SCALE).astype(BF16)
            grad_k = nn(scaled, spread(q))
            grad_q = gather_heads(tn(scaled, k))
            for n, value in enumerate((grad_q, grad_k)):
                dqkv_s[rows, pl.ds(n * C + g * 128, 128)] = value.astype(BF16)
        return carry

    lax.fori_loop(0, 2, backward_windows, 0)

    dqkv = dqkv_s[...]
    a_qkv[...] += nn(n1_low.T, dqkv)
    grad_normed = nt(dqkv, w_qkv_ref[...]).astype(BF16).astype(F32)
    token_grad = (grad_mid + normalize_back(n1, inv1, grad_normed)).astype(BF16)
    put_back(1, tgrad_ref, token_grad)

    @pl.when(step == pl.num_programs(0) - 1)
    def _():
        at = 0
        for ref in (a_qkv, a_proj, a_fc1, a_fc2):
            for b in range(ref.shape[1] // 128):
                packed[at : at + C, :] = ref[:, b * 128 : (b + 1) * 128].astype(BF16)
                at += C
        for b in range(6):
            packed[at : at + PAD, :] = a_bias[:, b * 128 : (b + 1) * 128].astype(BF16)
            at += PAD
        core = place_ref[3]
        copies = []
        for refs, owner in (((send_0, send_1, send_2), 1 - core), ((keep_0, keep_1, keep_2), core)):
            for p in range(PARTS):
                half, quarter = quarter_bits(place_ref[p], owner)
                pieces = (
                    half * 2 + quarter,
                    half * 2 + 1 - quarter,
                    (1 - half) * 2 + quarter,
                    (1 - half) * 2 + 1 - quarter,
                )
                for n, piece in enumerate(pieces):
                    at = ((owner * PARTS + p) * 4 + piece) * PIECE
                    copies.append(
                        pltpu.make_async_copy(
                            packed.at[pl.ds(pl.multiple_of(at, 16), PIECE), :],
                            refs[p].at[pl.ds(n * PIECE, PIECE), :],
                            sems.at[len(copies)],
                        )
                    )
        for copy in copies:
            copy.start()
        for copy in copies:
            copy.wait()


def in_vmem(values):
    return [pltpu.with_memory_space_constraint(a, pltpu.VMEM) for a in values]


def run_main(place, tiles, rims, reg_lane, bias, into, back, weights):
    def resident(shape):
        return pl.BlockSpec(shape, lambda i, c: (0,) * len(shape))

    band = pl.BlockSpec((SIDE, TILE, C), lambda i, c: (i, 0, 0))
    here = pl.BlockSpec(memory_space=pltpu.VMEM)
    hbm = pl.BlockSpec(memory_space=pltpu.HBM)
    grid_spec = pltpu.PrefetchScalarGridSpec(
        num_scalar_prefetch=1,
        grid=(4,),
        in_specs=[
            *[here] * 5,
            pl.BlockSpec((4, 1, BAND), lambda i, c: (i, 0, 0)),
            *[here] * 3,
            *[hbm] * 4,
        ],
        out_specs=[
            band,
            band,
            resident(rims[0].shape),
            pl.BlockSpec((2, SIDE, EDGE, C), lambda i, c: (0, i, 0, 0)),
            resident(rims[2].shape),
            *[hbm] * PARTS,
            *[here] * PARTS,
        ],
        scratch_shapes=[
            pltpu.VMEM((2, TILE, COLS, C), BF16),
            pltpu.VMEM((C, 3 * C), BF16),
            pltpu.VMEM((C, C), BF16),
            pltpu.VMEM((C, FFN), BF16),
            pltpu.VMEM((FFN, C), BF16),
            pltpu.VMEM((BAND, 3 * C), BF16),
            pltpu.VMEM((4, GROUPS, PAD, BAND), F32),
            pltpu.VMEM((BAND, C), BF16),
            pltpu.VMEM((BAND, C), BF16),
            pltpu.VMEM((BAND, 3 * C), BF16),
            pltpu.VMEM((C, 3 * C), F32),
            pltpu.VMEM((C, C), F32),
            pltpu.VMEM((C, FFN), F32),
            pltpu.VMEM((C, FFN), F32),
            pltpu.VMEM((PAD, HEADS * PAD), F32),
            pltpu.VMEM((BAND, FFN), F32),
            pltpu.VMEM((BAND, FFN), F32),
            pltpu.VMEM((BAND, FFN), BF16),
            pltpu.VMEM((BAND, FFN), BF16),
            pltpu.VMEM((BAND, C), F32),
            pltpu.VMEM((BAND, C), F32),
            pltpu.VMEM((ROWS, 128), BF16),
            pltpu.SemaphoreType.DMA((8 * PARTS,)),
        ],
    )
    third = (4 * PIECE, 128)
    tiles, rims = in_vmem(tiles), in_vmem(rims)
    bias, into, back = in_vmem((bias, into, back))
    return pl.pallas_call(
        main_body,
        grid_spec=grid_spec,
        out_shape=[jax.ShapeDtypeStruct(a.shape, BF16) for a in (*tiles, *rims)]
        + [jax.ShapeDtypeStruct(third, BF16)] * PARTS
        + [pltpu.VMEM(third, BF16)] * PARTS,
        compiler_params=pltpu.CompilerParams(
            dimension_semantics=("arbitrary",), vmem_limit_bytes=59 * 1024 * 1024
        ),
        name="block",
    )(place, *tiles, *rims, reg_lane, bias, into, back, *weights)


def rims_body(tokens_low, tokens_left, cot_low, cot_left, low_ref, right_ref, corner_ref):
    for n, (low, left) in enumerate(((tokens_low, tokens_left), (cot_low, cot_left))):
        low_ref[n] = low[...]
        right_ref[n] = left[:, :EDGE]
        corner_ref[n] = left[:SHIFT, :EDGE]


def cut_rims(tokens, cot):
    low = pl.BlockSpec((SHIFT, TILE, C), lambda i: (0, 0, 0))
    left = pl.BlockSpec((TILE, 16, C), lambda i: (0, 0, 0))
    shapes = [(2, SHIFT, TILE, C), (2, TILE, EDGE, C), (2, SHIFT, EDGE, C)]
    return pl.pallas_call(
        rims_body,
        grid=(1,),
        in_specs=[low, left, low, left],
        out_specs=[pl.BlockSpec(s, lambda i: (0, 0, 0, 0)) for s in shapes],
        out_shape=[jax.ShapeDtypeStruct(s, BF16) for s in shapes],
        name="rims",
    )(tokens, tokens, cot, cot)


def coordinates(index):
    ha, wa = index // 16, index % 16
    return (wa // 4, ha // 2, (wa // 2 % 2) * 2 + ha % 2, wa % 2)


def device_at(x, y, z, core):
    return (y * 2 + z % 2) * 16 + x * 4 + (z // 2) * 2 + core


def swap(value, axis, turn=0):
    pairs = []
    for index in range(128):
        place = list(coordinates(index))
        if axis == 3:
            place[3] = 1 - place[3]
        elif (turn + place[3]) % 2 == 0:
            place[axis] = place[axis] ^ 1
        else:
            place[axis] = 3 - place[axis]
        pairs.append((index, device_at(*place)))
    return lax.ppermute(value, AXES, pairs)


def quarter_bits(place, core):
    inner = lax.rem(lax.div(place + 1, 2), 2)
    upper = lax.div(place, 2)
    return inner + core * (upper - inner), upper + core * (inner - upper)


def add(*values):
    total = values[0].astype(F32)
    for value in values[1:]:
        total = total + value.astype(F32)
    return total.astype(BF16)


def table_map():
    out = np.zeros((SIDE, 128, 256), np.float32)
    for jr in range(SIDE):
        for head in range(2):
            for ir in range(SIDE):
                for ic in range(SIDE):
                    out[jr, head * PAD + 8 * ir + ic, head * 128 + (ir - jr + 6) * SIDE + ic] = 1.0
    return out


def last_body(place_ref, *refs):
    sources = refs[: 4 * PARTS]
    map_ref, entry_ref, *outs, g_table, packed = refs[4 * PARTS : 4 * PARTS + 8]
    stages = refs[4 * PARTS + 8 : 4 * PARTS + 12]
    squares, out_sems = refs[4 * PARTS + 12 :]
    core = place_ref[3]

    def squares_of(values):
        values = values.astype(F32)
        return jnp.sum((values * values).reshape(-1, 8, 128), 0)

    behind = BIAS % PIECE
    for n in range(2):
        owner = core if n == 0 else 1 - core
        for part in range(PARTS):
            half, quarter = quarter_bits(place_ref[part], owner)
            for far in range(2):
                for second in range(2):
                    h = half if far == 0 else 1 - half
                    q = quarter if second == 0 else 1 - quarter
                    piece = (owner * PARTS + part) * 4 + h * 2 + q
                    values = sources[(n * PARTS + part) * 2 + far][second * PIECE : (second + 1) * PIECE, :]
                    packed[pl.ds(pl.multiple_of(piece * PIECE, 16), PIECE), :] = values
                    rest = squares_of(values[behind:])
                    rest = jnp.where(piece == BIAS // PIECE, jnp.zeros_like(rest), rest)
                    squares[piece] = squares_of(values[:behind]) + rest

    base = BIAS
    by_row = jnp.zeros((48, 256), F32)
    for jr in range(SIDE):
        rows = jnp.concatenate(
            [packed[base + b * PAD + 8 * jr : base + b * PAD + 8 * jr + 8, :].astype(F32) for b in range(6)], 0
        )
        by_row = by_row + nn(rows.astype(BF16), map_ref[jr])
    high = by_row.astype(BF16)
    rest = by_row - high.astype(F32)
    mid = rest.astype(BF16)
    low = (rest - mid.astype(F32)).astype(BF16)
    table = jnp.zeros((16, 256), F32)
    for jc in range(SIDE):
        for part in (high, mid, low):
            picked = jnp.concatenate(
                [
                    part[b * 8 + jc : b * 8 + jc + 1, head * 128 : (head + 1) * 128].astype(F32)
                    for b in range(6)
                    for head in range(2)
                ]
                + [jnp.zeros((4, 128), F32)],
                0,
            )
            table = table + nn(picked.astype(BF16), entry_ref[jc])
    norm_sq = jnp.sum(jnp.sum(squares[...], 0)) + jnp.sum(table * table)
    norm = jnp.sqrt(jnp.full((8, 128), norm_sq, F32))
    factor = jnp.minimum(1.0, math.sqrt(PARAMS) / (norm + 1e-06))[:1, :]
    g_table[...] = (table * factor[:, :1])[:HEADS, :TABLE]

    first = 0
    for n in range(4):
        stage, out, sem = stages[n], outs[n], out_sems.at[n]

        def scale_block(b, carry, first=first, n=n, stage=stage, out=out, sem=sem):
            rows = pl.ds(pl.multiple_of((first + b) * C, C), C)
            block = packed[rows, :].astype(F32) * factor
            strip = pl.ds(pl.multiple_of(b * 128, 128), 128)
            if n == 3:
                stage[strip, :] = block.T
                pltpu.make_async_copy(stage.at[strip, :], out.at[strip, :], sem).start()
            else:
                stage[:, strip] = block
                pltpu.make_async_copy(stage.at[:, strip], out.at[:, strip], sem).start()
            return carry

        count = stage.shape[0] // 128 if n == 3 else stage.shape[1] // 128
        lax.fori_loop(0, count, scale_block, 0)
        first += count
    for n in range(4):
        pltpu.make_async_copy(stages[n], outs[n], out_sems.at[n]).wait()


def run_last(place, pieces, row_map, entry_map):
    hbm = pl.BlockSpec(memory_space=pl.ANY)

    def whole(shape):
        return pl.BlockSpec(shape, lambda i, p: (0,) * len(shape))

    shapes = [(C, 3 * C), (C, C), (C, FFN), (FFN, C), (HEADS, TABLE)]
    return pl.pallas_call(
        last_body,
        grid_spec=pltpu.PrefetchScalarGridSpec(
            num_scalar_prefetch=1,
            grid=(1,),
            in_specs=[pl.BlockSpec(memory_space=pltpu.VMEM)] * (4 * PARTS + 2),
            out_specs=[hbm] * 4 + [whole(shapes[4])],
            scratch_shapes=[
                pltpu.VMEM((ROWS, 128), BF16),
                *[pltpu.VMEM(s, F32) for s in shapes[:4]],
                pltpu.VMEM((8 * PARTS, 8, 128), F32),
                pltpu.SemaphoreType.DMA((4,)),
            ],
        ),
        out_shape=[jax.ShapeDtypeStruct(s, F32) for s in shapes],
        compiler_params=pltpu.CompilerParams(vmem_limit_bytes=24 * 1024 * 1024),
        name="clip",
    )(place, *in_vmem([*pieces, row_map, entry_map]))


def sum_over_devices(keep, send, on_the_way):
    near, far = [], []
    for p in range(PARTS):
        with jax.named_scope(f"core_{p}"):
            got = swap(send[p], 3)
        held = keep[p][:PIECE].astype(F32) + got[:PIECE].astype(F32)
        other_quarter = keep[p][PIECE : 2 * PIECE].astype(F32) + got[PIECE : 2 * PIECE].astype(F32)
        other_half = add(keep[p][2 * PIECE :], got[2 * PIECE :])
        with jax.named_scope(f"halve_{p}"):
            got = swap(other_half, p, 0)
        with jax.named_scope(f"quarter_{p}"):
            back = swap(add(other_quarter, got[PIECE:]), p, 1)
        held = add(held, got[:PIECE], back)
        for stage in (1, 2):
            for turn in (0, 1):
                with jax.named_scope(f"double_{stage}{turn}_{p}"):
                    held = add(held, swap(held, (p + stage) % 3, turn))
            if p == 0 and stage == 1:
                held = on_the_way(held)
        with jax.named_scope(f"gather_{p}"):
            half = jnp.concatenate([held, swap(held, p, 1)], 0)
        near.append(half)
        with jax.named_scope(f"regather_{p}"):
            far.append(swap(half, p, 0))
    mine = [value for p in range(PARTS) for value in (near[p], far[p])]
    other = []
    for n, value in enumerate(mine):
        with jax.named_scope(f"recore_{n}"):
            other.append(swap(value, 3))
    return mine + other


def from_behind(x, steps):
    sizes = [lax.axis_size(axis) for axis in AXES]
    pairs = []
    for i in range(sizes[0]):
        for j in range(sizes[1]):
            to = ((i + steps[0]) % sizes[0]) * sizes[1] + (j + steps[1]) % sizes[1]
            pairs.append((i * sizes[1] + j, to))
    return lax.ppermute(x, AXES, pairs)


def send_rims(low, right, corner, by):
    return from_behind(low, (by, 0)), from_behind(right, (0, by)), from_behind(corner, (by, by))


def place_body(out_ref, tgrad_ref, low_ref, right_ref, corner_ref, *rest):
    new_out, new_tgrad = rest[2:4]
    inner = TILE - SHIFT
    col = lax.broadcasted_iota(jnp.int32, (inner, EDGE, C), 1)
    for n, (source, new) in enumerate(((out_ref, new_out), (tgrad_ref, new_tgrad))):
        new[:SHIFT] = low_ref[n]
        new[SHIFT:] = source[:inner]
        for rows, rim, old in (
            (slice(0, SHIFT), corner_ref[n], low_ref[n, :, :EDGE]),
            (slice(SHIFT, TILE), right_ref[n, :inner], source[:inner, :EDGE]),
        ):
            new[rows, :EDGE] = jnp.where(
                col[: rim.shape[0]] < SHIFT, rim.astype(F32), old.astype(F32)
            ).astype(BF16)


def place_rims(out, tgrad, rims, passing, ready):
    def whole(a):
        return pl.BlockSpec(a.shape, lambda i: (0,) * a.ndim)

    here = pl.BlockSpec(memory_space=pltpu.VMEM)
    tiles = (out, tgrad)
    return pl.pallas_call(
        place_body,
        grid=(1,),
        in_specs=[*[whole(a) for a in (*tiles, *rims)], here, pl.BlockSpec(memory_space=pl.ANY)],
        out_specs=[*[whole(a) for a in tiles], here],
        out_shape=[jax.ShapeDtypeStruct(a.shape, BF16) for a in tiles]
        + [pltpu.VMEM(passing.shape, passing.dtype)],
        input_output_aliases={5: 2},
        name="place",
    )(*tiles, *rims, *in_vmem([passing]), ready)


def window_tables(bias_table, rel_index):
    by_offset = rel_index.reshape(SIDE, SIDE, SIDE, SIDE)
    spread_out = jnp.pad(
        by_offset.transpose(2, 3, 0, 1), ((0, 1), (0, 1), (0, 1), (0, 1)), constant_values=-1
    ).reshape(PAD * PAD)
    lookup = (spread_out[None, :] == jnp.arange(TABLE, dtype=jnp.int32)[:, None]).astype(F32)
    bias = jnp.dot(bias_table.T, lookup, precision=lax.Precision.HIGHEST)
    bias = bias.reshape(HEADS, PAD, PAD).transpose(1, 0, 2).reshape(PAD, HEADS * PAD)
    entries = jnp.concatenate(
        [by_offset[0, :, :0:-1, :].transpose(1, 0, 2), by_offset[:, :, 0, :]], 0
    )
    entries = entries.transpose(2, 0, 1).reshape(SIDE, 13 * SIDE)
    entries = jnp.pad(entries, ((0, 0), (0, 128 - 13 * SIDE)), constant_values=-1)
    entry_map = (entries[:, :, None] == jnp.arange(256, dtype=jnp.int32)).astype(BF16)
    return bias, entry_map


def local(tokens, cotangent, w_qkv, w_proj, w_fc1, w_fc2, bias_table, rel_index, region):
    index = lax.axis_index("ha") * 16 + lax.axis_index("wa")
    place = jnp.stack(coordinates(index)).astype(jnp.int32)
    rims = send_rims(*cut_rims(tokens, cotangent), -1)
    bias, entry_map = window_tables(bias_table, rel_index)
    windows = region.reshape(4, SIDE, 4, SIDE).transpose(0, 2, 1, 3).astype(F32)
    windows = jnp.pad(windows, ((0, 0), (0, 0), (0, 1), (0, 1)), constant_values=-1.0)
    reg_lane = jnp.tile(windows.reshape(16, PAD), (1, 4)).reshape(16, 1, BAND)
    into, back = band_maps()
    out, tgrad, low, right, corner, *parts = run_main(
        place,
        (tokens, cotangent),
        rims,
        reg_lane,
        bias,
        jnp.asarray(into, BF16),
        jnp.asarray(back, BF16),
        (w_qkv, w_proj, w_fc1, w_fc2),
    )
    rims = send_rims(low, right, corner, 1)
    placed = []

    def on_the_way(piece):
        block_out, token_grad, piece = place_rims(out, tgrad, rims, piece, entry_map)
        placed.extend((block_out, token_grad))
        return piece

    pieces = sum_over_devices(parts[:PARTS], parts[PARTS:], on_the_way)
    *grads, table = run_last(place, pieces, jnp.asarray(table_map(), BF16), entry_map)
    return (*placed, *grads, table.T)


def solution(mesh):
    tiled = P("ha", "wa", None)
    return jax.shard_map(
        local,
        mesh=mesh,
        in_specs=(tiled, tiled, P(), P(), P(), P(), P(), P(), P("ha", "wa")),
        out_specs=(tiled, tiled, P(), P(), P(), P(), P()),
        check_vma=False,
    )
```

```python
import math

import jax
import jax.numpy as jnp
import numpy as np
from jax import lax
from jax.experimental import pallas as pl
from jax.experimental.pallas import tpu as pltpu
from jax.sharding import PartitionSpec as P

HEADS = 12
SIDE = 7
SHIFT = 3
HEAD_DIM = 32
WINDOW = 49
TABLE = 169
PARAMS = 1771500
C = 384
FFN = 1536
TILE = 28
PAD = 64
BAND = 4 * PAD
COLS = 48
RIM = 32
EDGE = 4
GROUPS = 3
CHUNK = 256
RUN = 64
BLOCKS = 36
BIAS = BLOCKS * C
PIECE = 1184
PARTS = 3
ROWS = 2 * PARTS * 2 * PIECE

EPSILON = 1e-05
SCALE = HEAD_DIM ** (-0.5)
AXES = ("ha", "wa")
F32 = jnp.float32
BF16 = jnp.bfloat16


def row_place(position):
    return (position // SIDE) * 8 + position % SIDE


def band_maps():
    into = np.zeros((BAND, SIDE * COLS), np.float32)
    back = np.zeros((SIDE * COLS, BAND), np.float32)
    for row in range(SIDE):
        for col in range(TILE):
            place = (col // SIDE) * PAD + row * 8 + col % SIDE
            at = col + SHIFT if col + SHIFT < TILE else RIM + col + SHIFT - TILE
            into[place, row * COLS + at] = 1.0
            back[row * COLS + at, place] = 1.0
    return into, back


def nn(a, b):
    return jnp.dot(a, b, preferred_element_type=F32)


def nt(a, b):
    return lax.dot_general(a, b, (((1,), (1,)), ((), ())), preferred_element_type=F32)


def tn(a, b):
    return lax.dot_general(a, b, (((0,), (0,)), ((), ())), preferred_element_type=F32)


def normalize(values):
    average = jnp.mean(values, -1, keepdims=True)
    centred = values - average
    inverse = lax.rsqrt(jnp.mean(centred * centred, -1, keepdims=True) + EPSILON)
    return centred * inverse, inverse


def normalize_back(normal_rows, inverse, upstream):
    up_mean = jnp.mean(upstream, -1, keepdims=True)
    cross_mean = jnp.mean(upstream * normal_rows, -1, keepdims=True)
    return inverse * (upstream - up_mean - normal_rows * cross_mean)


def gelu_parts(v):
    density = jnp.exp(v * v * -0.5) * (2.0 * math.pi) ** (-0.5)
    t = 1.0 / (1.0 + (0.3275911 * 2.0 ** (-0.5)) * jnp.abs(v))
    half = 0.5 * (2.0 * math.pi) ** 0.5
    poly = 1.061405429 * half
    for factor in (-1.453152027, 1.421413741, -0.284496736, 0.254829592):
        poly = poly * t + factor * half
    upper = poly * t * density
    return jnp.where(v >= 0, 1.0 - upper, upper), density


def spread(rows):
    tall = jnp.concatenate([rows] * 4, 0)
    head_row = lax.broadcasted_iota(jnp.int32, (BAND, 128), 0) // PAD
    head_lane = lax.broadcasted_iota(jnp.int32, (BAND, 128), 1) // HEAD_DIM
    return jnp.where(head_row == head_lane, tall, jnp.zeros_like(tall))


def gather_heads(tall):
    head_lane = lax.broadcasted_iota(jnp.int32, (PAD, 128), 1) // HEAD_DIM
    out = jnp.where(head_lane == 0, tall[:PAD], 0.0)
    for h in range(1, 4):
        out = out + jnp.where(head_lane == h, tall[h * PAD : (h + 1) * PAD], 0.0)
    return out


def main_body(
    place_ref,
    tokens_far,
    cot_far,
    low_ref,
    right_ref,
    corner_ref,
    reg_lane_ref,
    bias_ref,
    into_ref,
    back_ref,
    w_qkv_far,
    w_proj_far,
    w_fc1_far,
    w_fc2_far,
    out_ref,
    tgrad_ref,
    low_out,
    right_out,
    corner_out,
    keep_0,
    keep_1,
    keep_2,
    send_0,
    send_1,
    send_2,
    rows_s,
    tokens_ref,
    cot_ref,
    w_qkv_ref,
    w_proj_ref,
    w_fc1_ref,
    w_fc2_ref,
    qkv_s,
    probs_s,
    attn_s,
    gattn_s,
    dqkv_s,
    a_qkv,
    a_proj,
    a_fc1,
    a_fc2,
    a_bias,
    pre_s,
    up_s,
    act_s,
    gpre_s,
    ffn_s,
    second_s,
    wide_s,
    n1_s,
    n2_s,
    middle_s,
    inv1_s,
    inv2_s,
    x_s,
    cot_s,
    n1_low_s,
    n2_low_s,
    low_s,
    gproj_s,
    packed,
    sems,
):
    step = pl.program_id(0)

    def copy_in(n):
        far = (tokens_far, cot_far, w_qkv_far, w_proj_far, w_fc1_far, w_fc2_far)[n]
        near = (tokens_ref, cot_ref, w_qkv_ref, w_proj_ref, w_fc1_ref, w_fc2_ref)[n]
        return pltpu.make_async_copy(far, near, sems.at[n])

    @pl.when(step == 0)
    def _():
        for n in range(6):
            copy_in(n).start()
        for ref in (a_qkv, a_proj, a_fc1, a_fc2, a_bias):
            ref[...] = jnp.zeros_like(ref)
        rows_s[...] = jnp.zeros_like(rows_s)
        for n, ref in enumerate((tokens_ref, cot_ref)):
            copy_in(n).wait()
            rows_s[n, : TILE - SHIFT, :TILE, :] = ref[SHIFT:]
            rows_s[n, TILE - SHIFT :, :TILE, :] = low_ref[n]
            rows_s[n, : TILE - SHIFT, RIM : RIM + EDGE, :] = right_ref[n, SHIFT:]
            rows_s[n, TILE - SHIFT :, RIM : RIM + EDGE, :] = corner_ref[n]

    into = into_ref[...]
    back = back_ref[...]
    band = pl.ds(step * SIDE, SIDE)
    blocks = [slice(r, r + RUN) for r in range(0, BAND, RUN)]
    wide_s[...] = nn(into, rows_s[0, band].reshape(SIDE * COLS, C))
    cot_s[...] = nn(into, rows_s[1, band].reshape(SIDE * COLS, C)).astype(BF16)
    for rows in blocks:
        x = wide_s[rows]
        x_s[rows] = x.astype(BF16)
        normal, inverse = normalize(x)
        n1_s[rows] = normal
        inv1_s[rows] = jnp.broadcast_to(inverse, (RUN, 128))
        n1_low_s[rows] = normal.astype(BF16)

    def same_region(w):
        across = reg_lane_ref[w]
        down = jnp.broadcast_to(across[:, :128], (128, 128)).T[:PAD]
        return jnp.concatenate([down, down], 1) == across

    def put_back(n, ref, values):
        rows = nn(back, values).astype(BF16).reshape(SIDE, COLS, C)
        ref[...] = rows[:, :TILE]
        right_out[n] = rows[:, RIM : RIM + EDGE]

        @pl.when(step == pl.num_programs(0) - 1)
        def _():
            low_out[n] = rows[SIDE - SHIFT :, :TILE]
            corner_out[n] = rows[SIDE - SHIFT :, RIM : RIM + EDGE]

    @pl.when(step == 0)
    def _():
        copy_in(2).wait()

    qkv_s[...] = nn(n1_low_s[...], w_qkv_ref[...]).astype(BF16)

    def parts(rows, g):
        lanes = slice(g * 128, (g + 1) * 128)
        return [
            qkv_s[rows, pl.ds(k * C + g * 128, 128)] for k in range(3)
        ], lanes

    def forward_windows(pair, carry):
        chains = []
        for n in range(2):
            w = pair * 2 + n
            rows = pl.ds(pl.multiple_of(w * PAD, PAD), PAD)
            same = same_region(w)
            for g in range(GROUPS):
                (q, k, v), lanes = parts(rows, g)
                scores = nt(k, spread(q)) * SCALE + bias_ref[:, g * BAND : (g + 1) * BAND]
                chains.append((w, g, rows, lanes, v, jnp.where(same, scores, -1e30)))
        for w, g, rows, lanes, v, scores in chains:
            exponent = jnp.exp(scores - jnp.max(scores, 0, keepdims=True))
            probs = exponent * (1.0 / jnp.sum(exponent, 0, keepdims=True))
            probs_s[w, g] = probs
            attn_s[rows, lanes] = gather_heads(tn(probs.astype(BF16), v)).astype(BF16)
        return carry

    lax.fori_loop(0, 2, forward_windows, 0)

    @pl.when(step == 0)
    def _():
        for n in range(3, 6):
            copy_in(n).wait()

    wide_s[...] = nn(attn_s[...], w_proj_ref[...])
    for rows in blocks:
        middle = x_s[rows].astype(F32) + wide_s[rows].astype(BF16).astype(F32)
        middle_s[rows] = middle
        normal, inverse = normalize(middle)
        n2_s[rows] = normal
        inv2_s[rows] = jnp.broadcast_to(inverse, (RUN, 128))
        n2_low_s[rows] = normal.astype(BF16)
    n2_low = n2_low_s[...]
    cot_low = cot_s[...]
    n2_t = n2_low.T
    cot_t = cot_low.T

    def enter(f):
        hidden = slice(f, f + CHUNK)
        pre_s[:, hidden] = nn(n2_low, w_fc1_ref[:, hidden])
        up_s[:, hidden] = nt(cot_low, w_fc2_ref[hidden, :])

    def bend(f):
        hidden = slice(f, f + CHUNK)
        pre = pre_s[:, hidden]
        cdf, density = gelu_parts(pre)
        act_s[:, hidden] = (pre * cdf).astype(BF16)
        gpre_s[:, hidden] = (up_s[:, hidden] * (cdf + pre * density)).astype(BF16)

    def leave(f):
        hidden = slice(f, f + CHUNK)
        activated, grad_pre = act_s[:, hidden], gpre_s[:, hidden]
        a_fc2[:, hidden] += nn(cot_t, activated)
        a_fc1[:, hidden] += nn(n2_t, grad_pre)
        forward = nn(activated, w_fc2_ref[hidden, :])
        backward = nt(grad_pre, w_fc1_ref[:, hidden])
        ffn_s[...] = forward if f == 0 else ffn_s[...] + forward
        second_s[...] = backward if f == 0 else second_s[...] + backward

    enter(0)
    for f in range(0, FFN + CHUNK, CHUNK):
        if f + CHUNK < FFN:
            enter(f + CHUNK)
        if f < FFN:
            bend(f)
        if f > 0:
            leave(f - CHUNK)
    for rows in blocks:
        low_s[rows] = (middle_s[rows] + ffn_s[rows]).astype(BF16)
        grad_mid = cot_s[rows].astype(F32) + normalize_back(n2_s[rows], inv2_s[rows, :1], second_s[rows])
        middle_s[rows] = grad_mid
        gproj_s[rows] = grad_mid.astype(BF16)
    put_back(0, out_ref, low_s[...])
    a_proj[...] += nn(attn_s[...].T, gproj_s[...])
    gattn_s[...] = nt(gproj_s[...], w_proj_ref[...]).astype(BF16)

    def backward_windows(pair, carry):
        chains = []
        for n in range(2):
            w = pair * 2 + n
            rows = pl.ds(pl.multiple_of(w * PAD, PAD), PAD)
            for g in range(GROUPS):
                (q, k, v), lanes = parts(rows, g)
                grad_tall = spread(gattn_s[rows, lanes])
                grad_probs = nt(v, grad_tall)
                grad_v = nn(probs_s[w, g].astype(BF16), grad_tall)
                dqkv_s[rows, pl.ds(2 * C + g * 128, 128)] = grad_v.astype(BF16)
                chains.append((w, g, rows, q, k, grad_probs))
        for w, g, rows, q, k, grad_probs in chains:
            probs = probs_s[w, g]
            weighted = probs * grad_probs
            grad_scores = weighted - probs * jnp.sum(weighted, 0, keepdims=True)
            a_bias[:, g * BAND : (g + 1) * BAND] += grad_scores
            scaled = (grad_scores * SCALE).astype(BF16)
            grad_k = nn(scaled, spread(q))
            grad_q = gather_heads(tn(scaled, k))
            for n, value in enumerate((grad_q, grad_k)):
                dqkv_s[rows, pl.ds(n * C + g * 128, 128)] = value.astype(BF16)
        return carry

    lax.fori_loop(0, 2, backward_windows, 0)

    dqkv = dqkv_s[...]
    wide_s[...] = nt(dqkv, w_qkv_ref[...])
    a_qkv[...] += nn(n1_low_s[...].T, dqkv)
    for rows in blocks:
        grad_normed = wide_s[rows].astype(BF16).astype(F32)
        back_grad = normalize_back(n1_s[rows], inv1_s[rows, :1], grad_normed)
        low_s[rows] = (middle_s[rows] + back_grad).astype(BF16)
    put_back(1, tgrad_ref, low_s[...])

    @pl.when(step == pl.num_programs(0) - 1)
    def _():
        at = 0
        for ref in (a_qkv, a_proj, a_fc1, a_fc2):
            for b in range(ref.shape[1] // 128):
                packed[at : at + C, :] = ref[:, b * 128 : (b + 1) * 128].astype(BF16)
                at += C
        for b in range(6):
            packed[at : at + PAD, :] = a_bias[:, b * 128 : (b + 1) * 128].astype(BF16)
            at += PAD
        core = place_ref[3]
        copies = []
        for refs, owner in (((send_0, send_1, send_2), 1 - core), ((keep_0, keep_1, keep_2), core)):
            for p in range(PARTS):
                half = half_bit(place_ref[p], owner)
                for n, piece in enumerate((half, 1 - half)):
                    at = ((owner * PARTS + p) * 2 + piece) * PIECE
                    copies.append(
                        pltpu.make_async_copy(
                            packed.at[pl.ds(pl.multiple_of(at, 16), PIECE), :],
                            refs[p].at[pl.ds(n * PIECE, PIECE), :],
                            sems.at[len(copies)],
                        )
                    )
        for copy in copies:
            copy.start()
        for copy in copies:
            copy.wait()


def in_vmem(values):
    return [pltpu.with_memory_space_constraint(a, pltpu.VMEM) for a in values]


def run_main(place, tiles, rims, reg_lane, bias, into, back, weights):
    def resident(shape):
        return pl.BlockSpec(shape, lambda i, c: (0,) * len(shape))

    band = pl.BlockSpec((SIDE, TILE, C), lambda i, c: (i, 0, 0))
    here = pl.BlockSpec(memory_space=pltpu.VMEM)
    hbm = pl.BlockSpec(memory_space=pltpu.HBM)
    grid_spec = pltpu.PrefetchScalarGridSpec(
        num_scalar_prefetch=1,
        grid=(4,),
        in_specs=[
            *[hbm] * 2,
            *[here] * 3,
            pl.BlockSpec((4, 1, BAND), lambda i, c: (i, 0, 0)),
            *[here] * 3,
            *[hbm] * 4,
        ],
        out_specs=[
            band,
            band,
            resident(rims[0].shape),
            pl.BlockSpec((2, SIDE, EDGE, C), lambda i, c: (0, i, 0, 0)),
            resident(rims[2].shape),
            *[hbm] * PARTS,
            *[here] * PARTS,
        ],
        scratch_shapes=[
            pltpu.VMEM((2, TILE, COLS, C), BF16),
            *[pltpu.VMEM((TILE, TILE, C), BF16)] * 2,
            pltpu.VMEM((C, 3 * C), BF16),
            pltpu.VMEM((C, C), BF16),
            pltpu.VMEM((C, FFN), BF16),
            pltpu.VMEM((FFN, C), BF16),
            pltpu.VMEM((BAND, 3 * C), BF16),
            pltpu.VMEM((4, GROUPS, PAD, BAND), F32),
            pltpu.VMEM((BAND, C), BF16),
            pltpu.VMEM((BAND, C), BF16),
            pltpu.VMEM((BAND, 3 * C), BF16),
            pltpu.VMEM((C, 3 * C), F32),
            pltpu.VMEM((C, C), F32),
            pltpu.VMEM((C, FFN), F32),
            pltpu.VMEM((C, FFN), F32),
            pltpu.VMEM((PAD, HEADS * PAD), F32),
            pltpu.VMEM((BAND, FFN), F32),
            pltpu.VMEM((BAND, FFN), F32),
            pltpu.VMEM((BAND, FFN), BF16),
            pltpu.VMEM((BAND, FFN), BF16),
            *[pltpu.VMEM((BAND, C), F32)] * 6,
            *[pltpu.VMEM((BAND, 128), F32)] * 2,
            *[pltpu.VMEM((BAND, C), BF16)] * 6,
            pltpu.VMEM((ROWS, 128), BF16),
            pltpu.SemaphoreType.DMA((4 * PARTS,)),
        ],
    )
    third = (2 * PIECE, 128)
    rims = in_vmem(rims)
    bias, into, back = in_vmem((bias, into, back))
    return pl.pallas_call(
        main_body,
        grid_spec=grid_spec,
        out_shape=[jax.ShapeDtypeStruct(a.shape, BF16) for a in (*tiles, *rims)]
        + [jax.ShapeDtypeStruct(third, BF16)] * PARTS
        + [pltpu.VMEM(third, BF16)] * PARTS,
        compiler_params=pltpu.CompilerParams(
            dimension_semantics=("arbitrary",), vmem_limit_bytes=59 * 1024 * 1024
        ),
        name="block",
    )(place, *tiles, *rims, reg_lane, bias, into, back, *weights)


def rims_body(tokens_low, tokens_left, cot_low, cot_left, low_ref, right_ref, corner_ref):
    for n, (low, left) in enumerate(((tokens_low, tokens_left), (cot_low, cot_left))):
        low_ref[n] = low[...]
        right_ref[n] = left[:, :EDGE]
        corner_ref[n] = left[:SHIFT, :EDGE]


def cut_rims(tokens, cot):
    low = pl.BlockSpec((SHIFT, TILE, C), lambda i: (0, 0, 0))
    left = pl.BlockSpec((TILE, 16, C), lambda i: (0, 0, 0))
    shapes = [(2, SHIFT, TILE, C), (2, TILE, EDGE, C), (2, SHIFT, EDGE, C)]
    return pl.pallas_call(
        rims_body,
        grid=(1,),
        in_specs=[low, left, low, left],
        out_specs=[pl.BlockSpec(s, lambda i: (0, 0, 0, 0)) for s in shapes],
        out_shape=[jax.ShapeDtypeStruct(s, BF16) for s in shapes],
        name="rims",
    )(tokens, tokens, cot, cot)


def coordinates(index):
    ha, wa = index // 16, index % 16
    return (wa // 4, ha // 2, (wa // 2 % 2) * 2 + ha % 2, wa % 2)


def device_at(x, y, z, core):
    return (y * 2 + z % 2) * 16 + x * 4 + (z // 2) * 2 + core


def swap(value, axis, turn=0):
    pairs = []
    for index in range(128):
        place = list(coordinates(index))
        if axis == 3:
            place[3] = 1 - place[3]
        elif (turn + place[3]) % 2 == 0:
            place[axis] = place[axis] ^ 1
        else:
            place[axis] = 3 - place[axis]
        pairs.append((index, device_at(*place)))
    return lax.ppermute(value, AXES, pairs)


def half_bit(place, core):
    inner = lax.rem(lax.div(place + 1, 2), 2)
    upper = lax.div(place, 2)
    return inner + core * (upper - inner)


def add(*values):
    total = values[0].astype(F32)
    for value in values[1:]:
        total = total + value.astype(F32)
    return total.astype(BF16)


def table_map():
    out = np.zeros((SIDE, 128, 256), np.float32)
    for jr in range(SIDE):
        for head in range(2):
            for ir in range(SIDE):
                for ic in range(SIDE):
                    out[jr, head * PAD + 8 * ir + ic, head * 128 + (ir - jr + 6) * SIDE + ic] = 1.0
    return out


def last_body(place_ref, *refs):
    sources = refs[: 4 * PARTS]
    map_ref, entry_ref, *outs, g_table, packed = refs[4 * PARTS : 4 * PARTS + 8]
    stages = refs[4 * PARTS + 8 : 4 * PARTS + 12]
    squares, out_sems = refs[4 * PARTS + 12 :]
    core = place_ref[3]

    def squares_of(values):
        values = values.astype(F32)
        return jnp.sum((values * values).reshape(-1, 8, 128), 0)

    behind = BIAS % PIECE
    for n in range(2):
        owner = core if n == 0 else 1 - core
        for part in range(PARTS):
            half = half_bit(place_ref[part], owner)
            for far in range(2):
                piece = (owner * PARTS + part) * 2 + (half if far == 0 else 1 - half)
                values = sources[(n * PARTS + part) * 2 + far][...]
                packed[pl.ds(pl.multiple_of(piece * PIECE, 16), PIECE), :] = values
                rest = squares_of(values[behind:])
                rest = jnp.where(piece == BIAS // PIECE, jnp.zeros_like(rest), rest)
                squares[piece] = squares_of(values[:behind]) + rest

    base = BIAS
    by_row = jnp.zeros((48, 256), F32)
    for jr in range(SIDE):
        rows = jnp.concatenate(
            [packed[base + b * PAD + 8 * jr : base + b * PAD + 8 * jr + 8, :].astype(F32) for b in range(6)], 0
        )
        by_row = by_row + nn(rows.astype(BF16), map_ref[jr])
    high = by_row.astype(BF16)
    rest = by_row - high.astype(F32)
    mid = rest.astype(BF16)
    low = (rest - mid.astype(F32)).astype(BF16)
    table = jnp.zeros((16, 256), F32)
    for jc in range(SIDE):
        for part in (high, mid, low):
            picked = jnp.concatenate(
                [
                    part[b * 8 + jc : b * 8 + jc + 1, head * 128 : (head + 1) * 128].astype(F32)
                    for b in range(6)
                    for head in range(2)
                ]
                + [jnp.zeros((4, 128), F32)],
                0,
            )
            table = table + nn(picked.astype(BF16), entry_ref[jc])
    norm_sq = jnp.sum(jnp.sum(squares[...], 0)) + jnp.sum(table * table)
    norm = jnp.sqrt(jnp.full((8, 128), norm_sq, F32))
    factor = jnp.minimum(1.0, math.sqrt(PARAMS) / (norm + 1e-06))[:1, :]
    g_table[...] = (table * factor[:, :1])[:HEADS, :TABLE]

    first = 0
    for n in range(4):
        stage, out, sem = stages[n], outs[n], out_sems.at[n]

        def scale_block(b, carry, first=first, n=n, stage=stage, out=out, sem=sem):
            rows = pl.ds(pl.multiple_of((first + b) * C, C), C)
            block = packed[rows, :].astype(F32) * factor
            strip = pl.ds(pl.multiple_of(b * 128, 128), 128)
            if n == 3:
                stage[strip, :] = block.T
                pltpu.make_async_copy(stage.at[strip, :], out.at[strip, :], sem).start()
            else:
                stage[:, strip] = block
                pltpu.make_async_copy(stage.at[:, strip], out.at[:, strip], sem).start()
            return carry

        count = stage.shape[0] // 128 if n == 3 else stage.shape[1] // 128
        lax.fori_loop(0, count, scale_block, 0)
        first += count
    for n in range(4):
        pltpu.make_async_copy(stages[n], outs[n], out_sems.at[n]).wait()


def run_last(place, pieces, row_map, entry_map):
    hbm = pl.BlockSpec(memory_space=pl.ANY)

    def whole(shape):
        return pl.BlockSpec(shape, lambda i, p: (0,) * len(shape))

    shapes = [(C, 3 * C), (C, C), (C, FFN), (FFN, C), (HEADS, TABLE)]
    return pl.pallas_call(
        last_body,
        grid_spec=pltpu.PrefetchScalarGridSpec(
            num_scalar_prefetch=1,
            grid=(1,),
            in_specs=[pl.BlockSpec(memory_space=pltpu.VMEM)] * (4 * PARTS + 2),
            out_specs=[hbm] * 4 + [whole(shapes[4])],
            scratch_shapes=[
                pltpu.VMEM((ROWS, 128), BF16),
                *[pltpu.VMEM(s, F32) for s in shapes[:4]],
                pltpu.VMEM((4 * PARTS, 8, 128), F32),
                pltpu.SemaphoreType.DMA((4,)),
            ],
        ),
        out_shape=[jax.ShapeDtypeStruct(s, F32) for s in shapes],
        compiler_params=pltpu.CompilerParams(vmem_limit_bytes=24 * 1024 * 1024),
        name="clip",
    )(place, *in_vmem([*pieces, row_map, entry_map]))


def sum_over_devices(keep, send, on_the_way):
    near, far = [], []
    for p in range(PARTS):
        with jax.named_scope(f"core_{p}"):
            got = swap(send[p], 3)
        other_half = add(keep[p][PIECE:], got[PIECE:])
        held = keep[p][:PIECE].astype(F32) + got[:PIECE].astype(F32)
        with jax.named_scope(f"halve_{p}"):
            held = add(held, swap(other_half, p, 0))
        for n, (axis, turn) in enumerate(((p, 1), (p + 1, 0), (p + 1, 1), (p + 2, 0), (p + 2, 1))):
            with jax.named_scope(f"double_{n}_{p}"):
                held = add(held, swap(held, axis % 3, turn))
            if p == 0 and n == 1:
                held = on_the_way(held)
        near.append(held)
        with jax.named_scope(f"regather_{p}"):
            far.append(swap(held, p, 0))
    mine = [value for p in range(PARTS) for value in (near[p], far[p])]
    other = []
    for n, value in enumerate(mine):
        with jax.named_scope(f"recore_{n}"):
            other.append(swap(value, 3))
    return mine + other


def from_behind(x, steps):
    sizes = [lax.axis_size(axis) for axis in AXES]
    pairs = []
    for i in range(sizes[0]):
        for j in range(sizes[1]):
            to = ((i + steps[0]) % sizes[0]) * sizes[1] + (j + steps[1]) % sizes[1]
            pairs.append((i * sizes[1] + j, to))
    return lax.ppermute(x, AXES, pairs)


def send_rims(low, right, corner, by):
    return from_behind(low, (by, 0)), from_behind(right, (0, by)), from_behind(corner, (by, by))


def place_body(out_ref, tgrad_ref, low_ref, right_ref, corner_ref, *rest):
    new_out, new_tgrad = rest[2:4]
    inner = TILE - SHIFT
    col = lax.broadcasted_iota(jnp.int32, (inner, EDGE, C), 1)
    for n, (source, new) in enumerate(((out_ref, new_out), (tgrad_ref, new_tgrad))):
        new[:SHIFT] = low_ref[n]
        new[SHIFT:] = source[:inner]
        for rows, rim, old in (
            (slice(0, SHIFT), corner_ref[n], low_ref[n, :, :EDGE]),
            (slice(SHIFT, TILE), right_ref[n, :inner], source[:inner, :EDGE]),
        ):
            new[rows, :EDGE] = jnp.where(
                col[: rim.shape[0]] < SHIFT, rim.astype(F32), old.astype(F32)
            ).astype(BF16)


def place_rims(out, tgrad, rims, passing, ready):
    def whole(a):
        return pl.BlockSpec(a.shape, lambda i: (0,) * a.ndim)

    here = pl.BlockSpec(memory_space=pltpu.VMEM)
    tiles = (out, tgrad)
    return pl.pallas_call(
        place_body,
        grid=(1,),
        in_specs=[*[whole(a) for a in (*tiles, *rims)], here, pl.BlockSpec(memory_space=pl.ANY)],
        out_specs=[*[whole(a) for a in tiles], here],
        out_shape=[jax.ShapeDtypeStruct(a.shape, BF16) for a in tiles]
        + [pltpu.VMEM(passing.shape, passing.dtype)],
        input_output_aliases={5: 2},
        name="place",
    )(*tiles, *rims, *in_vmem([passing]), ready)


def window_tables(bias_table, rel_index):
    by_offset = rel_index.reshape(SIDE, SIDE, SIDE, SIDE)
    spread_out = jnp.pad(
        by_offset.transpose(2, 3, 0, 1), ((0, 1), (0, 1), (0, 1), (0, 1)), constant_values=-1
    ).reshape(PAD * PAD)
    lookup = (spread_out[None, :] == jnp.arange(TABLE, dtype=jnp.int32)[:, None]).astype(F32)
    bias = jnp.dot(bias_table.T, lookup, precision=lax.Precision.HIGHEST)
    bias = bias.reshape(HEADS, PAD, PAD).transpose(1, 0, 2).reshape(PAD, HEADS * PAD)
    entries = jnp.concatenate(
        [by_offset[0, :, :0:-1, :].transpose(1, 0, 2), by_offset[:, :, 0, :]], 0
    )
    entries = entries.transpose(2, 0, 1).reshape(SIDE, 13 * SIDE)
    entries = jnp.pad(entries, ((0, 0), (0, 128 - 13 * SIDE)), constant_values=-1)
    entry_map = (entries[:, :, None] == jnp.arange(256, dtype=jnp.int32)).astype(BF16)
    return bias, entry_map


def local(tokens, cotangent, w_qkv, w_proj, w_fc1, w_fc2, bias_table, rel_index, region):
    index = lax.axis_index("ha") * 16 + lax.axis_index("wa")
    place = jnp.stack(coordinates(index)).astype(jnp.int32)
    rims = send_rims(*cut_rims(tokens, cotangent), -1)
    bias, entry_map = window_tables(bias_table, rel_index)
    windows = region.reshape(4, SIDE, 4, SIDE).transpose(0, 2, 1, 3).astype(F32)
    windows = jnp.pad(windows, ((0, 0), (0, 0), (0, 1), (0, 1)), constant_values=-1.0)
    reg_lane = jnp.tile(windows.reshape(16, PAD), (1, 4)).reshape(16, 1, BAND)
    into, back = band_maps()
    out, tgrad, low, right, corner, *parts = run_main(
        place,
        (tokens, cotangent),
        rims,
        reg_lane,
        bias,
        jnp.asarray(into, BF16),
        jnp.asarray(back, BF16),
        (w_qkv, w_proj, w_fc1, w_fc2),
    )
    rims = send_rims(low, right, corner, 1)
    placed = []

    def on_the_way(piece):
        block_out, token_grad, piece = place_rims(out, tgrad, rims, piece, entry_map)
        placed.extend((block_out, token_grad))
        return piece

    pieces = sum_over_devices(parts[:PARTS], parts[PARTS:], on_the_way)
    *grads, table = run_last(place, pieces, jnp.asarray(table_map(), BF16), entry_map)
    return (*placed, *grads, table.T)


def solution(mesh):
    tiled = P("ha", "wa", None)
    return jax.shard_map(
        local,
        mesh=mesh,
        in_specs=(tiled, tiled, P(), P(), P(), P(), P(), P(), P("ha", "wa")),
        out_specs=(tiled, tiled, P(), P(), P(), P(), P()),
        check_vma=False,
    )
```

```python
import math

import jax
import jax.numpy as jnp
import numpy as np
from jax import lax
from jax.experimental import pallas as pl
from jax.experimental.pallas import tpu as pltpu
from jax.sharding import PartitionSpec as P

HEADS = 12
SIDE = 7
SHIFT = 3
HEAD_DIM = 32
WINDOW = 49
TABLE = 169
PARAMS = 1771500
C = 384
FFN = 1536
TILE = 28
PAD = 64
BAND = 4 * PAD
COLS = 48
RIM = 32
EDGE = 4
GROUPS = 3
CHUNK = 256
RUN = 64
BLOCKS = 36
BIAS = BLOCKS * C
PIECE = 592
PARTS = 3
ROWS = 2 * PARTS * 4 * PIECE

EPSILON = 1e-05
SCALE = HEAD_DIM ** (-0.5)
AXES = ("ha", "wa")
F32 = jnp.float32
BF16 = jnp.bfloat16


def row_place(position):
    return (position // SIDE) * 8 + position % SIDE


def band_maps():
    into = np.zeros((BAND, SIDE * COLS), np.float32)
    back = np.zeros((SIDE * COLS, BAND), np.float32)
    for row in range(SIDE):
        for col in range(TILE):
            place = (col // SIDE) * PAD + row * 8 + col % SIDE
            at = col + SHIFT if col + SHIFT < TILE else RIM + col + SHIFT - TILE
            into[place, row * COLS + at] = 1.0
            back[row * COLS + at, place] = 1.0
    return into, back


def nn(a, b):
    return jnp.dot(a, b, preferred_element_type=F32)


def nt(a, b):
    return lax.dot_general(a, b, (((1,), (1,)), ((), ())), preferred_element_type=F32)


def tn(a, b):
    return lax.dot_general(a, b, (((0,), (0,)), ((), ())), preferred_element_type=F32)


def normalize(values):
    average = jnp.mean(values, -1, keepdims=True)
    centred = values - average
    inverse = lax.rsqrt(jnp.mean(centred * centred, -1, keepdims=True) + EPSILON)
    return centred * inverse, inverse


def normalize_back(normal_rows, inverse, upstream):
    up_mean = jnp.mean(upstream, -1, keepdims=True)
    cross_mean = jnp.mean(upstream * normal_rows, -1, keepdims=True)
    return inverse * (upstream - up_mean - normal_rows * cross_mean)


def gelu_parts(v):
    density = jnp.exp(v * v * -0.5) * (2.0 * math.pi) ** (-0.5)
    t = 1.0 / (1.0 + (0.3275911 * 2.0 ** (-0.5)) * jnp.abs(v))
    half = 0.5 * (2.0 * math.pi) ** 0.5
    poly = 1.061405429 * half
    for factor in (-1.453152027, 1.421413741, -0.284496736, 0.254829592):
        poly = poly * t + factor * half
    upper = poly * t * density
    return jnp.where(v >= 0, 1.0 - upper, upper), density


def spread(rows):
    tall = jnp.concatenate([rows] * 4, 0)
    head_row = lax.broadcasted_iota(jnp.int32, (BAND, 128), 0) // PAD
    head_lane = lax.broadcasted_iota(jnp.int32, (BAND, 128), 1) // HEAD_DIM
    return jnp.where(head_row == head_lane, tall, jnp.zeros_like(tall))


def gather_heads(tall):
    head_lane = lax.broadcasted_iota(jnp.int32, (PAD, 128), 1) // HEAD_DIM
    out = jnp.where(head_lane == 0, tall[:PAD], 0.0)
    for h in range(1, 4):
        out = out + jnp.where(head_lane == h, tall[h * PAD : (h + 1) * PAD], 0.0)
    return out


def main_body(
    place_ref,
    tokens_far,
    cot_far,
    low_ref,
    right_ref,
    corner_ref,
    reg_lane_ref,
    bias_ref,
    into_ref,
    back_ref,
    w_qkv_far,
    w_proj_far,
    w_fc1_far,
    w_fc2_far,
    out_ref,
    tgrad_ref,
    low_out,
    right_out,
    corner_out,
    keep_0,
    keep_1,
    keep_2,
    send_0,
    send_1,
    send_2,
    rows_s,
    tokens_ref,
    cot_ref,
    w_qkv_ref,
    w_proj_ref,
    w_fc1_ref,
    w_fc2_ref,
    qkv_s,
    probs_s,
    attn_s,
    gattn_s,
    dqkv_s,
    a_qkv,
    a_proj,
    a_fc1,
    a_fc2,
    a_bias,
    pre_s,
    up_s,
    act_s,
    gpre_s,
    ffn_s,
    second_s,
    wide_s,
    n1_s,
    n2_s,
    middle_s,
    inv1_s,
    inv2_s,
    x_s,
    cot_s,
    n1_low_s,
    n2_low_s,
    low_s,
    gproj_s,
    packed,
    sems,
):
    step = pl.program_id(0)

    def copy_in(n):
        far = (tokens_far, cot_far, w_qkv_far, w_proj_far, w_fc1_far, w_fc2_far)[n]
        near = (tokens_ref, cot_ref, w_qkv_ref, w_proj_ref, w_fc1_ref, w_fc2_ref)[n]
        return pltpu.make_async_copy(far, near, sems.at[n])

    @pl.when(step == 0)
    def _():
        for n in range(6):
            copy_in(n).start()
        for ref in (a_qkv, a_proj, a_fc1, a_fc2, a_bias):
            ref[...] = jnp.zeros_like(ref)
        rows_s[...] = jnp.zeros_like(rows_s)
        for n, ref in enumerate((tokens_ref, cot_ref)):
            copy_in(n).wait()
            rows_s[n, : TILE - SHIFT, :TILE, :] = ref[SHIFT:]
            rows_s[n, TILE - SHIFT :, :TILE, :] = low_ref[n]
            rows_s[n, : TILE - SHIFT, RIM : RIM + EDGE, :] = right_ref[n, SHIFT:]
            rows_s[n, TILE - SHIFT :, RIM : RIM + EDGE, :] = corner_ref[n]

    into = into_ref[...]
    back = back_ref[...]
    band = pl.ds(step * SIDE, SIDE)
    blocks = [slice(r, r + RUN) for r in range(0, BAND, RUN)]
    wide_s[...] = nn(into, rows_s[0, band].reshape(SIDE * COLS, C))
    cot_s[...] = nn(into, rows_s[1, band].reshape(SIDE * COLS, C)).astype(BF16)
    for rows in blocks:
        x = wide_s[rows]
        x_s[rows] = x.astype(BF16)
        normal, inverse = normalize(x)
        n1_s[rows] = normal
        inv1_s[rows] = jnp.broadcast_to(inverse, (RUN, 128))
        n1_low_s[rows] = normal.astype(BF16)

    def same_region(w):
        across = reg_lane_ref[w]
        down = jnp.broadcast_to(across[:, :128], (128, 128)).T[:PAD]
        return jnp.concatenate([down, down], 1) == across

    def put_back(n, ref, values):
        rows = nn(back, values).astype(BF16).reshape(SIDE, COLS, C)
        ref[...] = rows[:, :TILE]
        right_out[n] = rows[:, RIM : RIM + EDGE]

        @pl.when(step == pl.num_programs(0) - 1)
        def _():
            low_out[n] = rows[SIDE - SHIFT :, :TILE]
            corner_out[n] = rows[SIDE - SHIFT :, RIM : RIM + EDGE]

    @pl.when(step == 0)
    def _():
        copy_in(2).wait()

    qkv_s[...] = nn(n1_low_s[...], w_qkv_ref[...]).astype(BF16)

    def parts(rows, g):
        lanes = slice(g * 128, (g + 1) * 128)
        return [
            qkv_s[rows, pl.ds(k * C + g * 128, 128)] for k in range(3)
        ], lanes

    def forward_windows(pair, carry):
        chains = []
        for n in range(2):
            w = pair * 2 + n
            rows = pl.ds(pl.multiple_of(w * PAD, PAD), PAD)
            same = same_region(w)
            for g in range(GROUPS):
                (q, k, v), lanes = parts(rows, g)
                scores = nt(k, spread(q)) * SCALE + bias_ref[:, g * BAND : (g + 1) * BAND]
                chains.append((w, g, rows, lanes, v, jnp.where(same, scores, -1e30)))
        for w, g, rows, lanes, v, scores in chains:
            exponent = jnp.exp(scores - jnp.max(scores, 0, keepdims=True))
            probs = exponent * (1.0 / jnp.sum(exponent, 0, keepdims=True))
            probs_s[w, g] = probs
            attn_s[rows, lanes] = gather_heads(tn(probs.astype(BF16), v)).astype(BF16)
        return carry

    lax.fori_loop(0, 2, forward_windows, 0)

    @pl.when(step == 0)
    def _():
        for n in range(3, 6):
            copy_in(n).wait()

    wide_s[...] = nn(attn_s[...], w_proj_ref[...])
    for rows in blocks:
        middle = x_s[rows].astype(F32) + wide_s[rows].astype(BF16).astype(F32)
        middle_s[rows] = middle
        normal, inverse = normalize(middle)
        n2_s[rows] = normal
        inv2_s[rows] = jnp.broadcast_to(inverse, (RUN, 128))
        n2_low_s[rows] = normal.astype(BF16)
    n2_low = n2_low_s[...]
    cot_low = cot_s[...]
    n2_t = n2_low.T
    cot_t = cot_low.T

    def enter(f):
        hidden = slice(f, f + CHUNK)
        pre_s[:, hidden] = nn(n2_low, w_fc1_ref[:, hidden])
        up_s[:, hidden] = nt(cot_low, w_fc2_ref[hidden, :])

    def bend(f):
        hidden = slice(f, f + CHUNK)
        pre = pre_s[:, hidden]
        cdf, density = gelu_parts(pre)
        act_s[:, hidden] = (pre * cdf).astype(BF16)
        gpre_s[:, hidden] = (up_s[:, hidden] * (cdf + pre * density)).astype(BF16)

    def leave(f):
        hidden = slice(f, f + CHUNK)
        activated, grad_pre = act_s[:, hidden], gpre_s[:, hidden]
        a_fc2[:, hidden] += nn(cot_t, activated)
        a_fc1[:, hidden] += nn(n2_t, grad_pre)
        forward = nn(activated, w_fc2_ref[hidden, :])
        backward = nt(grad_pre, w_fc1_ref[:, hidden])
        ffn_s[...] = forward if f == 0 else ffn_s[...] + forward
        second_s[...] = backward if f == 0 else second_s[...] + backward

    enter(0)
    for f in range(0, FFN + CHUNK, CHUNK):
        if f + CHUNK < FFN:
            enter(f + CHUNK)
        if f < FFN:
            bend(f)
        if f > 0:
            leave(f - CHUNK)
    for rows in blocks:
        low_s[rows] = (middle_s[rows] + ffn_s[rows]).astype(BF16)
        grad_mid = cot_s[rows].astype(F32) + normalize_back(n2_s[rows], inv2_s[rows, :1], second_s[rows])
        middle_s[rows] = grad_mid
        gproj_s[rows] = grad_mid.astype(BF16)
    put_back(0, out_ref, low_s[...])
    a_proj[...] += nn(attn_s[...].T, gproj_s[...])
    gattn_s[...] = nt(gproj_s[...], w_proj_ref[...]).astype(BF16)

    def backward_windows(pair, carry):
        chains = []
        for n in range(2):
            w = pair * 2 + n
            rows = pl.ds(pl.multiple_of(w * PAD, PAD), PAD)
            for g in range(GROUPS):
                (q, k, v), lanes = parts(rows, g)
                grad_tall = spread(gattn_s[rows, lanes])
                grad_probs = nt(v, grad_tall)
                grad_v = nn(probs_s[w, g].astype(BF16), grad_tall)
                dqkv_s[rows, pl.ds(2 * C + g * 128, 128)] = grad_v.astype(BF16)
                chains.append((w, g, rows, q, k, grad_probs))
        for w, g, rows, q, k, grad_probs in chains:
            probs = probs_s[w, g]
            weighted = probs * grad_probs
            grad_scores = weighted - probs * jnp.sum(weighted, 0, keepdims=True)
            a_bias[:, g * BAND : (g + 1) * BAND] += grad_scores
            scaled = (grad_scores * SCALE).astype(BF16)
            grad_k = nn(scaled, spread(q))
            grad_q = gather_heads(tn(scaled, k))
            for n, value in enumerate((grad_q, grad_k)):
                dqkv_s[rows, pl.ds(n * C + g * 128, 128)] = value.astype(BF16)
        return carry

    lax.fori_loop(0, 2, backward_windows, 0)

    dqkv = dqkv_s[...]
    wide_s[...] = nt(dqkv, w_qkv_ref[...])
    a_qkv[...] += nn(n1_low_s[...].T, dqkv)
    for rows in blocks:
        grad_normed = wide_s[rows].astype(BF16).astype(F32)
        back_grad = normalize_back(n1_s[rows], inv1_s[rows, :1], grad_normed)
        low_s[rows] = (middle_s[rows] + back_grad).astype(BF16)
    put_back(1, tgrad_ref, low_s[...])

    @pl.when(step == pl.num_programs(0) - 1)
    def _():
        at = 0
        for ref in (a_qkv, a_proj, a_fc1, a_fc2):
            for b in range(ref.shape[1] // 128):
                packed[at : at + C, :] = ref[:, b * 128 : (b + 1) * 128].astype(BF16)
                at += C
        for b in range(6):
            packed[at : at + PAD, :] = a_bias[:, b * 128 : (b + 1) * 128].astype(BF16)
            at += PAD
        core = place_ref[3]
        copies = []
        for refs, owner in (((send_0, send_1, send_2), 1 - core), ((keep_0, keep_1, keep_2), core)):
            for p in range(PARTS):
                half, quarter = quarter_bits(place_ref[p], owner)
                pieces = (
                    half * 2 + quarter,
                    half * 2 + 1 - quarter,
                    (1 - half) * 2 + quarter,
                    (1 - half) * 2 + 1 - quarter,
                )
                for n, piece in enumerate(pieces):
                    at = ((owner * PARTS + p) * 4 + piece) * PIECE
                    copies.append(
                        pltpu.make_async_copy(
                            packed.at[pl.ds(pl.multiple_of(at, 16), PIECE), :],
                            refs[p].at[pl.ds(n * PIECE, PIECE), :],
                            sems.at[len(copies)],
                        )
                    )
        for copy in copies:
            copy.start()
        for copy in copies:
            copy.wait()


def in_vmem(values):
    return [pltpu.with_memory_space_constraint(a, pltpu.VMEM) for a in values]


def run_main(place, tiles, rims, reg_lane, bias, into, back, weights):
    def resident(shape):
        return pl.BlockSpec(shape, lambda i, c: (0,) * len(shape))

    band = pl.BlockSpec((SIDE, TILE, C), lambda i, c: (i, 0, 0))
    here = pl.BlockSpec(memory_space=pltpu.VMEM)
    hbm = pl.BlockSpec(memory_space=pltpu.HBM)
    grid_spec = pltpu.PrefetchScalarGridSpec(
        num_scalar_prefetch=1,
        grid=(4,),
        in_specs=[
            *[hbm] * 2,
            *[here] * 3,
            pl.BlockSpec((4, 1, BAND), lambda i, c: (i, 0, 0)),
            *[here] * 3,
            *[hbm] * 4,
        ],
        out_specs=[
            band,
            band,
            resident(rims[0].shape),
            pl.BlockSpec((2, SIDE, EDGE, C), lambda i, c: (0, i, 0, 0)),
            resident(rims[2].shape),
            *[here] * PARTS,
            *[hbm] * PARTS,
        ],
        scratch_shapes=[
            pltpu.VMEM((2, TILE, COLS, C), BF16),
            *[pltpu.VMEM((TILE, TILE, C), BF16)] * 2,
            pltpu.VMEM((C, 3 * C), BF16),
            pltpu.VMEM((C, C), BF16),
            pltpu.VMEM((C, FFN), BF16),
            pltpu.VMEM((FFN, C), BF16),
            pltpu.VMEM((BAND, 3 * C), BF16),
            pltpu.VMEM((4, GROUPS, PAD, BAND), F32),
            pltpu.VMEM((BAND, C), BF16),
            pltpu.VMEM((BAND, C), BF16),
            pltpu.VMEM((BAND, 3 * C), BF16),
            pltpu.VMEM((C, 3 * C), F32),
            pltpu.VMEM((C, C), F32),
            pltpu.VMEM((C, FFN), F32),
            pltpu.VMEM((C, FFN), F32),
            pltpu.VMEM((PAD, HEADS * PAD), F32),
            pltpu.VMEM((BAND, FFN), F32),
            pltpu.VMEM((BAND, FFN), F32),
            pltpu.VMEM((BAND, FFN), BF16),
            pltpu.VMEM((BAND, FFN), BF16),
            *[pltpu.VMEM((BAND, C), F32)] * 6,
            *[pltpu.VMEM((BAND, 128), F32)] * 2,
            *[pltpu.VMEM((BAND, C), BF16)] * 6,
            pltpu.VMEM((ROWS, 128), BF16),
            pltpu.SemaphoreType.DMA((8 * PARTS,)),
        ],
    )
    third = (4 * PIECE, 128)
    rims = in_vmem(rims)
    bias, into, back = in_vmem((bias, into, back))
    return pl.pallas_call(
        main_body,
        grid_spec=grid_spec,
        out_shape=[jax.ShapeDtypeStruct(a.shape, BF16) for a in (*tiles, *rims)]
        + [pltpu.VMEM(third, BF16)] * PARTS
        + [jax.ShapeDtypeStruct(third, BF16)] * PARTS,
        compiler_params=pltpu.CompilerParams(
            dimension_semantics=("arbitrary",), vmem_limit_bytes=59 * 1024 * 1024
        ),
        name="block",
    )(place, *tiles, *rims, reg_lane, bias, into, back, *weights)


def rims_body(tokens_low, tokens_left, cot_low, cot_left, low_ref, right_ref, corner_ref):
    for n, (low, left) in enumerate(((tokens_low, tokens_left), (cot_low, cot_left))):
        low_ref[n] = low[...]
        right_ref[n] = left[:, :EDGE]
        corner_ref[n] = left[:SHIFT, :EDGE]


def cut_rims(tokens, cot):
    low = pl.BlockSpec((SHIFT, TILE, C), lambda i: (0, 0, 0))
    left = pl.BlockSpec((TILE, 16, C), lambda i: (0, 0, 0))
    shapes = [(2, SHIFT, TILE, C), (2, TILE, EDGE, C), (2, SHIFT, EDGE, C)]
    return pl.pallas_call(
        rims_body,
        grid=(1,),
        in_specs=[low, left, low, left],
        out_specs=[pl.BlockSpec(s, lambda i: (0, 0, 0, 0)) for s in shapes],
        out_shape=[jax.ShapeDtypeStruct(s, BF16) for s in shapes],
        name="rims",
    )(tokens, tokens, cot, cot)


def coordinates(index):
    ha, wa = index // 16, index % 16
    return (wa // 4, ha // 2, (wa // 2 % 2) * 2 + ha % 2, wa % 2)


def device_at(x, y, z, core):
    return (y * 2 + z % 2) * 16 + x * 4 + (z // 2) * 2 + core


def swap(value, axis, turn=0):
    pairs = []
    for index in range(128):
        place = list(coordinates(index))
        if axis == 3:
            place[3] = 1 - place[3]
        elif (turn + place[3]) % 2 == 0:
            place[axis] = place[axis] ^ 1
        else:
            place[axis] = 3 - place[axis]
        pairs.append((index, device_at(*place)))
    return lax.ppermute(value, AXES, pairs)


def quarter_bits(place, core):
    inner = lax.rem(lax.div(place + 1, 2), 2)
    upper = lax.div(place, 2)
    return inner + core * (upper - inner), upper + core * (inner - upper)


def add(*values):
    total = values[0].astype(F32)
    for value in values[1:]:
        total = total + value.astype(F32)
    return total.astype(BF16)


def table_map():
    out = np.zeros((SIDE, 128, 256), np.float32)
    for jr in range(SIDE):
        for head in range(2):
            for ir in range(SIDE):
                for ic in range(SIDE):
                    out[jr, head * PAD + 8 * ir + ic, head * 128 + (ir - jr + 6) * 8 + ic] = 1.0
    return out


def last_body(place_ref, *refs):
    sources = refs[: 4 * PARTS]
    map_ref, index_ref, *outs, g_table, packed = refs[4 * PARTS : 4 * PARTS + 8]
    stages = refs[4 * PARTS + 8 : 4 * PARTS + 12]
    squares, index_s, out_sems = refs[4 * PARTS + 12 :]
    core = place_ref[3]

    def squares_of(values):
        values = values.astype(F32)
        return jnp.sum((values * values).reshape(-1, 8, 128), 0)

    behind = BIAS % PIECE
    for n in range(2):
        owner = core if n == 0 else 1 - core
        for part in range(PARTS):
            half, quarter = quarter_bits(place_ref[part], owner)
            for far in range(2):
                for second in range(2):
                    h = half if far == 0 else 1 - half
                    q = quarter if second == 0 else 1 - quarter
                    piece = (owner * PARTS + part) * 4 + h * 2 + q
                    values = sources[(n * PARTS + part) * 2 + far][second * PIECE : (second + 1) * PIECE, :]
                    packed[pl.ds(pl.multiple_of(piece * PIECE, 16), PIECE), :] = values
                    rest = squares_of(values[behind:])
                    rest = jnp.where(piece == BIAS // PIECE, jnp.zeros_like(rest), rest)
                    squares[piece] = squares_of(values[:behind]) + rest

    base = BIAS
    by_row = jnp.zeros((48, 256), F32)
    for jr in range(SIDE):
        rows = jnp.concatenate(
            [packed[base + b * PAD + 8 * jr : base + b * PAD + 8 * jr + 8, :].astype(F32) for b in range(6)], 0
        )
        by_row = by_row + nn(rows.astype(BF16), map_ref[jr])
    high = by_row.astype(BF16)
    rest = by_row - high.astype(F32)
    mid = rest.astype(BF16)
    low = (rest - mid.astype(F32)).astype(BF16)
    table = jnp.zeros((16, 256), F32)
    index_s[...] = jnp.zeros_like(index_s)
    index_s[:WINDOW, :WINDOW] = index_ref[...]
    entry = lax.broadcasted_iota(jnp.int32, (8, 256), 1)
    for jc in range(SIDE):
        pairs = [(0, 7 * up + jc) for up in range(6, 0, -1)] + [(7 * down, jc) for down in range(7)]
        picks = jnp.concatenate(
            [(index_s[i : i + 8, j : j + 1] == entry).astype(F32) for i, j in pairs]
            + [jnp.zeros((24, 256), F32)],
            0,
        ).astype(BF16)
        for part in (high, mid, low):
            picked = jnp.concatenate(
                [
                    part[b * 8 + jc : b * 8 + jc + 1, head * 128 : (head + 1) * 128].astype(F32)
                    for b in range(6)
                    for head in range(2)
                ]
                + [jnp.zeros((4, 128), F32)],
                0,
            )
            table = table + nn(picked.astype(BF16), picks)
    norm_sq = jnp.sum(jnp.sum(squares[...], 0)) + jnp.sum(table * table)
    norm = jnp.sqrt(jnp.full((8, 128), norm_sq, F32))
    factor = jnp.minimum(1.0, math.sqrt(PARAMS) / (norm + 1e-06))[:1, :]
    g_table[...] = (table * factor[:, :1])[:HEADS, :TABLE]

    first = 0
    for n in range(4):
        stage, out, sem = stages[n], outs[n], out_sems.at[n]

        def scale_block(b, carry, first=first, n=n, stage=stage, out=out, sem=sem):
            rows = pl.ds(pl.multiple_of((first + b) * C, C), C)
            block = packed[rows, :].astype(F32) * factor
            strip = pl.ds(pl.multiple_of(b * 128, 128), 128)
            if n == 3:
                stage[strip, :] = block.T
                pltpu.make_async_copy(stage.at[strip, :], out.at[strip, :], sem).start()
            else:
                stage[:, strip] = block
                pltpu.make_async_copy(stage.at[:, strip], out.at[:, strip], sem).start()
            return carry

        count = stage.shape[0] // 128 if n == 3 else stage.shape[1] // 128
        lax.fori_loop(0, count, scale_block, 0)
        first += count
    for n in range(4):
        pltpu.make_async_copy(stages[n], outs[n], out_sems.at[n]).wait()


def run_last(place, pieces, row_map, rel_index):
    hbm = pl.BlockSpec(memory_space=pl.ANY)

    def whole(shape):
        return pl.BlockSpec(shape, lambda i, p: (0,) * len(shape))

    shapes = [(C, 3 * C), (C, C), (C, FFN), (FFN, C), (HEADS, TABLE)]
    return pl.pallas_call(
        last_body,
        grid_spec=pltpu.PrefetchScalarGridSpec(
            num_scalar_prefetch=1,
            grid=(1,),
            in_specs=[pl.BlockSpec(memory_space=pltpu.VMEM)] * (4 * PARTS + 2),
            out_specs=[hbm] * 4 + [whole(shapes[4])],
            scratch_shapes=[
                pltpu.VMEM((ROWS, 128), BF16),
                *[pltpu.VMEM(s, F32) for s in shapes[:4]],
                pltpu.VMEM((8 * PARTS, 8, 128), F32),
                pltpu.VMEM((PAD, 128), jnp.int32),
                pltpu.SemaphoreType.DMA((4,)),
            ],
        ),
        out_shape=[jax.ShapeDtypeStruct(s, F32) for s in shapes],
        compiler_params=pltpu.CompilerParams(vmem_limit_bytes=24 * 1024 * 1024),
        name="clip",
    )(place, *in_vmem([*pieces, row_map, rel_index]))


def sum_over_devices(keep, send, on_the_way):
    near, far = [], []
    for p in range(PARTS):
        with jax.named_scope(f"core_{p}"):
            got = swap(send[p], 3)
        held = keep[p][:PIECE].astype(F32) + got[:PIECE].astype(F32)
        other_quarter = keep[p][PIECE : 2 * PIECE].astype(F32) + got[PIECE : 2 * PIECE].astype(F32)
        other_half = add(keep[p][2 * PIECE :], got[2 * PIECE :])
        with jax.named_scope(f"halve_{p}"):
            got = swap(other_half, p, 0)
        with jax.named_scope(f"quarter_{p}"):
            back = swap(add(other_quarter, got[PIECE:]), p, 1)
        held = add(held, got[:PIECE], back)
        for stage in (1, 2):
            for turn in (0, 1):
                with jax.named_scope(f"double_{stage}{turn}_{p}"):
                    held = add(held, swap(held, (p + stage) % 3, turn))
            if p == 0 and stage == 1:
                held = on_the_way(held)
        with jax.named_scope(f"gather_{p}"):
            half = jnp.concatenate([held, swap(held, p, 1)], 0)
        near.append(half)
        with jax.named_scope(f"regather_{p}"):
            far.append(swap(half, p, 0))
    mine = [value for p in range(PARTS) for value in (near[p], far[p])]
    other = []
    for n, value in enumerate(mine):
        with jax.named_scope(f"recore_{n}"):
            other.append(swap(value, 3))
    return mine + other


def from_behind(x, steps):
    sizes = [lax.axis_size(axis) for axis in AXES]
    pairs = []
    for i in range(sizes[0]):
        for j in range(sizes[1]):
            to = ((i + steps[0]) % sizes[0]) * sizes[1] + (j + steps[1]) % sizes[1]
            pairs.append((i * sizes[1] + j, to))
    return lax.ppermute(x, AXES, pairs)


def send_rims(low, right, corner, by):
    return from_behind(low, (by, 0)), from_behind(right, (0, by)), from_behind(corner, (by, by))


def place_body(out_ref, tgrad_ref, low_ref, right_ref, corner_ref, *rest):
    new_out, new_tgrad = rest[1:3]
    inner = TILE - SHIFT
    col = lax.broadcasted_iota(jnp.int32, (inner, EDGE, C), 1)
    for n, (source, new) in enumerate(((out_ref, new_out), (tgrad_ref, new_tgrad))):
        new[:SHIFT] = low_ref[n]
        new[SHIFT:] = source[:inner]
        for rows, rim, old in (
            (slice(0, SHIFT), corner_ref[n], low_ref[n, :, :EDGE]),
            (slice(SHIFT, TILE), right_ref[n, :inner], source[:inner, :EDGE]),
        ):
            new[rows, :EDGE] = jnp.where(
                col[: rim.shape[0]] < SHIFT, rim.astype(F32), old.astype(F32)
            ).astype(BF16)


def place_rims(out, tgrad, rims, passing):
    def whole(a):
        return pl.BlockSpec(a.shape, lambda i: (0,) * a.ndim)

    here = pl.BlockSpec(memory_space=pltpu.VMEM)
    tiles = (out, tgrad)
    return pl.pallas_call(
        place_body,
        grid=(1,),
        in_specs=[*[whole(a) for a in (*tiles, *rims)], here],
        out_specs=[*[whole(a) for a in tiles], here],
        out_shape=[jax.ShapeDtypeStruct(a.shape, BF16) for a in tiles]
        + [pltpu.VMEM(passing.shape, passing.dtype)],
        input_output_aliases={5: 2},
        name="place",
    )(*tiles, *rims, *in_vmem([passing]))


def window_bias(bias_table, rel_index):
    by_offset = rel_index.reshape(SIDE, SIDE, SIDE, SIDE)
    spread_out = jnp.pad(
        by_offset.transpose(2, 3, 0, 1), ((0, 1), (0, 1), (0, 1), (0, 1)), constant_values=-1
    ).reshape(PAD * PAD)
    lookup = (spread_out[None, :] == jnp.arange(TABLE, dtype=jnp.int32)[:, None]).astype(F32)
    bias = jnp.dot(bias_table.T, lookup, precision=lax.Precision.HIGHEST)
    bias = bias.reshape(HEADS, PAD, PAD).transpose(1, 0, 2).reshape(PAD, HEADS * PAD)
    return bias


def local(tokens, cotangent, w_qkv, w_proj, w_fc1, w_fc2, bias_table, rel_index, region):
    index = lax.axis_index("ha") * 16 + lax.axis_index("wa")
    place = jnp.stack(coordinates(index)).astype(jnp.int32)
    rims = send_rims(*cut_rims(tokens, cotangent), -1)
    bias = window_bias(bias_table, rel_index)
    windows = region.reshape(4, SIDE, 4, SIDE).transpose(0, 2, 1, 3).astype(F32)
    windows = jnp.pad(windows, ((0, 0), (0, 0), (0, 1), (0, 1)), constant_values=-1.0)
    reg_lane = jnp.tile(windows.reshape(16, PAD), (1, 4)).reshape(16, 1, BAND)
    into, back = band_maps()
    out, tgrad, low, right, corner, *parts = run_main(
        place,
        (tokens, cotangent),
        rims,
        reg_lane,
        bias,
        jnp.asarray(into, BF16),
        jnp.asarray(back, BF16),
        (w_qkv, w_proj, w_fc1, w_fc2),
    )
    rims = send_rims(low, right, corner, 1)
    placed = []

    def on_the_way(piece):
        block_out, token_grad, piece = place_rims(out, tgrad, rims, piece)
        placed.extend((block_out, token_grad))
        return piece

    pieces = sum_over_devices(parts[:PARTS], parts[PARTS:], on_the_way)
    *grads, table = run_last(place, pieces, jnp.asarray(table_map(), BF16), rel_index)
    return (*placed, *grads, table.T)


def solution(mesh):
    tiled = P("ha", "wa", None)
    return jax.shard_map(
        local,
        mesh=mesh,
        in_specs=(tiled, tiled, P(), P(), P(), P(), P(), P(), P("ha", "wa")),
        out_specs=(tiled, tiled, P(), P(), P(), P(), P()),
        check_vma=False,
    )
```

```python
import math

import jax
import jax.numpy as jnp
import numpy as np
from jax import lax
from jax.experimental import pallas as pl
from jax.experimental.pallas import tpu as pltpu
from jax.sharding import PartitionSpec as P

HEADS = 12
SIDE = 7
SHIFT = 3
HEAD_DIM = 32
WINDOW = 49
TABLE = 169
PARAMS = 1771500
C = 384
FFN = 1536
TILE = 28
PAD = 64
BAND = 4 * PAD
COLS = 48
RIM = 32
EDGE = 4
GROUPS = 3
CHUNK = 256
RUN = 64
BLOCKS = 36
BIAS = BLOCKS * C
PIECE = 592
PARTS = 3
ROWS = 2 * PARTS * 4 * PIECE

EPSILON = 1e-05
SCALE = HEAD_DIM ** (-0.5)
AXES = ("ha", "wa")
F32 = jnp.float32
BF16 = jnp.bfloat16


def row_place(position):
    return (position // SIDE) * 8 + position % SIDE


def band_maps():
    into = np.zeros((BAND, SIDE * COLS), np.float32)
    back = np.zeros((SIDE * COLS, BAND), np.float32)
    for row in range(SIDE):
        for col in range(TILE):
            place = (col // SIDE) * PAD + row * 8 + col % SIDE
            at = col + SHIFT if col + SHIFT < TILE else RIM + col + SHIFT - TILE
            into[place, row * COLS + at] = 1.0
            back[row * COLS + at, place] = 1.0
    return into, back


def nn(a, b):
    return jnp.dot(a, b, preferred_element_type=F32)


def nt(a, b):
    return lax.dot_general(a, b, (((1,), (1,)), ((), ())), preferred_element_type=F32)


def tn(a, b):
    return lax.dot_general(a, b, (((0,), (0,)), ((), ())), preferred_element_type=F32)


def normalize(values):
    average = jnp.mean(values, -1, keepdims=True)
    centred = values - average
    inverse = lax.rsqrt(jnp.mean(centred * centred, -1, keepdims=True) + EPSILON)
    return centred * inverse, inverse


def normalize_back(normal_rows, inverse, upstream):
    up_mean = jnp.mean(upstream, -1, keepdims=True)
    cross_mean = jnp.mean(upstream * normal_rows, -1, keepdims=True)
    return inverse * (upstream - up_mean - normal_rows * cross_mean)


def gelu_parts(v):
    density = jnp.exp(v * v * -0.5) * (2.0 * math.pi) ** (-0.5)
    t = 1.0 / (1.0 + (0.3275911 * 2.0 ** (-0.5)) * jnp.abs(v))
    half = 0.5 * (2.0 * math.pi) ** 0.5
    poly = 1.061405429 * half
    for factor in (-1.453152027, 1.421413741, -0.284496736, 0.254829592):
        poly = poly * t + factor * half
    upper = poly * t * density
    return jnp.where(v >= 0, 1.0 - upper, upper), density


def spread(rows):
    tall = jnp.concatenate([rows] * 4, 0)
    head_row = lax.broadcasted_iota(jnp.int32, (BAND, 128), 0) // PAD
    head_lane = lax.broadcasted_iota(jnp.int32, (BAND, 128), 1) // HEAD_DIM
    return jnp.where(head_row == head_lane, tall, jnp.zeros_like(tall))


def gather_heads(tall):
    head_lane = lax.broadcasted_iota(jnp.int32, (PAD, 128), 1) // HEAD_DIM
    out = jnp.where(head_lane == 0, tall[:PAD], 0.0)
    for h in range(1, 4):
        out = out + jnp.where(head_lane == h, tall[h * PAD : (h + 1) * PAD], 0.0)
    return out


def main_body(
    tokens_far,
    cot_far,
    low_ref,
    right_ref,
    corner_ref,
    reg_lane_ref,
    bias_ref,
    into_ref,
    back_ref,
    w_qkv_far,
    w_proj_far,
    w_fc1_far,
    w_fc2_far,
    out_ref,
    tgrad_ref,
    low_out,
    right_out,
    corner_out,
    keep_0,
    keep_1,
    keep_2,
    send_0,
    send_1,
    send_2,
    rows_s,
    tokens_ref,
    cot_ref,
    w_qkv_ref,
    w_proj_ref,
    w_fc1_ref,
    w_fc2_ref,
    qkv_s,
    probs_s,
    attn_s,
    gattn_s,
    dqkv_s,
    a_qkv,
    a_proj,
    a_fc1,
    a_fc2,
    a_bias,
    pre_s,
    up_s,
    act_s,
    gpre_s,
    ffn_s,
    second_s,
    wide_s,
    n1_s,
    n2_s,
    middle_s,
    inv1_s,
    inv2_s,
    x_s,
    cot_s,
    n1_low_s,
    n2_low_s,
    low_s,
    gproj_s,
    packed,
    sems,
):
    step = pl.program_id(0)

    def copy_in(n):
        far = (tokens_far, cot_far, w_qkv_far, w_proj_far, w_fc1_far, w_fc2_far)[n]
        near = (tokens_ref, cot_ref, w_qkv_ref, w_proj_ref, w_fc1_ref, w_fc2_ref)[n]
        return pltpu.make_async_copy(far, near, sems.at[n])

    @pl.when(step == 0)
    def _():
        for n in range(6):
            copy_in(n).start()
        for ref in (a_qkv, a_proj, a_fc1, a_fc2, a_bias):
            ref[...] = jnp.zeros_like(ref)
        rows_s[...] = jnp.zeros_like(rows_s)
        for n, ref in enumerate((tokens_ref, cot_ref)):
            copy_in(n).wait()
            rows_s[n, : TILE - SHIFT, :TILE, :] = ref[SHIFT:]
            rows_s[n, TILE - SHIFT :, :TILE, :] = low_ref[n]
            rows_s[n, : TILE - SHIFT, RIM : RIM + EDGE, :] = right_ref[n, SHIFT:]
            rows_s[n, TILE - SHIFT :, RIM : RIM + EDGE, :] = corner_ref[n]

    into = into_ref[...]
    back = back_ref[...]
    band = pl.ds(step * SIDE, SIDE)
    blocks = [slice(r, r + RUN) for r in range(0, BAND, RUN)]
    wide_s[...] = nn(into, rows_s[0, band].reshape(SIDE * COLS, C))
    cot_s[...] = nn(into, rows_s[1, band].reshape(SIDE * COLS, C)).astype(BF16)
    for rows in blocks:
        x = wide_s[rows]
        x_s[rows] = x.astype(BF16)
        normal, inverse = normalize(x)
        n1_s[rows] = normal
        inv1_s[rows] = jnp.broadcast_to(inverse, (RUN, 128))
        n1_low_s[rows] = normal.astype(BF16)

    def same_region(w):
        across = reg_lane_ref[w]
        down = jnp.broadcast_to(across[:, :128], (128, 128)).T[:PAD]
        return jnp.concatenate([down, down], 1) == across

    def put_back(n, ref, values):
        rows = nn(back, values).astype(BF16).reshape(SIDE, COLS, C)
        ref[...] = rows[:, :TILE]
        right_out[n] = rows[:, RIM : RIM + EDGE]

        @pl.when(step == pl.num_programs(0) - 1)
        def _():
            low_out[n] = rows[SIDE - SHIFT :, :TILE]
            corner_out[n] = rows[SIDE - SHIFT :, RIM : RIM + EDGE]

    @pl.when(step == 0)
    def _():
        copy_in(2).wait()

    qkv_s[...] = nn(n1_low_s[...], w_qkv_ref[...]).astype(BF16)

    def parts(rows, g):
        lanes = slice(g * 128, (g + 1) * 128)
        return [
            qkv_s[rows, pl.ds(k * C + g * 128, 128)] for k in range(3)
        ], lanes

    def forward_windows(pair, carry):
        chains = []
        for n in range(2):
            w = pair * 2 + n
            rows = pl.ds(pl.multiple_of(w * PAD, PAD), PAD)
            same = same_region(w)
            for g in range(GROUPS):
                (q, k, v), lanes = parts(rows, g)
                scores = nt(k, spread(q)) * SCALE + bias_ref[:, g * BAND : (g + 1) * BAND]
                chains.append((w, g, rows, lanes, v, jnp.where(same, scores, -1e30)))
        for w, g, rows, lanes, v, scores in chains:
            exponent = jnp.exp(scores - jnp.max(scores, 0, keepdims=True))
            probs = exponent * (1.0 / jnp.sum(exponent, 0, keepdims=True))
            probs_s[w, g] = probs
            attn_s[rows, lanes] = gather_heads(tn(probs.astype(BF16), v)).astype(BF16)
        return carry

    lax.fori_loop(0, 2, forward_windows, 0)

    @pl.when(step == 0)
    def _():
        for n in range(3, 6):
            copy_in(n).wait()

    wide_s[...] = nn(attn_s[...], w_proj_ref[...])
    for rows in blocks:
        middle = x_s[rows].astype(F32) + wide_s[rows].astype(BF16).astype(F32)
        middle_s[rows] = middle
        normal, inverse = normalize(middle)
        n2_s[rows] = normal
        inv2_s[rows] = jnp.broadcast_to(inverse, (RUN, 128))
        n2_low_s[rows] = normal.astype(BF16)
    n2_low = n2_low_s[...]
    cot_low = cot_s[...]
    n2_t = n2_low.T
    cot_t = cot_low.T

    def enter(f):
        hidden = slice(f, f + CHUNK)
        pre_s[:, hidden] = nn(n2_low, w_fc1_ref[:, hidden])
        up_s[:, hidden] = nt(cot_low, w_fc2_ref[hidden, :])

    def bend(f):
        hidden = slice(f, f + CHUNK)
        pre = pre_s[:, hidden]
        cdf, density = gelu_parts(pre)
        act_s[:, hidden] = (pre * cdf).astype(BF16)
        gpre_s[:, hidden] = (up_s[:, hidden] * (cdf + pre * density)).astype(BF16)

    def leave(f):
        hidden = slice(f, f + CHUNK)
        activated, grad_pre = act_s[:, hidden], gpre_s[:, hidden]
        a_fc2[:, hidden] += nn(cot_t, activated)
        a_fc1[:, hidden] += nn(n2_t, grad_pre)
        forward = nn(activated, w_fc2_ref[hidden, :])
        backward = nt(grad_pre, w_fc1_ref[:, hidden])
        ffn_s[...] = forward if f == 0 else ffn_s[...] + forward
        second_s[...] = backward if f == 0 else second_s[...] + backward

    enter(0)
    for f in range(0, FFN + CHUNK, CHUNK):
        if f + CHUNK < FFN:
            enter(f + CHUNK)
        if f < FFN:
            bend(f)
        if f > 0:
            leave(f - CHUNK)
    for rows in blocks:
        low_s[rows] = (middle_s[rows] + ffn_s[rows]).astype(BF16)
        grad_mid = cot_s[rows].astype(F32) + normalize_back(n2_s[rows], inv2_s[rows, :1], second_s[rows])
        middle_s[rows] = grad_mid
        gproj_s[rows] = grad_mid.astype(BF16)
    put_back(0, out_ref, low_s[...])
    a_proj[...] += nn(attn_s[...].T, gproj_s[...])
    gattn_s[...] = nt(gproj_s[...], w_proj_ref[...]).astype(BF16)

    def backward_windows(pair, carry):
        chains = []
        for n in range(2):
            w = pair * 2 + n
            rows = pl.ds(pl.multiple_of(w * PAD, PAD), PAD)
            for g in range(GROUPS):
                (q, k, v), lanes = parts(rows, g)
                grad_tall = spread(gattn_s[rows, lanes])
                grad_probs = nt(v, grad_tall)
                grad_v = nn(probs_s[w, g].astype(BF16), grad_tall)
                dqkv_s[rows, pl.ds(2 * C + g * 128, 128)] = grad_v.astype(BF16)
                chains.append((w, g, rows, q, k, grad_probs))
        for w, g, rows, q, k, grad_probs in chains:
            probs = probs_s[w, g]
            weighted = probs * grad_probs
            grad_scores = weighted - probs * jnp.sum(weighted, 0, keepdims=True)
            a_bias[:, g * BAND : (g + 1) * BAND] += grad_scores
            scaled = (grad_scores * SCALE).astype(BF16)
            grad_k = nn(scaled, spread(q))
            grad_q = gather_heads(tn(scaled, k))
            for n, value in enumerate((grad_q, grad_k)):
                dqkv_s[rows, pl.ds(n * C + g * 128, 128)] = value.astype(BF16)
        return carry

    lax.fori_loop(0, 2, backward_windows, 0)

    dqkv = dqkv_s[...]
    wide_s[...] = nt(dqkv, w_qkv_ref[...])
    a_qkv[...] += nn(n1_low_s[...].T, dqkv)
    for rows in blocks:
        grad_normed = wide_s[rows].astype(BF16).astype(F32)
        back_grad = normalize_back(n1_s[rows], inv1_s[rows, :1], grad_normed)
        low_s[rows] = (middle_s[rows] + back_grad).astype(BF16)
    put_back(1, tgrad_ref, low_s[...])

    @pl.when(step == pl.num_programs(0) - 1)
    def _():
        at = 0
        for ref in (a_qkv, a_proj, a_fc1, a_fc2):
            for b in range(ref.shape[1] // 128):
                packed[at : at + C, :] = ref[:, b * 128 : (b + 1) * 128].astype(BF16)
                at += C
        for b in range(6):
            packed[at : at + PAD, :] = a_bias[:, b * 128 : (b + 1) * 128].astype(BF16)
            at += PAD
        place = own_place()
        core = place[3]
        for refs, owner in (((send_0, send_1, send_2), 1 - core), ((keep_0, keep_1, keep_2), core)):
            for p in range(PARTS):
                half, quarter = quarter_bits(place[p], owner)
                pieces = (
                    half * 2 + quarter,
                    half * 2 + 1 - quarter,
                    (1 - half) * 2 + quarter,
                    (1 - half) * 2 + 1 - quarter,
                )
                for n, piece in enumerate(pieces):
                    at = ((owner * PARTS + p) * 4 + piece) * PIECE
                    rows = pl.ds(pl.multiple_of(at, 16), PIECE)
                    refs[p][n * PIECE : (n + 1) * PIECE, :] = packed[rows, :]


def in_vmem(values):
    return [pltpu.with_memory_space_constraint(a, pltpu.VMEM) for a in values]


def run_main(tiles, rims, reg_lane, bias, into, back, weights):
    def resident(shape):
        return pl.BlockSpec(shape, lambda i: (0,) * len(shape))

    band = pl.BlockSpec((SIDE, TILE, C), lambda i: (i, 0, 0))
    here = pl.BlockSpec(memory_space=pltpu.VMEM)
    hbm = pl.BlockSpec(memory_space=pltpu.HBM)
    grid_spec = pl.GridSpec(
        grid=(4,),
        in_specs=[
            *[hbm] * 2,
            *[here] * 3,
            pl.BlockSpec((4, 1, BAND), lambda i: (i, 0, 0)),
            *[here] * 3,
            *[hbm] * 4,
        ],
        out_specs=[
            band,
            band,
            resident(rims[0].shape),
            pl.BlockSpec((2, SIDE, EDGE, C), lambda i: (0, i, 0, 0)),
            resident(rims[2].shape),
            *[here] * (2 * PARTS),
        ],
        scratch_shapes=[
            pltpu.VMEM((2, TILE, COLS, C), BF16),
            *[pltpu.VMEM((TILE, TILE, C), BF16)] * 2,
            pltpu.VMEM((C, 3 * C), BF16),
            pltpu.VMEM((C, C), BF16),
            pltpu.VMEM((C, FFN), BF16),
            pltpu.VMEM((FFN, C), BF16),
            pltpu.VMEM((BAND, 3 * C), BF16),
            pltpu.VMEM((4, GROUPS, PAD, BAND), F32),
            pltpu.VMEM((BAND, C), BF16),
            pltpu.VMEM((BAND, C), BF16),
            pltpu.VMEM((BAND, 3 * C), BF16),
            pltpu.VMEM((C, 3 * C), F32),
            pltpu.VMEM((C, C), F32),
            pltpu.VMEM((C, FFN), F32),
            pltpu.VMEM((C, FFN), F32),
            pltpu.VMEM((PAD, HEADS * PAD), F32),
            pltpu.VMEM((BAND, FFN), F32),
            pltpu.VMEM((BAND, FFN), F32),
            pltpu.VMEM((BAND, FFN), BF16),
            pltpu.VMEM((BAND, FFN), BF16),
            *[pltpu.VMEM((BAND, C), F32)] * 6,
            *[pltpu.VMEM((BAND, 128), F32)] * 2,
            *[pltpu.VMEM((BAND, C), BF16)] * 6,
            pltpu.VMEM((ROWS, 128), BF16),
            pltpu.SemaphoreType.DMA((6,)),
        ],
    )
    third = (4 * PIECE, 128)
    rims = in_vmem(rims)
    bias, into, back = in_vmem((bias, into, back))
    return pl.pallas_call(
        main_body,
        grid_spec=grid_spec,
        out_shape=[jax.ShapeDtypeStruct(a.shape, BF16) for a in (*tiles, *rims)]
        + [pltpu.VMEM(third, BF16)] * (2 * PARTS),
        compiler_params=pltpu.CompilerParams(
            dimension_semantics=("arbitrary",), vmem_limit_bytes=58 * 1024 * 1024
        ),
        name="block",
    )(*tiles, *rims, reg_lane, bias, into, back, *weights)


def rims_body(tokens_low, tokens_left, cot_low, cot_left, low_ref, right_ref, corner_ref):
    for n, (low, left) in enumerate(((tokens_low, tokens_left), (cot_low, cot_left))):
        low_ref[n] = low[...]
        right_ref[n] = left[:, :EDGE]
        corner_ref[n] = left[:SHIFT, :EDGE]


def cut_rims(tokens, cot):
    low = pl.BlockSpec((SHIFT, TILE, C), lambda i: (0, 0, 0))
    left = pl.BlockSpec((TILE, 16, C), lambda i: (0, 0, 0))
    shapes = [(2, SHIFT, TILE, C), (2, TILE, EDGE, C), (2, SHIFT, EDGE, C)]
    return pl.pallas_call(
        rims_body,
        grid=(1,),
        in_specs=[low, left, low, left],
        out_specs=[pl.BlockSpec(s, lambda i: (0, 0, 0, 0)) for s in shapes],
        out_shape=[jax.ShapeDtypeStruct(s, BF16) for s in shapes],
        name="rims",
    )(tokens, tokens, cot, cot)


def coordinates(index):
    ha, wa = index // 16, index % 16
    return (wa // 4, ha // 2, (wa // 2 % 2) * 2 + ha % 2, wa % 2)


def own_place():
    ha, wa = lax.axis_index("ha"), lax.axis_index("wa")
    y, z_low = lax.div(ha, 2), lax.rem(ha, 2)
    x, z_high = lax.div(wa, 4), lax.rem(lax.div(wa, 2), 2)
    return x, y, z_high * 2 + z_low, lax.rem(wa, 2)


def device_at(x, y, z, core):
    return (y * 2 + z % 2) * 16 + x * 4 + (z // 2) * 2 + core


def swap(value, axis, turn=0):
    pairs = []
    for index in range(128):
        place = list(coordinates(index))
        if axis == 3:
            place[3] = 1 - place[3]
        elif (turn + place[3]) % 2 == 0:
            place[axis] = place[axis] ^ 1
        else:
            place[axis] = 3 - place[axis]
        pairs.append((index, device_at(*place)))
    return lax.ppermute(value, AXES, pairs)


def quarter_bits(place, core):
    inner = lax.rem(lax.div(place + 1, 2), 2)
    upper = lax.div(place, 2)
    return inner + core * (upper - inner), upper + core * (inner - upper)


def add(*values):
    total = values[0].astype(F32)
    for value in values[1:]:
        total = total + value.astype(F32)
    return total.astype(BF16)


def table_map():
    out = np.zeros((SIDE, 128, 256), np.float32)
    for jr in range(SIDE):
        for head in range(2):
            for ir in range(SIDE):
                for ic in range(SIDE):
                    out[jr, head * PAD + 8 * ir + ic, head * 128 + (ir - jr + 6) * 8 + ic] = 1.0
    return out


def last_body(*refs):
    sources = refs[: 4 * PARTS]
    map_ref, index_ref, *outs, g_table, packed = refs[4 * PARTS : 4 * PARTS + 8]
    stages = refs[4 * PARTS + 8 : 4 * PARTS + 12]
    squares, index_s, out_sems = refs[4 * PARTS + 12 :]
    place = own_place()
    core = place[3]

    def squares_of(values):
        values = values.astype(F32)
        return jnp.sum((values * values).reshape(-1, 8, 128), 0)

    behind = BIAS % PIECE
    for n in range(2):
        owner = core if n == 0 else 1 - core
        for part in range(PARTS):
            half, quarter = quarter_bits(place[part], owner)
            for far in range(2):
                for second in range(2):
                    h = half if far == 0 else 1 - half
                    q = quarter if second == 0 else 1 - quarter
                    piece = (owner * PARTS + part) * 4 + h * 2 + q
                    values = sources[(n * PARTS + part) * 2 + far][second * PIECE : (second + 1) * PIECE, :]
                    packed[pl.ds(pl.multiple_of(piece * PIECE, 16), PIECE), :] = values
                    rest = squares_of(values[behind:])
                    rest = jnp.where(piece == BIAS // PIECE, jnp.zeros_like(rest), rest)
                    squares[piece] = squares_of(values[:behind]) + rest

    base = BIAS
    by_row = jnp.zeros((48, 256), F32)
    for jr in range(SIDE):
        rows = jnp.concatenate(
            [packed[base + b * PAD + 8 * jr : base + b * PAD + 8 * jr + 8, :].astype(F32) for b in range(6)], 0
        )
        by_row = by_row + nn(rows.astype(BF16), map_ref[jr])
    high = by_row.astype(BF16)
    rest = by_row - high.astype(F32)
    mid = rest.astype(BF16)
    low = (rest - mid.astype(F32)).astype(BF16)
    table = jnp.zeros((16, 256), F32)
    index_s[...] = jnp.zeros_like(index_s)
    index_s[:WINDOW, :WINDOW] = index_ref[...]
    entry = lax.broadcasted_iota(jnp.int32, (8, 256), 1)
    for jc in range(SIDE):
        pairs = [(0, 7 * up + jc) for up in range(6, 0, -1)] + [(7 * down, jc) for down in range(7)]
        picks = jnp.concatenate(
            [(index_s[i : i + 8, j : j + 1] == entry).astype(F32) for i, j in pairs]
            + [jnp.zeros((24, 256), F32)],
            0,
        ).astype(BF16)
        for part in (high, mid, low):
            picked = jnp.concatenate(
                [
                    part[b * 8 + jc : b * 8 + jc + 1, head * 128 : (head + 1) * 128].astype(F32)
                    for b in range(6)
                    for head in range(2)
                ]
                + [jnp.zeros((4, 128), F32)],
                0,
            )
            table = table + nn(picked.astype(BF16), picks)
    norm_sq = jnp.sum(jnp.sum(squares[...], 0)) + jnp.sum(table * table)
    norm = jnp.sqrt(jnp.full((8, 128), norm_sq, F32))
    factor = jnp.minimum(1.0, math.sqrt(PARAMS) / (norm + 1e-06))[:1, :]
    g_table[...] = (table * factor[:, :1])[:HEADS, :TABLE]

    first = 0
    for n in range(4):
        stage, out, sem = stages[n], outs[n], out_sems.at[n]

        def scale_block(b, carry, first=first, n=n, stage=stage, out=out, sem=sem):
            rows = pl.ds(pl.multiple_of((first + b) * C, C), C)
            block = packed[rows, :].astype(F32) * factor
            strip = pl.ds(pl.multiple_of(b * 128, 128), 128)
            if n == 3:
                stage[strip, :] = block.T
                pltpu.make_async_copy(stage.at[strip, :], out.at[strip, :], sem).start()
            else:
                stage[:, strip] = block
                pltpu.make_async_copy(stage.at[:, strip], out.at[:, strip], sem).start()
            return carry

        count = stage.shape[0] // 128 if n == 3 else stage.shape[1] // 128
        lax.fori_loop(0, count, scale_block, 0)
        first += count
    for n in range(4):
        pltpu.make_async_copy(stages[n], outs[n], out_sems.at[n]).wait()


def run_last(pieces, row_map, rel_index):
    hbm = pl.BlockSpec(memory_space=pl.ANY)

    def whole(shape):
        return pl.BlockSpec(shape, lambda i: (0,) * len(shape))

    shapes = [(C, 3 * C), (C, C), (C, FFN), (FFN, C), (HEADS, TABLE)]
    return pl.pallas_call(
        last_body,
        grid_spec=pl.GridSpec(
            grid=(1,),
            in_specs=[pl.BlockSpec(memory_space=pltpu.VMEM)] * (4 * PARTS + 2),
            out_specs=[hbm] * 4 + [whole(shapes[4])],
            scratch_shapes=[
                pltpu.VMEM((ROWS, 128), BF16),
                *[pltpu.VMEM(s, F32) for s in shapes[:4]],
                pltpu.VMEM((8 * PARTS, 8, 128), F32),
                pltpu.VMEM((PAD, 128), jnp.int32),
                pltpu.SemaphoreType.DMA((4,)),
            ],
        ),
        out_shape=[jax.ShapeDtypeStruct(s, F32) for s in shapes],
        compiler_params=pltpu.CompilerParams(vmem_limit_bytes=24 * 1024 * 1024),
        name="clip",
    )(*in_vmem([*pieces, row_map, rel_index]))


def sum_over_devices(keep, send, on_the_way):
    near, far = [], []
    for p in range(PARTS):
        with jax.named_scope(f"core_{p}"):
            got = swap(send[p], 3)
        held = keep[p][:PIECE].astype(F32) + got[:PIECE].astype(F32)
        other_quarter = keep[p][PIECE : 2 * PIECE].astype(F32) + got[PIECE : 2 * PIECE].astype(F32)
        other_half = add(keep[p][2 * PIECE :], got[2 * PIECE :])
        with jax.named_scope(f"halve_{p}"):
            got = swap(other_half, p, 0)
        with jax.named_scope(f"quarter_{p}"):
            back = swap(add(other_quarter, got[PIECE:]), p, 1)
        held = add(held, got[:PIECE], back)
        for stage in (1, 2):
            for turn in (0, 1):
                with jax.named_scope(f"double_{stage}{turn}_{p}"):
                    held = add(held, swap(held, (p + stage) % 3, turn))
            if p == 0 and stage == 1:
                held = on_the_way(held)
        with jax.named_scope(f"gather_{p}"):
            half = jnp.concatenate([held, swap(held, p, 1)], 0)
        near.append(half)
        with jax.named_scope(f"regather_{p}"):
            far.append(swap(half, p, 0))
    mine = [value for p in range(PARTS) for value in (near[p], far[p])]
    other = []
    for n, value in enumerate(mine):
        with jax.named_scope(f"recore_{n}"):
            other.append(swap(value, 3))
    return mine + other


def from_behind(x, steps):
    sizes = [lax.axis_size(axis) for axis in AXES]
    pairs = []
    for i in range(sizes[0]):
        for j in range(sizes[1]):
            to = ((i + steps[0]) % sizes[0]) * sizes[1] + (j + steps[1]) % sizes[1]
            pairs.append((i * sizes[1] + j, to))
    return lax.ppermute(x, AXES, pairs)


def send_rims(low, right, corner, by):
    return from_behind(low, (by, 0)), from_behind(right, (0, by)), from_behind(corner, (by, by))


def place_body(out_ref, tgrad_ref, low_ref, right_ref, corner_ref, *rest):
    new_out, new_tgrad = rest[1:3]
    inner = TILE - SHIFT
    col = lax.broadcasted_iota(jnp.int32, (inner, EDGE, C), 1)
    for n, (source, new) in enumerate(((out_ref, new_out), (tgrad_ref, new_tgrad))):
        new[:SHIFT] = low_ref[n]
        new[SHIFT:] = source[:inner]
        for rows, rim, old in (
            (slice(0, SHIFT), corner_ref[n], low_ref[n, :, :EDGE]),
            (slice(SHIFT, TILE), right_ref[n, :inner], source[:inner, :EDGE]),
        ):
            new[rows, :EDGE] = jnp.where(
                col[: rim.shape[0]] < SHIFT, rim.astype(F32), old.astype(F32)
            ).astype(BF16)


def place_rims(out, tgrad, rims, passing):
    def whole(a):
        return pl.BlockSpec(a.shape, lambda i: (0,) * a.ndim)

    here = pl.BlockSpec(memory_space=pltpu.VMEM)
    tiles = (out, tgrad)
    return pl.pallas_call(
        place_body,
        grid=(1,),
        in_specs=[*[whole(a) for a in (*tiles, *rims)], here],
        out_specs=[*[whole(a) for a in tiles], here],
        out_shape=[jax.ShapeDtypeStruct(a.shape, BF16) for a in tiles]
        + [pltpu.VMEM(passing.shape, passing.dtype)],
        input_output_aliases={5: 2},
        name="place",
    )(*tiles, *rims, *in_vmem([passing]))


def window_bias(bias_table, rel_index):
    by_offset = rel_index.reshape(SIDE, SIDE, SIDE, SIDE)
    spread_out = jnp.pad(
        by_offset.transpose(2, 3, 0, 1), ((0, 1), (0, 1), (0, 1), (0, 1)), constant_values=-1
    ).reshape(PAD * PAD)
    lookup = (spread_out[None, :] == jnp.arange(TABLE, dtype=jnp.int32)[:, None]).astype(F32)
    bias = jnp.dot(bias_table.T, lookup, precision=lax.Precision.HIGHEST)
    bias = bias.reshape(HEADS, PAD, PAD).transpose(1, 0, 2).reshape(PAD, HEADS * PAD)
    return bias


def local(tokens, cotangent, w_qkv, w_proj, w_fc1, w_fc2, bias_table, rel_index, region):
    rims = send_rims(*cut_rims(tokens, cotangent), -1)
    bias = window_bias(bias_table, rel_index)
    windows = region.reshape(4, SIDE, 4, SIDE).transpose(0, 2, 1, 3).astype(F32)
    windows = jnp.pad(windows, ((0, 0), (0, 0), (0, 1), (0, 1)), constant_values=-1.0)
    reg_lane = jnp.tile(windows.reshape(16, PAD), (1, 4)).reshape(16, 1, BAND)
    into, back = band_maps()
    out, tgrad, low, right, corner, *parts = run_main(
        (tokens, cotangent),
        rims,
        reg_lane,
        bias,
        jnp.asarray(into, BF16),
        jnp.asarray(back, BF16),
        (w_qkv, w_proj, w_fc1, w_fc2),
    )
    rims = send_rims(low, right, corner, 1)
    placed = []

    def on_the_way(piece):
        block_out, token_grad, piece = place_rims(out, tgrad, rims, piece)
        placed.extend((block_out, token_grad))
        return piece

    pieces = sum_over_devices(parts[:PARTS], parts[PARTS:], on_the_way)
    *grads, table = run_last(pieces, jnp.asarray(table_map(), BF16), rel_index)
    return (*placed, *grads, table.T)


def solution(mesh):
    tiled = P("ha", "wa", None)
    return jax.shard_map(
        local,
        mesh=mesh,
        in_specs=(tiled, tiled, P(), P(), P(), P(), P(), P(), P("ha", "wa")),
        out_specs=(tiled, tiled, P(), P(), P(), P(), P()),
        check_vma=False,
    )
```

```python
import math

import jax
import jax.numpy as jnp
import numpy as np
from jax import lax
from jax.experimental import pallas as pl
from jax.experimental.pallas import tpu as pltpu
from jax.sharding import PartitionSpec as P

HEADS = 12
SIDE = 7
SHIFT = 3
HEAD_DIM = 32
WINDOW = 49
TABLE = 169
PARAMS = 1771500
C = 384
FFN = 1536
TILE = 28
PAD = 64
BAND = 4 * PAD
COLS = 48
RIM = 32
EDGE = 4
GROUPS = 3
CHUNK = 256
RUN = 64
BLOCKS = 36
BIAS = BLOCKS * C
PIECE = 592
PARTS = 3
ROWS = 2 * PARTS * 4 * PIECE

EPSILON = 1e-05
SCALE = HEAD_DIM ** (-0.5)
AXES = ("ha", "wa")
F32 = jnp.float32
BF16 = jnp.bfloat16


def row_place(position):
    return (position // SIDE) * 8 + position % SIDE


def band_maps():
    into = np.zeros((BAND, SIDE * COLS), np.float32)
    back = np.zeros((SIDE * COLS, BAND), np.float32)
    for row in range(SIDE):
        for col in range(TILE):
            place = (col // SIDE) * PAD + row * 8 + col % SIDE
            at = col + SHIFT if col + SHIFT < TILE else RIM + col + SHIFT - TILE
            into[place, row * COLS + at] = 1.0
            back[row * COLS + at, place] = 1.0
    return into, back


def nn(a, b):
    return jnp.dot(a, b, preferred_element_type=F32)


def nt(a, b):
    return lax.dot_general(a, b, (((1,), (1,)), ((), ())), preferred_element_type=F32)


def tn(a, b):
    return lax.dot_general(a, b, (((0,), (0,)), ((), ())), preferred_element_type=F32)


def normalize(values):
    average = jnp.mean(values, -1, keepdims=True)
    centred = values - average
    inverse = lax.rsqrt(jnp.mean(centred * centred, -1, keepdims=True) + EPSILON)
    return centred * inverse, inverse


def normalize_back(normal_rows, inverse, upstream):
    up_mean = jnp.mean(upstream, -1, keepdims=True)
    cross_mean = jnp.mean(upstream * normal_rows, -1, keepdims=True)
    return inverse * (upstream - up_mean - normal_rows * cross_mean)


def gelu_parts(v):
    density = jnp.exp(v * v * -0.5) * (2.0 * math.pi) ** (-0.5)
    t = 1.0 / (1.0 + (0.3275911 * 2.0 ** (-0.5)) * jnp.abs(v))
    half = 0.5 * (2.0 * math.pi) ** 0.5
    poly = 1.061405429 * half
    for factor in (-1.453152027, 1.421413741, -0.284496736, 0.254829592):
        poly = poly * t + factor * half
    upper = poly * t * density
    return jnp.where(v >= 0, 1.0 - upper, upper), density


def spread(rows):
    tall = jnp.concatenate([rows] * 4, 0)
    head_row = lax.broadcasted_iota(jnp.int32, (BAND, 128), 0) // PAD
    head_lane = lax.broadcasted_iota(jnp.int32, (BAND, 128), 1) // HEAD_DIM
    return jnp.where(head_row == head_lane, tall, jnp.zeros_like(tall))


def gather_heads(tall):
    head_lane = lax.broadcasted_iota(jnp.int32, (PAD, 128), 1) // HEAD_DIM
    out = jnp.where(head_lane == 0, tall[:PAD], 0.0)
    for h in range(1, 4):
        out = out + jnp.where(head_lane == h, tall[h * PAD : (h + 1) * PAD], 0.0)
    return out


def main_body(
    tokens_far,
    cot_far,
    low_ref,
    right_ref,
    corner_ref,
    reg_lane_ref,
    bias_ref,
    into_ref,
    back_ref,
    w_qkv_far,
    w_proj_far,
    w_fc1_far,
    w_fc2_far,
    out_ref,
    tgrad_ref,
    low_out,
    right_out,
    corner_out,
    keep_0,
    keep_1,
    keep_2,
    send_0,
    send_1,
    send_2,
    rows_s,
    tokens_ref,
    cot_ref,
    w_qkv_ref,
    w_proj_ref,
    w_fc1_ref,
    w_fc2_ref,
    qkv_s,
    probs_s,
    attn_s,
    gattn_s,
    dqkv_s,
    a_qkv,
    a_proj,
    a_fc1,
    a_fc2,
    a_bias,
    pre_s,
    up_s,
    act_s,
    gpre_s,
    ffn_s,
    second_s,
    wide_s,
    n1_s,
    n2_s,
    middle_s,
    inv1_s,
    inv2_s,
    x_s,
    cot_s,
    n1_low_s,
    n2_low_s,
    low_s,
    gproj_s,
    packed,
    sems,
):
    step = pl.program_id(0)

    def copy_in(n):
        far = (tokens_far, cot_far, w_qkv_far, w_proj_far, w_fc1_far, w_fc2_far)[n]
        near = (tokens_ref, cot_ref, w_qkv_ref, w_proj_ref, w_fc1_ref, w_fc2_ref)[n]
        return pltpu.make_async_copy(far, near, sems.at[n])

    @pl.when(step == 0)
    def _():
        for n in range(6):
            copy_in(n).start()
        for ref in (a_qkv, a_proj, a_fc1, a_fc2, a_bias):
            ref[...] = jnp.zeros_like(ref)
        rows_s[...] = jnp.zeros_like(rows_s)
        for n, ref in enumerate((tokens_ref, cot_ref)):
            copy_in(n).wait()
            rows_s[n, : TILE - SHIFT, :TILE, :] = ref[SHIFT:]
            rows_s[n, TILE - SHIFT :, :TILE, :] = low_ref[n]
            rows_s[n, : TILE - SHIFT, RIM : RIM + EDGE, :] = right_ref[n, SHIFT:]
            rows_s[n, TILE - SHIFT :, RIM : RIM + EDGE, :] = corner_ref[n]

    into = into_ref[...]
    back = back_ref[...]
    band = pl.ds(step * SIDE, SIDE)
    blocks = [slice(r, r + RUN) for r in range(0, BAND, RUN)]
    wide_s[...] = nn(into, rows_s[0, band].reshape(SIDE * COLS, C))
    cot_s[...] = nn(into, rows_s[1, band].reshape(SIDE * COLS, C)).astype(BF16)
    for rows in blocks:
        x = wide_s[rows]
        x_s[rows] = x.astype(BF16)
        normal, inverse = normalize(x)
        n1_s[rows] = normal
        inv1_s[rows] = jnp.broadcast_to(inverse, (RUN, 128))
        n1_low_s[rows] = normal.astype(BF16)

    def same_region(w):
        across = reg_lane_ref[w]
        down = jnp.broadcast_to(across[:, :128], (128, 128)).T[:PAD]
        return jnp.concatenate([down, down], 1) == across

    def put_back(n, ref, values):
        rows = nn(back, values).astype(BF16).reshape(SIDE, COLS, C)
        ref[...] = rows[:, :TILE]
        right_out[n] = rows[:, RIM : RIM + EDGE]

        @pl.when(step == pl.num_programs(0) - 1)
        def _():
            low_out[n] = rows[SIDE - SHIFT :, :TILE]
            corner_out[n] = rows[SIDE - SHIFT :, RIM : RIM + EDGE]

    @pl.when(step == 0)
    def _():
        copy_in(2).wait()

    qkv_s[...] = nn(n1_low_s[...], w_qkv_ref[...]).astype(BF16)

    def parts(rows, g):
        lanes = slice(g * 128, (g + 1) * 128)
        return [
            qkv_s[rows, pl.ds(k * C + g * 128, 128)] for k in range(3)
        ], lanes

    def forward_windows(pair, carry):
        chains = []
        for n in range(2):
            w = pair * 2 + n
            rows = pl.ds(pl.multiple_of(w * PAD, PAD), PAD)
            same = same_region(w)
            for g in range(GROUPS):
                (q, k, v), lanes = parts(rows, g)
                scores = nt(k, spread(q)) * SCALE + bias_ref[:, g * BAND : (g + 1) * BAND]
                chains.append((w, g, rows, lanes, v, jnp.where(same, scores, -1e30)))
        for w, g, rows, lanes, v, scores in chains:
            exponent = jnp.exp(scores - jnp.max(scores, 0, keepdims=True))
            probs = exponent * (1.0 / jnp.sum(exponent, 0, keepdims=True))
            probs_s[w, g] = probs
            attn_s[rows, lanes] = gather_heads(tn(probs.astype(BF16), v)).astype(BF16)
        return carry

    lax.fori_loop(0, 2, forward_windows, 0)

    @pl.when(step == 0)
    def _():
        for n in range(3, 6):
            copy_in(n).wait()

    wide_s[...] = nn(attn_s[...], w_proj_ref[...])
    for rows in blocks:
        middle = x_s[rows].astype(F32) + wide_s[rows].astype(BF16).astype(F32)
        middle_s[rows] = middle
        normal, inverse = normalize(middle)
        n2_s[rows] = normal
        inv2_s[rows] = jnp.broadcast_to(inverse, (RUN, 128))
        n2_low_s[rows] = normal.astype(BF16)
    n2_low = n2_low_s[...]
    cot_low = cot_s[...]
    n2_t = n2_low.T
    cot_t = cot_low.T

    def enter(f):
        hidden = slice(f, f + CHUNK)
        pre_s[:, hidden] = nn(n2_low, w_fc1_ref[:, hidden])
        up_s[:, hidden] = nt(cot_low, w_fc2_ref[hidden, :])

    def bend(f):
        hidden = slice(f, f + CHUNK)
        pre = pre_s[:, hidden]
        cdf, density = gelu_parts(pre)
        act_s[:, hidden] = (pre * cdf).astype(BF16)
        gpre_s[:, hidden] = (up_s[:, hidden] * (cdf + pre * density)).astype(BF16)

    def leave(f):
        hidden = slice(f, f + CHUNK)
        activated, grad_pre = act_s[:, hidden], gpre_s[:, hidden]
        a_fc2[:, hidden] += nn(cot_t, activated)
        a_fc1[:, hidden] += nn(n2_t, grad_pre)
        forward = nn(activated, w_fc2_ref[hidden, :])
        backward = nt(grad_pre, w_fc1_ref[:, hidden])
        ffn_s[...] = forward if f == 0 else ffn_s[...] + forward
        second_s[...] = backward if f == 0 else second_s[...] + backward

    enter(0)
    for f in range(0, FFN + CHUNK, CHUNK):
        if f + CHUNK < FFN:
            enter(f + CHUNK)
        if f < FFN:
            bend(f)
        if f > 0:
            leave(f - CHUNK)
    for rows in blocks:
        low_s[rows] = (middle_s[rows] + ffn_s[rows]).astype(BF16)
        grad_mid = cot_s[rows].astype(F32) + normalize_back(n2_s[rows], inv2_s[rows, :1], second_s[rows])
        middle_s[rows] = grad_mid
        gproj_s[rows] = grad_mid.astype(BF16)
    put_back(0, out_ref, low_s[...])
    a_proj[...] += nn(attn_s[...].T, gproj_s[...])
    gattn_s[...] = nt(gproj_s[...], w_proj_ref[...]).astype(BF16)

    def backward_windows(pair, carry):
        chains = []
        for n in range(2):
            w = pair * 2 + n
            rows = pl.ds(pl.multiple_of(w * PAD, PAD), PAD)
            for g in range(GROUPS):
                (q, k, v), lanes = parts(rows, g)
                grad_tall = spread(gattn_s[rows, lanes])
                grad_probs = nt(v, grad_tall)
                grad_v = nn(probs_s[w, g].astype(BF16), grad_tall)
                dqkv_s[rows, pl.ds(2 * C + g * 128, 128)] = grad_v.astype(BF16)
                chains.append((w, g, rows, q, k, grad_probs))
        for w, g, rows, q, k, grad_probs in chains:
            probs = probs_s[w, g]
            weighted = probs * grad_probs
            grad_scores = weighted - probs * jnp.sum(weighted, 0, keepdims=True)
            a_bias[:, g * BAND : (g + 1) * BAND] += grad_scores
            scaled = (grad_scores * SCALE).astype(BF16)
            grad_k = nn(scaled, spread(q))
            grad_q = gather_heads(tn(scaled, k))
            for n, value in enumerate((grad_q, grad_k)):
                dqkv_s[rows, pl.ds(n * C + g * 128, 128)] = value.astype(BF16)
        return carry

    lax.fori_loop(0, 2, backward_windows, 0)

    dqkv = dqkv_s[...]
    wide_s[...] = nt(dqkv, w_qkv_ref[...])
    a_qkv[...] += nn(n1_low_s[...].T, dqkv)
    for rows in blocks:
        grad_normed = wide_s[rows].astype(BF16).astype(F32)
        back_grad = normalize_back(n1_s[rows], inv1_s[rows, :1], grad_normed)
        low_s[rows] = (middle_s[rows] + back_grad).astype(BF16)
    put_back(1, tgrad_ref, low_s[...])

    @pl.when(step == pl.num_programs(0) - 1)
    def _():
        at = 0
        for ref in (a_qkv, a_proj, a_fc1, a_fc2):
            for b in range(ref.shape[1] // 128):
                packed[at : at + C, :] = ref[:, b * 128 : (b + 1) * 128].astype(BF16)
                at += C
        for b in range(6):
            packed[at : at + PAD, :] = a_bias[:, b * 128 : (b + 1) * 128].astype(BF16)
            at += PAD
        place = own_place()
        core = place[3]
        for refs, owner in (((send_0, send_1, send_2), 1 - core), ((keep_0, keep_1, keep_2), core)):
            for p in range(PARTS):
                half, quarter = quarter_bits(place[p], owner)
                pieces = (
                    half * 2 + quarter,
                    half * 2 + 1 - quarter,
                    (1 - half) * 2 + quarter,
                    (1 - half) * 2 + 1 - quarter,
                )
                for n, piece in enumerate(pieces):
                    at = ((owner * PARTS + p) * 4 + piece) * PIECE
                    rows = pl.ds(pl.multiple_of(at, 16), PIECE)
                    refs[p][n * PIECE : (n + 1) * PIECE, :] = packed[rows, :]


def in_vmem(values):
    return [pltpu.with_memory_space_constraint(a, pltpu.VMEM) for a in values]


def run_main(tiles, rims, reg_lane, bias, into, back, weights):
    def resident(shape):
        return pl.BlockSpec(shape, lambda i: (0,) * len(shape))

    band = pl.BlockSpec((SIDE, TILE, C), lambda i: (i, 0, 0))
    here = pl.BlockSpec(memory_space=pltpu.VMEM)
    hbm = pl.BlockSpec(memory_space=pltpu.HBM)
    grid_spec = pl.GridSpec(
        grid=(4,),
        in_specs=[
            *[hbm] * 2,
            *[here] * 3,
            pl.BlockSpec((4, 1, BAND), lambda i: (i, 0, 0)),
            *[here] * 3,
            *[hbm] * 4,
        ],
        out_specs=[
            band,
            band,
            resident(rims[0].shape),
            pl.BlockSpec((2, SIDE, EDGE, C), lambda i: (0, i, 0, 0)),
            resident(rims[2].shape),
            *[here] * (2 * PARTS),
        ],
        scratch_shapes=[
            pltpu.VMEM((2, TILE, COLS, C), BF16),
            *[pltpu.VMEM((TILE, TILE, C), BF16)] * 2,
            pltpu.VMEM((C, 3 * C), BF16),
            pltpu.VMEM((C, C), BF16),
            pltpu.VMEM((C, FFN), BF16),
            pltpu.VMEM((FFN, C), BF16),
            pltpu.VMEM((BAND, 3 * C), BF16),
            pltpu.VMEM((4, GROUPS, PAD, BAND), F32),
            pltpu.VMEM((BAND, C), BF16),
            pltpu.VMEM((BAND, C), BF16),
            pltpu.VMEM((BAND, 3 * C), BF16),
            pltpu.VMEM((C, 3 * C), F32),
            pltpu.VMEM((C, C), F32),
            pltpu.VMEM((C, FFN), F32),
            pltpu.VMEM((C, FFN), F32),
            pltpu.VMEM((PAD, HEADS * PAD), F32),
            pltpu.VMEM((BAND, FFN), F32),
            pltpu.VMEM((BAND, FFN), F32),
            pltpu.VMEM((BAND, FFN), BF16),
            pltpu.VMEM((BAND, FFN), BF16),
            *[pltpu.VMEM((BAND, C), F32)] * 6,
            *[pltpu.VMEM((BAND, 128), F32)] * 2,
            *[pltpu.VMEM((BAND, C), BF16)] * 6,
            pltpu.VMEM((ROWS, 128), BF16),
            pltpu.SemaphoreType.DMA((6,)),
        ],
    )
    third = (4 * PIECE, 128)
    rims = in_vmem(rims)
    bias, into, back = in_vmem((bias, into, back))
    return pl.pallas_call(
        main_body,
        grid_spec=grid_spec,
        out_shape=[jax.ShapeDtypeStruct(a.shape, BF16) for a in (*tiles, *rims)]
        + [pltpu.VMEM(third, BF16)] * (2 * PARTS),
        compiler_params=pltpu.CompilerParams(
            dimension_semantics=("arbitrary",), vmem_limit_bytes=58 * 1024 * 1024
        ),
        name="block",
    )(*tiles, *rims, reg_lane, bias, into, back, *weights)


def rims_body(tokens_low, tokens_left, cot_low, cot_left, low_ref, right_ref, corner_ref):
    for n, (low, left) in enumerate(((tokens_low, tokens_left), (cot_low, cot_left))):
        low_ref[n] = low[...]
        right_ref[n] = left[:, :EDGE]
        corner_ref[n] = left[:SHIFT, :EDGE]


def cut_rims(tokens, cot):
    low = pl.BlockSpec((SHIFT, TILE, C), lambda i: (0, 0, 0))
    left = pl.BlockSpec((TILE, 16, C), lambda i: (0, 0, 0))
    shapes = [(2, SHIFT, TILE, C), (2, TILE, EDGE, C), (2, SHIFT, EDGE, C)]
    return pl.pallas_call(
        rims_body,
        grid=(1,),
        in_specs=[low, left, low, left],
        out_specs=[pl.BlockSpec(s, lambda i: (0, 0, 0, 0)) for s in shapes],
        out_shape=[jax.ShapeDtypeStruct(s, BF16) for s in shapes],
        name="rims",
    )(tokens, tokens, cot, cot)


def coordinates(index):
    ha, wa = index // 16, index % 16
    return (wa // 4, ha // 2, (wa // 2 % 2) * 2 + ha % 2, wa % 2)


def own_place():
    ha, wa = lax.axis_index("ha"), lax.axis_index("wa")
    y, z_low = lax.div(ha, 2), lax.rem(ha, 2)
    x, z_high = lax.div(wa, 4), lax.rem(lax.div(wa, 2), 2)
    return x, y, z_high * 2 + z_low, lax.rem(wa, 2)


def device_at(x, y, z, core):
    return (y * 2 + z % 2) * 16 + x * 4 + (z // 2) * 2 + core


def swap(value, axis, turn=0):
    pairs = []
    for index in range(128):
        place = list(coordinates(index))
        if axis == 3:
            place[3] = 1 - place[3]
        elif (turn + place[3]) % 2 == 0:
            place[axis] = place[axis] ^ 1
        else:
            place[axis] = 3 - place[axis]
        pairs.append((index, device_at(*place)))
    return lax.ppermute(value, AXES, pairs)


def quarter_bits(place, core):
    inner = lax.rem(lax.div(place + 1, 2), 2)
    upper = lax.div(place, 2)
    return inner + core * (upper - inner), upper + core * (inner - upper)


def add(*values):
    total = values[0].astype(F32)
    for value in values[1:]:
        total = total + value.astype(F32)
    return total.astype(BF16)


def table_map():
    out = np.zeros((SIDE, 128, 256), np.float32)
    for jr in range(SIDE):
        for head in range(2):
            for ir in range(SIDE):
                for ic in range(SIDE):
                    out[jr, head * PAD + 8 * ir + ic, head * 128 + (ir - jr + 6) * 8 + ic] = 1.0
    return out


def last_body(*refs):
    sources = refs[: 4 * PARTS]
    map_ref, index_ref, *outs, g_table, packed = refs[4 * PARTS : 4 * PARTS + 8]
    stages = refs[4 * PARTS + 8 : 4 * PARTS + 12]
    squares, index_s, out_sems = refs[4 * PARTS + 12 :]
    place = own_place()
    core = place[3]

    def squares_of(values):
        values = values.astype(F32)
        return jnp.sum((values * values).reshape(-1, 8, 128), 0)

    behind = BIAS % PIECE
    for n in range(2):
        owner = core if n == 0 else 1 - core
        for part in range(PARTS):
            half, quarter = quarter_bits(place[part], owner)
            for far in range(2):
                for second in range(2):
                    h = half if far == 0 else 1 - half
                    q = quarter if second == 0 else 1 - quarter
                    piece = (owner * PARTS + part) * 4 + h * 2 + q
                    values = sources[(n * PARTS + part) * 2 + far][second * PIECE : (second + 1) * PIECE, :]
                    packed[pl.ds(pl.multiple_of(piece * PIECE, 16), PIECE), :] = values
                    rest = squares_of(values[behind:])
                    rest = jnp.where(piece == BIAS // PIECE, jnp.zeros_like(rest), rest)
                    squares[piece] = squares_of(values[:behind]) + rest

    base = BIAS
    by_row = jnp.zeros((48, 256), F32)
    for jr in range(SIDE):
        rows = jnp.concatenate(
            [packed[base + b * PAD + 8 * jr : base + b * PAD + 8 * jr + 8, :].astype(F32) for b in range(6)], 0
        )
        by_row = by_row + nn(rows.astype(BF16), map_ref[jr])
    high = by_row.astype(BF16)
    rest = by_row - high.astype(F32)
    mid = rest.astype(BF16)
    low = (rest - mid.astype(F32)).astype(BF16)
    table = jnp.zeros((16, 256), F32)
    index_s[...] = jnp.zeros_like(index_s)
    index_s[:WINDOW, :WINDOW] = index_ref[...]
    entry = lax.broadcasted_iota(jnp.int32, (8, 256), 1)
    for jc in range(SIDE):
        pairs = [(0, 7 * up + jc) for up in range(6, 0, -1)] + [(7 * down, jc) for down in range(7)]
        picks = jnp.concatenate(
            [(index_s[i : i + 8, j : j + 1] == entry).astype(F32) for i, j in pairs]
            + [jnp.zeros((24, 256), F32)],
            0,
        ).astype(BF16)
        for part in (high, mid, low):
            picked = jnp.concatenate(
                [
                    part[b * 8 + jc : b * 8 + jc + 1, head * 128 : (head + 1) * 128].astype(F32)
                    for b in range(6)
                    for head in range(2)
                ]
                + [jnp.zeros((4, 128), F32)],
                0,
            )
            table = table + nn(picked.astype(BF16), picks)
    norm_sq = jnp.sum(jnp.sum(squares[...], 0)) + jnp.sum(table * table)
    norm = jnp.sqrt(jnp.full((8, 128), norm_sq, F32))
    factor = jnp.minimum(1.0, math.sqrt(PARAMS) / (norm + 1e-06))[:1, :]
    g_table[...] = (table * factor[:, :1])[:HEADS, :TABLE]

    first = 0
    for n in range(4):
        stage, out, sem = stages[n], outs[n], out_sems.at[n]

        def scale_block(b, carry, first=first, n=n, stage=stage, out=out, sem=sem):
            rows = pl.ds(pl.multiple_of((first + b) * C, C), C)
            block = packed[rows, :].astype(F32) * factor
            strip = pl.ds(pl.multiple_of(b * 128, 128), 128)
            if n == 3:
                stage[strip, :] = block.T
                pltpu.make_async_copy(stage.at[strip, :], out.at[strip, :], sem).start()
            else:
                stage[:, strip] = block
                pltpu.make_async_copy(stage.at[:, strip], out.at[:, strip], sem).start()
            return carry

        count = stage.shape[0] // 128 if n == 3 else stage.shape[1] // 128
        lax.fori_loop(0, count, scale_block, 0)
        first += count
    for n in range(4):
        pltpu.make_async_copy(stages[n], outs[n], out_sems.at[n]).wait()


def run_last(pieces, row_map, rel_index):
    hbm = pl.BlockSpec(memory_space=pl.ANY)

    def whole(shape):
        return pl.BlockSpec(shape, lambda i: (0,) * len(shape))

    shapes = [(C, 3 * C), (C, C), (C, FFN), (FFN, C), (HEADS, TABLE)]
    return pl.pallas_call(
        last_body,
        grid_spec=pl.GridSpec(
            grid=(1,),
            in_specs=[pl.BlockSpec(memory_space=pltpu.VMEM)] * (4 * PARTS + 2),
            out_specs=[hbm] * 4 + [whole(shapes[4])],
            scratch_shapes=[
                pltpu.VMEM((ROWS, 128), BF16),
                *[pltpu.VMEM(s, F32) for s in shapes[:4]],
                pltpu.VMEM((8 * PARTS, 8, 128), F32),
                pltpu.VMEM((PAD, 128), jnp.int32),
                pltpu.SemaphoreType.DMA((4,)),
            ],
        ),
        out_shape=[jax.ShapeDtypeStruct(s, F32) for s in shapes],
        compiler_params=pltpu.CompilerParams(vmem_limit_bytes=24 * 1024 * 1024),
        name="clip",
    )(*in_vmem([*pieces, row_map, rel_index]))


def sum_over_devices(keep, send, on_the_way):
    near, far = [], []
    for p in range(PARTS):
        with jax.named_scope(f"core_{p}"):
            got = swap(send[p], 3)
        held = keep[p][:PIECE].astype(F32) + got[:PIECE].astype(F32)
        other_quarter = keep[p][PIECE : 2 * PIECE].astype(F32) + got[PIECE : 2 * PIECE].astype(F32)
        other_half = add(keep[p][2 * PIECE :], got[2 * PIECE :])
        with jax.named_scope(f"halve_{p}"):
            got = swap(other_half, p, 0)
        with jax.named_scope(f"quarter_{p}"):
            back = swap(add(other_quarter, got[PIECE:]), p, 1)
        held = add(held, got[:PIECE], back)
        for stage in (1, 2):
            for turn in (0, 1):
                with jax.named_scope(f"double_{stage}{turn}_{p}"):
                    held = add(held, swap(held, (p + stage) % 3, turn))
        with jax.named_scope(f"gather_{p}"):
            half = jnp.concatenate([held, swap(held, p, 1)], 0)
        near.append(half)
        with jax.named_scope(f"regather_{p}"):
            far.append(swap(half, p, 0))
    near[0] = on_the_way(near[0])
    mine = [value for p in range(PARTS) for value in (near[p], far[p])]
    other = []
    for n, value in enumerate(mine):
        with jax.named_scope(f"recore_{n}"):
            other.append(swap(value, 3))
    return mine + other


def from_behind(x, steps):
    sizes = [lax.axis_size(axis) for axis in AXES]
    pairs = []
    for i in range(sizes[0]):
        for j in range(sizes[1]):
            to = ((i + steps[0]) % sizes[0]) * sizes[1] + (j + steps[1]) % sizes[1]
            pairs.append((i * sizes[1] + j, to))
    return lax.ppermute(x, AXES, pairs)


def send_rims(low, right, corner, by):
    return from_behind(low, (by, 0)), from_behind(right, (0, by)), from_behind(corner, (by, by))


def place_body(out_ref, tgrad_ref, low_ref, right_ref, corner_ref, *rest):
    new_out, new_tgrad = rest[1:3]
    inner = TILE - SHIFT
    col = lax.broadcasted_iota(jnp.int32, (inner, EDGE, C), 1)
    for n, (source, new) in enumerate(((out_ref, new_out), (tgrad_ref, new_tgrad))):
        new[:SHIFT] = low_ref[n]
        new[SHIFT:] = source[:inner]
        for rows, rim, old in (
            (slice(0, SHIFT), corner_ref[n], low_ref[n, :, :EDGE]),
            (slice(SHIFT, TILE), right_ref[n, :inner], source[:inner, :EDGE]),
        ):
            new[rows, :EDGE] = jnp.where(
                col[: rim.shape[0]] < SHIFT, rim.astype(F32), old.astype(F32)
            ).astype(BF16)


def place_rims(out, tgrad, rims, passing):
    def whole(a):
        return pl.BlockSpec(a.shape, lambda i: (0,) * a.ndim)

    here = pl.BlockSpec(memory_space=pltpu.VMEM)
    tiles = (out, tgrad)
    return pl.pallas_call(
        place_body,
        grid=(1,),
        in_specs=[*[whole(a) for a in (*tiles, *rims)], here],
        out_specs=[*[whole(a) for a in tiles], here],
        out_shape=[jax.ShapeDtypeStruct(a.shape, BF16) for a in tiles]
        + [pltpu.VMEM(passing.shape, passing.dtype)],
        input_output_aliases={5: 2},
        name="place",
    )(*tiles, *rims, *in_vmem([passing]))


def window_bias(bias_table, rel_index):
    by_offset = rel_index.reshape(SIDE, SIDE, SIDE, SIDE)
    spread_out = jnp.pad(
        by_offset.transpose(2, 3, 0, 1), ((0, 1), (0, 1), (0, 1), (0, 1)), constant_values=-1
    ).reshape(PAD * PAD)
    lookup = (spread_out[None, :] == jnp.arange(TABLE, dtype=jnp.int32)[:, None]).astype(F32)
    bias = jnp.dot(bias_table.T, lookup, precision=lax.Precision.HIGHEST)
    bias = bias.reshape(HEADS, PAD, PAD).transpose(1, 0, 2).reshape(PAD, HEADS * PAD)
    return bias


def local(tokens, cotangent, w_qkv, w_proj, w_fc1, w_fc2, bias_table, rel_index, region):
    rims = send_rims(*cut_rims(tokens, cotangent), -1)
    bias = window_bias(bias_table, rel_index)
    windows = region.reshape(4, SIDE, 4, SIDE).transpose(0, 2, 1, 3).astype(F32)
    windows = jnp.pad(windows, ((0, 0), (0, 0), (0, 1), (0, 1)), constant_values=-1.0)
    reg_lane = jnp.tile(windows.reshape(16, PAD), (1, 4)).reshape(16, 1, BAND)
    into, back = band_maps()
    out, tgrad, low, right, corner, *parts = run_main(
        (tokens, cotangent),
        rims,
        reg_lane,
        bias,
        jnp.asarray(into, BF16),
        jnp.asarray(back, BF16),
        (w_qkv, w_proj, w_fc1, w_fc2),
    )
    rims = send_rims(low, right, corner, 1)
    placed = []

    def on_the_way(piece):
        block_out, token_grad, piece = place_rims(out, tgrad, rims, piece)
        placed.extend((block_out, token_grad))
        return piece

    pieces = sum_over_devices(parts[:PARTS], parts[PARTS:], on_the_way)
    *grads, table = run_last(pieces, jnp.asarray(table_map(), BF16), rel_index)
    return (*placed, *grads, table.T)


def solution(mesh):
    tiled = P("ha", "wa", None)
    return jax.shard_map(
        local,
        mesh=mesh,
        in_specs=(tiled, tiled, P(), P(), P(), P(), P(), P(), P("ha", "wa")),
        out_specs=(tiled, tiled, P(), P(), P(), P(), P()),
        check_vma=False,
    )
```

```python
import math

import jax
import jax.numpy as jnp
import numpy as np
from jax import lax
from jax.experimental import pallas as pl
from jax.experimental.pallas import tpu as pltpu
from jax.sharding import PartitionSpec as P

HEADS = 12
SIDE = 7
SHIFT = 3
HEAD_DIM = 32
WINDOW = 49
TABLE = 169
PARAMS = 1771500
C = 384
FFN = 1536
TILE = 28
PAD = 64
BAND = 4 * PAD
COLS = 48
RIM = 32
EDGE = 4
GROUPS = 3
CHUNK = 256
RUN = 64
BLOCKS = 36
BIAS = BLOCKS * C
PIECE = 592
PARTS = 3
ROWS = 2 * PARTS * 4 * PIECE

EPSILON = 1e-05
SCALE = HEAD_DIM ** (-0.5)
AXES = ("ha", "wa")
F32 = jnp.float32
BF16 = jnp.bfloat16


def row_place(position):
    return (position // SIDE) * 8 + position % SIDE


def band_maps():
    into = np.zeros((BAND, SIDE * COLS), np.float32)
    back = np.zeros((SIDE * COLS, BAND), np.float32)
    for row in range(SIDE):
        for col in range(TILE):
            place = (col // SIDE) * PAD + row * 8 + col % SIDE
            at = col + SHIFT if col + SHIFT < TILE else RIM + col + SHIFT - TILE
            into[place, row * COLS + at] = 1.0
            back[row * COLS + at, place] = 1.0
    return into, back


def nn(a, b):
    return jnp.dot(a, b, preferred_element_type=F32)


def nt(a, b):
    return lax.dot_general(a, b, (((1,), (1,)), ((), ())), preferred_element_type=F32)


def tn(a, b):
    return lax.dot_general(a, b, (((0,), (0,)), ((), ())), preferred_element_type=F32)


def normalize(values):
    average = jnp.mean(values, -1, keepdims=True)
    centred = values - average
    inverse = lax.rsqrt(jnp.mean(centred * centred, -1, keepdims=True) + EPSILON)
    return centred * inverse, inverse


def normalize_back(normal_rows, inverse, upstream):
    up_mean = jnp.mean(upstream, -1, keepdims=True)
    cross_mean = jnp.mean(upstream * normal_rows, -1, keepdims=True)
    return inverse * (upstream - up_mean - normal_rows * cross_mean)


def gelu_parts(v):
    density = jnp.exp(v * v * -0.5) * (2.0 * math.pi) ** (-0.5)
    t = 1.0 / (1.0 + (0.3275911 * 2.0 ** (-0.5)) * jnp.abs(v))
    half = 0.5 * (2.0 * math.pi) ** 0.5
    poly = 1.061405429 * half
    for factor in (-1.453152027, 1.421413741, -0.284496736, 0.254829592):
        poly = poly * t + factor * half
    upper = poly * t * density
    return jnp.where(v >= 0, 1.0 - upper, upper), density


def spread(rows):
    tall = jnp.concatenate([rows] * 4, 0)
    head_row = lax.broadcasted_iota(jnp.int32, (BAND, 128), 0) // PAD
    head_lane = lax.broadcasted_iota(jnp.int32, (BAND, 128), 1) // HEAD_DIM
    return jnp.where(head_row == head_lane, tall, jnp.zeros_like(tall))


def gather_heads(tall):
    head_lane = lax.broadcasted_iota(jnp.int32, (PAD, 128), 1) // HEAD_DIM
    out = jnp.where(head_lane == 0, tall[:PAD], 0.0)
    for h in range(1, 4):
        out = out + jnp.where(head_lane == h, tall[h * PAD : (h + 1) * PAD], 0.0)
    return out


def main_body(
    tokens_far,
    cot_far,
    low_ref,
    right_ref,
    corner_ref,
    reg_lane_ref,
    bias_ref,
    into_ref,
    back_ref,
    w_qkv_far,
    w_proj_far,
    w_fc1_far,
    w_fc2_far,
    out_ref,
    tgrad_ref,
    low_out,
    right_out,
    corner_out,
    keep_0,
    keep_1,
    keep_2,
    send_0,
    send_1,
    send_2,
    rows_s,
    tokens_ref,
    cot_ref,
    w_qkv_ref,
    w_proj_ref,
    w_fc1_ref,
    w_fc2_ref,
    qkv_s,
    probs_s,
    attn_s,
    gattn_s,
    dqkv_s,
    a_qkv,
    a_proj,
    a_fc1,
    a_fc2,
    a_bias,
    pre_s,
    up_s,
    act_s,
    gpre_s,
    ffn_s,
    second_s,
    wide_s,
    n1_s,
    n2_s,
    middle_s,
    inv1_s,
    inv2_s,
    x_s,
    cot_s,
    n1_low_s,
    n2_low_s,
    low_s,
    gproj_s,
    packed,
    sems,
):
    step = pl.program_id(0)

    def copy_in(n):
        far = (tokens_far, cot_far, w_qkv_far, w_proj_far, w_fc1_far, w_fc2_far)[n]
        near = (tokens_ref, cot_ref, w_qkv_ref, w_proj_ref, w_fc1_ref, w_fc2_ref)[n]
        return pltpu.make_async_copy(far, near, sems.at[n])

    @pl.when(step == 0)
    def _():
        for n in range(6):
            copy_in(n).start()
        for ref in (a_qkv, a_proj, a_fc1, a_fc2, a_bias):
            ref[...] = jnp.zeros_like(ref)
        rows_s[...] = jnp.zeros_like(rows_s)
        for n, ref in enumerate((tokens_ref, cot_ref)):
            copy_in(n).wait()
            rows_s[n, : TILE - SHIFT, :TILE, :] = ref[SHIFT:]
            rows_s[n, TILE - SHIFT :, :TILE, :] = low_ref[n]
            rows_s[n, : TILE - SHIFT, RIM : RIM + EDGE, :] = right_ref[n, SHIFT:]
            rows_s[n, TILE - SHIFT :, RIM : RIM + EDGE, :] = corner_ref[n]

    into = into_ref[...]
    back = back_ref[...]
    band = pl.ds(step * SIDE, SIDE)
    blocks = [slice(r, r + RUN) for r in range(0, BAND, RUN)]
    wide_s[...] = nn(into, rows_s[0, band].reshape(SIDE * COLS, C))
    cot_s[...] = nn(into, rows_s[1, band].reshape(SIDE * COLS, C)).astype(BF16)
    for rows in blocks:
        x = wide_s[rows]
        x_s[rows] = x.astype(BF16)
        normal, inverse = normalize(x)
        n1_s[rows] = normal
        inv1_s[rows] = jnp.broadcast_to(inverse, (RUN, 128))
        n1_low_s[rows] = normal.astype(BF16)

    def same_region(w):
        across = reg_lane_ref[w]
        down = jnp.broadcast_to(across[:, :128], (128, 128)).T[:PAD]
        return jnp.concatenate([down, down], 1) == across

    def put_back(n, ref, values):
        rows = nn(back, values).astype(BF16).reshape(SIDE, COLS, C)
        ref[...] = rows[:, :TILE]
        right_out[n] = rows[:, RIM : RIM + EDGE]

        @pl.when(step == pl.num_programs(0) - 1)
        def _():
            low_out[n] = rows[SIDE - SHIFT :, :TILE]
            corner_out[n] = rows[SIDE - SHIFT :, RIM : RIM + EDGE]

    @pl.when(step == 0)
    def _():
        copy_in(2).wait()

    qkv_s[...] = nn(n1_low_s[...], w_qkv_ref[...]).astype(BF16)

    def parts(rows, g):
        lanes = slice(g * 128, (g + 1) * 128)
        return [
            qkv_s[rows, pl.ds(k * C + g * 128, 128)] for k in range(3)
        ], lanes

    def forward_windows(pair, carry):
        chains = []
        for n in range(2):
            w = pair * 2 + n
            rows = pl.ds(pl.multiple_of(w * PAD, PAD), PAD)
            same = same_region(w)
            for g in range(GROUPS):
                (q, k, v), lanes = parts(rows, g)
                scores = nt(k, spread(q)) * SCALE + bias_ref[:, g * BAND : (g + 1) * BAND]
                chains.append((w, g, rows, lanes, v, jnp.where(same, scores, -1e30)))
        for w, g, rows, lanes, v, scores in chains:
            exponent = jnp.exp(scores - jnp.max(scores, 0, keepdims=True))
            probs = exponent * (1.0 / jnp.sum(exponent, 0, keepdims=True))
            probs_s[w, g] = probs
            attn_s[rows, lanes] = gather_heads(tn(probs.astype(BF16), v)).astype(BF16)
        return carry

    lax.fori_loop(0, 2, forward_windows, 0)

    @pl.when(step == 0)
    def _():
        for n in range(3, 6):
            copy_in(n).wait()

    wide_s[...] = nn(attn_s[...], w_proj_ref[...])
    for rows in blocks:
        middle = x_s[rows].astype(F32) + wide_s[rows].astype(BF16).astype(F32)
        middle_s[rows] = middle
        normal, inverse = normalize(middle)
        n2_s[rows] = normal
        inv2_s[rows] = jnp.broadcast_to(inverse, (RUN, 128))
        n2_low_s[rows] = normal.astype(BF16)
    n2_low = n2_low_s[...]
    cot_low = cot_s[...]
    n2_t = n2_low.T
    cot_t = cot_low.T

    def enter(f):
        hidden = slice(f, f + CHUNK)
        pre_s[:, hidden] = nn(n2_low, w_fc1_ref[:, hidden])
        up_s[:, hidden] = nt(cot_low, w_fc2_ref[hidden, :])

    def bend(f):
        hidden = slice(f, f + CHUNK)
        pre = pre_s[:, hidden]
        cdf, density = gelu_parts(pre)
        act_s[:, hidden] = (pre * cdf).astype(BF16)
        gpre_s[:, hidden] = (up_s[:, hidden] * (cdf + pre * density)).astype(BF16)

    def leave(f):
        hidden = slice(f, f + CHUNK)
        activated, grad_pre = act_s[:, hidden], gpre_s[:, hidden]
        a_fc2[:, hidden] += nn(cot_t, activated)
        a_fc1[:, hidden] += nn(n2_t, grad_pre)
        forward = nn(activated, w_fc2_ref[hidden, :])
        backward = nt(grad_pre, w_fc1_ref[:, hidden])
        ffn_s[...] = forward if f == 0 else ffn_s[...] + forward
        second_s[...] = backward if f == 0 else second_s[...] + backward

    enter(0)
    for f in range(0, FFN + CHUNK, CHUNK):
        if f + CHUNK < FFN:
            enter(f + CHUNK)
        if f < FFN:
            bend(f)
        if f > 0:
            leave(f - CHUNK)
    for rows in blocks:
        low_s[rows] = (middle_s[rows] + ffn_s[rows]).astype(BF16)
        grad_mid = cot_s[rows].astype(F32) + normalize_back(n2_s[rows], inv2_s[rows, :1], second_s[rows])
        middle_s[rows] = grad_mid
        gproj_s[rows] = grad_mid.astype(BF16)
    put_back(0, out_ref, low_s[...])
    a_proj[...] += nn(attn_s[...].T, gproj_s[...])
    gattn_s[...] = nt(gproj_s[...], w_proj_ref[...]).astype(BF16)

    def backward_windows(pair, carry):
        chains = []
        for n in range(2):
            w = pair * 2 + n
            rows = pl.ds(pl.multiple_of(w * PAD, PAD), PAD)
            for g in range(GROUPS):
                (q, k, v), lanes = parts(rows, g)
                grad_tall = spread(gattn_s[rows, lanes])
                grad_probs = nt(v, grad_tall)
                grad_v = nn(probs_s[w, g].astype(BF16), grad_tall)
                dqkv_s[rows, pl.ds(2 * C + g * 128, 128)] = grad_v.astype(BF16)
                chains.append((w, g, rows, q, k, grad_probs))
        for w, g, rows, q, k, grad_probs in chains:
            probs = probs_s[w, g]
            weighted = probs * grad_probs
            grad_scores = weighted - probs * jnp.sum(weighted, 0, keepdims=True)
            a_bias[:, g * BAND : (g + 1) * BAND] += grad_scores
            scaled = (grad_scores * SCALE).astype(BF16)
            grad_k = nn(scaled, spread(q))
            grad_q = gather_heads(tn(scaled, k))
            for n, value in enumerate((grad_q, grad_k)):
                dqkv_s[rows, pl.ds(n * C + g * 128, 128)] = value.astype(BF16)
        return carry

    lax.fori_loop(0, 2, backward_windows, 0)

    dqkv = dqkv_s[...]
    wide_s[...] = nt(dqkv, w_qkv_ref[...])
    a_qkv[...] += nn(n1_low_s[...].T, dqkv)
    for rows in blocks:
        grad_normed = wide_s[rows].astype(BF16).astype(F32)
        back_grad = normalize_back(n1_s[rows], inv1_s[rows, :1], grad_normed)
        low_s[rows] = (middle_s[rows] + back_grad).astype(BF16)
    put_back(1, tgrad_ref, low_s[...])

    @pl.when(step == pl.num_programs(0) - 1)
    def _():
        at = 0
        for ref in (a_qkv, a_proj, a_fc1, a_fc2):
            for b in range(ref.shape[1] // 128):
                packed[at : at + C, :] = ref[:, b * 128 : (b + 1) * 128].astype(BF16)
                at += C
        for b in range(6):
            packed[at : at + PAD, :] = a_bias[:, b * 128 : (b + 1) * 128].astype(BF16)
            at += PAD
        place = own_place()
        core = place[3]
        for refs, owner in (((send_0, send_1, send_2), 1 - core), ((keep_0, keep_1, keep_2), core)):
            for p in range(PARTS):
                half, quarter = quarter_bits(place[p], owner)
                pieces = (
                    half * 2 + quarter,
                    half * 2 + 1 - quarter,
                    (1 - half) * 2 + quarter,
                    (1 - half) * 2 + 1 - quarter,
                )
                for n, piece in enumerate(pieces):
                    at = ((owner * PARTS + p) * 4 + piece) * PIECE
                    rows = pl.ds(pl.multiple_of(at, 16), PIECE)
                    refs[p][n * PIECE : (n + 1) * PIECE, :] = packed[rows, :]


def in_vmem(values):
    return [pltpu.with_memory_space_constraint(a, pltpu.VMEM) for a in values]


def run_main(tiles, rims, reg_lane, bias, into, back, weights):
    def resident(shape):
        return pl.BlockSpec(shape, lambda i: (0,) * len(shape))

    band = pl.BlockSpec((SIDE, TILE, C), lambda i: (i, 0, 0))
    here = pl.BlockSpec(memory_space=pltpu.VMEM)
    hbm = pl.BlockSpec(memory_space=pltpu.HBM)
    grid_spec = pl.GridSpec(
        grid=(4,),
        in_specs=[
            *[hbm] * 2,
            *[here] * 3,
            pl.BlockSpec((4, 1, BAND), lambda i: (i, 0, 0)),
            *[here] * 3,
            *[hbm] * 4,
        ],
        out_specs=[
            band,
            band,
            resident(rims[0].shape),
            pl.BlockSpec((2, SIDE, EDGE, C), lambda i: (0, i, 0, 0)),
            resident(rims[2].shape),
            *[here] * (2 * PARTS),
        ],
        scratch_shapes=[
            pltpu.VMEM((2, TILE, COLS, C), BF16),
            *[pltpu.VMEM((TILE, TILE, C), BF16)] * 2,
            pltpu.VMEM((C, 3 * C), BF16),
            pltpu.VMEM((C, C), BF16),
            pltpu.VMEM((C, FFN), BF16),
            pltpu.VMEM((FFN, C), BF16),
            pltpu.VMEM((BAND, 3 * C), BF16),
            pltpu.VMEM((4, GROUPS, PAD, BAND), F32),
            pltpu.VMEM((BAND, C), BF16),
            pltpu.VMEM((BAND, C), BF16),
            pltpu.VMEM((BAND, 3 * C), BF16),
            pltpu.VMEM((C, 3 * C), F32),
            pltpu.VMEM((C, C), F32),
            pltpu.VMEM((C, FFN), F32),
            pltpu.VMEM((C, FFN), F32),
            pltpu.VMEM((PAD, HEADS * PAD), F32),
            pltpu.VMEM((BAND, FFN), F32),
            pltpu.VMEM((BAND, FFN), F32),
            pltpu.VMEM((BAND, FFN), BF16),
            pltpu.VMEM((BAND, FFN), BF16),
            *[pltpu.VMEM((BAND, C), F32)] * 6,
            *[pltpu.VMEM((BAND, 128), F32)] * 2,
            *[pltpu.VMEM((BAND, C), BF16)] * 6,
            pltpu.VMEM((ROWS, 128), BF16),
            pltpu.SemaphoreType.DMA((6,)),
        ],
    )
    third = (4 * PIECE, 128)
    rims = in_vmem(rims)
    bias, into, back = in_vmem((bias, into, back))
    return pl.pallas_call(
        main_body,
        grid_spec=grid_spec,
        out_shape=[jax.ShapeDtypeStruct(a.shape, BF16) for a in (*tiles, *rims)]
        + [pltpu.VMEM(third, BF16)] * (2 * PARTS),
        compiler_params=pltpu.CompilerParams(
            dimension_semantics=("arbitrary",), vmem_limit_bytes=58 * 1024 * 1024
        ),
        name="block",
    )(*tiles, *rims, reg_lane, bias, into, back, *weights)


def rims_body(tokens_low, tokens_left, cot_low, cot_left, low_ref, right_ref, corner_ref):
    for n, (low, left) in enumerate(((tokens_low, tokens_left), (cot_low, cot_left))):
        low_ref[n] = low[...]
        right_ref[n] = left[:, :EDGE]
        corner_ref[n] = left[:SHIFT, :EDGE]


def cut_rims(tokens, cot):
    low = pl.BlockSpec((SHIFT, TILE, C), lambda i: (0, 0, 0))
    left = pl.BlockSpec((TILE, 16, C), lambda i: (0, 0, 0))
    shapes = [(2, SHIFT, TILE, C), (2, TILE, EDGE, C), (2, SHIFT, EDGE, C)]
    return pl.pallas_call(
        rims_body,
        grid=(1,),
        in_specs=[low, left, low, left],
        out_specs=[pl.BlockSpec(s, lambda i: (0, 0, 0, 0)) for s in shapes],
        out_shape=[jax.ShapeDtypeStruct(s, BF16) for s in shapes],
        name="rims",
    )(tokens, tokens, cot, cot)


def coordinates(index):
    ha, wa = index // 16, index % 16
    return (wa // 4, ha // 2, (wa // 2 % 2) * 2 + ha % 2, wa % 2)


def own_place():
    ha, wa = lax.axis_index("ha"), lax.axis_index("wa")
    y, z_low = lax.div(ha, 2), lax.rem(ha, 2)
    x, z_high = lax.div(wa, 4), lax.rem(lax.div(wa, 2), 2)
    return x, y, z_high * 2 + z_low, lax.rem(wa, 2)


def device_at(x, y, z, core):
    return (y * 2 + z % 2) * 16 + x * 4 + (z // 2) * 2 + core


def swap(value, axis, turn=0):
    pairs = []
    for index in range(128):
        place = list(coordinates(index))
        if axis == 3:
            place[3] = 1 - place[3]
        elif (turn + place[3]) % 2 == 0:
            place[axis] = place[axis] ^ 1
        else:
            place[axis] = 3 - place[axis]
        pairs.append((index, device_at(*place)))
    return lax.ppermute(value, AXES, pairs)


def quarter_bits(place, core):
    inner = lax.rem(lax.div(place + 1, 2), 2)
    upper = lax.div(place, 2)
    return inner + core * (upper - inner), upper + core * (inner - upper)


def add(*values):
    total = values[0].astype(F32)
    for value in values[1:]:
        total = total + value.astype(F32)
    return total.astype(BF16)


def table_map():
    out = np.zeros((SIDE, 128, 256), np.float32)
    for jr in range(SIDE):
        for head in range(2):
            for ir in range(SIDE):
                for ic in range(SIDE):
                    out[jr, head * PAD + 8 * ir + ic, head * 128 + (ir - jr + 6) * 8 + ic] = 1.0
    return out


def last_body(*refs):
    sources = refs[: 4 * PARTS]
    map_ref, index_ref, *outs, g_table, packed = refs[4 * PARTS : 4 * PARTS + 8]
    stages = refs[4 * PARTS + 8 : 4 * PARTS + 12]
    squares, index_s, out_sems = refs[4 * PARTS + 12 :]
    place = own_place()
    core = place[3]

    def squares_of(values):
        values = values.astype(F32)
        return jnp.sum((values * values).reshape(-1, 8, 128), 0)

    behind = BIAS % PIECE
    for n in range(2):
        owner = core if n == 0 else 1 - core
        for part in range(PARTS):
            half, quarter = quarter_bits(place[part], owner)
            for far in range(2):
                for second in range(2):
                    h = half if far == 0 else 1 - half
                    q = quarter if second == 0 else 1 - quarter
                    piece = (owner * PARTS + part) * 4 + h * 2 + q
                    values = sources[(n * PARTS + part) * 2 + far][second * PIECE : (second + 1) * PIECE, :]
                    packed[pl.ds(pl.multiple_of(piece * PIECE, 16), PIECE), :] = values
                    rest = squares_of(values[behind:])
                    rest = jnp.where(piece == BIAS // PIECE, jnp.zeros_like(rest), rest)
                    squares[piece] = squares_of(values[:behind]) + rest

    base = BIAS
    by_row = jnp.zeros((48, 256), F32)
    for jr in range(SIDE):
        rows = jnp.concatenate(
            [packed[base + b * PAD + 8 * jr : base + b * PAD + 8 * jr + 8, :].astype(F32) for b in range(6)], 0
        )
        by_row = by_row + nn(rows.astype(BF16), map_ref[jr])
    high = by_row.astype(BF16)
    rest = by_row - high.astype(F32)
    mid = rest.astype(BF16)
    low = (rest - mid.astype(F32)).astype(BF16)
    table = jnp.zeros((16, 256), F32)
    index_s[...] = jnp.zeros_like(index_s)
    index_s[:WINDOW, :WINDOW] = index_ref[...]
    entry = lax.broadcasted_iota(jnp.int32, (8, 256), 1)
    for jc in range(SIDE):
        pairs = [(0, 7 * up + jc) for up in range(6, 0, -1)] + [(7 * down, jc) for down in range(7)]
        picks = jnp.concatenate(
            [(index_s[i : i + 8, j : j + 1] == entry).astype(F32) for i, j in pairs]
            + [jnp.zeros((24, 256), F32)],
            0,
        ).astype(BF16)
        for part in (high, mid, low):
            picked = jnp.concatenate(
                [
                    part[b * 8 + jc : b * 8 + jc + 1, head * 128 : (head + 1) * 128].astype(F32)
                    for b in range(6)
                    for head in range(2)
                ]
                + [jnp.zeros((4, 128), F32)],
                0,
            )
            table = table + nn(picked.astype(BF16), picks)
    norm_sq = jnp.sum(jnp.sum(squares[...], 0)) + jnp.sum(table * table)
    norm = jnp.sqrt(jnp.full((8, 128), norm_sq, F32))
    factor = jnp.minimum(1.0, math.sqrt(PARAMS) / (norm + 1e-06))[:1, :]
    g_table[...] = (table * factor[:, :1])[:HEADS, :TABLE]

    first = 0
    for n in range(4):
        stage, out, sem = stages[n], outs[n], out_sems.at[n]

        def scale_block(b, carry, first=first, n=n, stage=stage, out=out, sem=sem):
            rows = pl.ds(pl.multiple_of((first + b) * C, C), C)
            block = packed[rows, :].astype(F32) * factor
            strip = pl.ds(pl.multiple_of(b * 128, 128), 128)
            if n == 3:
                stage[strip, :] = block.T
                pltpu.make_async_copy(stage.at[strip, :], out.at[strip, :], sem).start()
            else:
                stage[:, strip] = block
                pltpu.make_async_copy(stage.at[:, strip], out.at[:, strip], sem).start()
            return carry

        count = stage.shape[0] // 128 if n == 3 else stage.shape[1] // 128
        lax.fori_loop(0, count, scale_block, 0)
        first += count
    for n in range(4):
        pltpu.make_async_copy(stages[n], outs[n], out_sems.at[n]).wait()


def run_last(pieces, row_map, rel_index):
    hbm = pl.BlockSpec(memory_space=pl.ANY)

    def whole(shape):
        return pl.BlockSpec(shape, lambda i: (0,) * len(shape))

    shapes = [(C, 3 * C), (C, C), (C, FFN), (FFN, C), (HEADS, TABLE)]
    return pl.pallas_call(
        last_body,
        grid_spec=pl.GridSpec(
            grid=(1,),
            in_specs=[pl.BlockSpec(memory_space=pltpu.VMEM)] * (4 * PARTS + 2),
            out_specs=[hbm] * 4 + [whole(shapes[4])],
            scratch_shapes=[
                pltpu.VMEM((ROWS, 128), BF16),
                *[pltpu.VMEM(s, F32) for s in shapes[:4]],
                pltpu.VMEM((8 * PARTS, 8, 128), F32),
                pltpu.VMEM((PAD, 128), jnp.int32),
                pltpu.SemaphoreType.DMA((4,)),
            ],
        ),
        out_shape=[jax.ShapeDtypeStruct(s, F32) for s in shapes],
        compiler_params=pltpu.CompilerParams(vmem_limit_bytes=24 * 1024 * 1024),
        name="clip",
    )(*in_vmem([*pieces, row_map, rel_index]))


def sum_over_devices(keep, send, on_the_way):
    near, far = [], []
    for p in range(PARTS):
        with jax.named_scope(f"core_{p}"):
            got = swap(send[p], 3)
        held = keep[p][:PIECE].astype(F32) + got[:PIECE].astype(F32)
        other_quarter = keep[p][PIECE : 2 * PIECE].astype(F32) + got[PIECE : 2 * PIECE].astype(F32)
        other_half = add(keep[p][2 * PIECE :], got[2 * PIECE :])
        with jax.named_scope(f"halve_{p}"):
            got = swap(other_half, p, 0)
        with jax.named_scope(f"quarter_{p}"):
            back = swap(add(other_quarter, got[PIECE:]), p, 1)
        held = add(held, got[:PIECE], back)
        for stage in (1, 2):
            for turn in (0, 1):
                with jax.named_scope(f"double_{stage}{turn}_{p}"):
                    held = add(held, swap(held, (p + stage) % 3, turn))
            if p == 0 and stage == 1:
                held = on_the_way(held)
        with jax.named_scope(f"gather_{p}"):
            half = jnp.concatenate([held, swap(held, p, 1)], 0)
        near.append(half)
        with jax.named_scope(f"regather_{p}"):
            far.append(swap(half, p, 0))
    mine = [value for p in range(PARTS) for value in (near[p], far[p])]
    other = []
    for n, value in enumerate(mine):
        with jax.named_scope(f"recore_{n}"):
            other.append(swap(value, 3))
    return mine + other


def from_behind(x, steps):
    sizes = [lax.axis_size(axis) for axis in AXES]
    pairs = []
    for i in range(sizes[0]):
        for j in range(sizes[1]):
            to = ((i + steps[0]) % sizes[0]) * sizes[1] + (j + steps[1]) % sizes[1]
            pairs.append((i * sizes[1] + j, to))
    return lax.ppermute(x, AXES, pairs)


def send_rims(low, right, corner, by):
    return from_behind(low, (by, 0)), from_behind(right, (0, by)), from_behind(corner, (by, by))


def place_body(out_ref, tgrad_ref, low_ref, right_ref, corner_ref, *rest):
    new_out, new_tgrad = rest[1:3]
    inner = TILE - SHIFT
    col = lax.broadcasted_iota(jnp.int32, (inner, EDGE, C), 1)
    for n, (source, new) in enumerate(((out_ref, new_out), (tgrad_ref, new_tgrad))):
        new[:SHIFT] = low_ref[n]
        new[SHIFT:] = source[:inner]
        for rows, rim, old in (
            (slice(0, SHIFT), corner_ref[n], low_ref[n, :, :EDGE]),
            (slice(SHIFT, TILE), right_ref[n, :inner], source[:inner, :EDGE]),
        ):
            new[rows, :EDGE] = jnp.where(
                col[: rim.shape[0]] < SHIFT, rim.astype(F32), old.astype(F32)
            ).astype(BF16)


def place_rims(out, tgrad, rims, passing):
    def whole(a):
        return pl.BlockSpec(a.shape, lambda i: (0,) * a.ndim)

    here = pl.BlockSpec(memory_space=pltpu.VMEM)
    tiles = (out, tgrad)
    return pl.pallas_call(
        place_body,
        grid=(1,),
        in_specs=[*[whole(a) for a in tiles], *[here] * 4],
        out_specs=[*[whole(a) for a in tiles], here],
        out_shape=[jax.ShapeDtypeStruct(a.shape, BF16) for a in tiles]
        + [pltpu.VMEM(passing.shape, passing.dtype)],
        input_output_aliases={5: 2},
        name="place",
    )(*tiles, *in_vmem([*rims, passing]))


def window_bias(bias_table, rel_index):
    by_offset = rel_index.reshape(SIDE, SIDE, SIDE, SIDE)
    spread_out = jnp.pad(
        by_offset.transpose(2, 3, 0, 1), ((0, 1), (0, 1), (0, 1), (0, 1)), constant_values=-1
    ).reshape(PAD * PAD)
    lookup = (spread_out[None, :] == jnp.arange(TABLE, dtype=jnp.int32)[:, None]).astype(F32)
    bias = jnp.dot(bias_table.T, lookup, precision=lax.Precision.HIGHEST)
    bias = bias.reshape(HEADS, PAD, PAD).transpose(1, 0, 2).reshape(PAD, HEADS * PAD)
    return bias


def local(tokens, cotangent, w_qkv, w_proj, w_fc1, w_fc2, bias_table, rel_index, region):
    rims = send_rims(*cut_rims(tokens, cotangent), -1)
    bias = window_bias(bias_table, rel_index)
    windows = region.reshape(4, SIDE, 4, SIDE).transpose(0, 2, 1, 3).astype(F32)
    windows = jnp.pad(windows, ((0, 0), (0, 0), (0, 1), (0, 1)), constant_values=-1.0)
    reg_lane = jnp.tile(windows.reshape(16, PAD), (1, 4)).reshape(16, 1, BAND)
    into, back = band_maps()
    out, tgrad, low, right, corner, *parts = run_main(
        (tokens, cotangent),
        rims,
        reg_lane,
        bias,
        jnp.asarray(into, BF16),
        jnp.asarray(back, BF16),
        (w_qkv, w_proj, w_fc1, w_fc2),
    )
    rims = send_rims(low, right, corner, 1)
    placed = []

    def on_the_way(piece):
        block_out, token_grad, piece = place_rims(out, tgrad, rims, piece)
        placed.extend((block_out, token_grad))
        return piece

    pieces = sum_over_devices(parts[:PARTS], parts[PARTS:], on_the_way)
    *grads, table = run_last(pieces, jnp.asarray(table_map(), BF16), rel_index)
    return (*placed, *grads, table.T)


def solution(mesh):
    tiled = P("ha", "wa", None)
    return jax.shard_map(
        local,
        mesh=mesh,
        in_specs=(tiled, tiled, P(), P(), P(), P(), P(), P(), P("ha", "wa")),
        out_specs=(tiled, tiled, P(), P(), P(), P(), P()),
        check_vma=False,
    )
```
